768 devices in a mesh: gx: 96 (over x, z, y_hi), gy: 8 (over y_lo, core).
Axes of the slice: x: 4, y: 8 (y_hi: 2, y_lo: 4; y = y_hi * 4 + y_lo), z: 12, core: 2. Of those that a mesh axis runs over, the one named last changes fastest.
Arguments:
- distribution_values: float32 [19, 192, 64, 128], P(None, 'gx', 'gy'), may hold values from 0.02 to 0.09
- thermal_field: float32 [192, 64, 128], P('gx', 'gy'), may hold values from -0.5 to 0.5
- site_kind_code: int32 [192, 64, 128], P('gx', 'gy'), may hold values from 0 to 2, as said below
- entry_level_matrix: float32 [19, 128], replicated, may hold values from -16 to 16
- entry_level_offset: float32 [128], replicated, may hold values from -3 to 3
- inner_level_matrix: float32 [128, 128], replicated, may hold values from -0.5 to 0.5
- inner_level_offset: float32 [128], replicated, may hold values from -3 to 3
- exit_level_matrix: float32 [128, 19], replicated, may hold values from -0.125 to 0.125
- exit_level_offset: float32 [19], replicated, may hold values from -0.75 to 0.75
- closing_density_adjoint: float32 [19, 192, 64, 128], P(None, 'gx', 'gy'), may hold values from -6 to 6
- closing_thermal_adjoint: float32 [192, 64, 128], P('gx', 'gy'), may hold values from -6 to 6
Outputs:
- adjoint_populations: float32 [19, 192, 64, 128], P(None, 'gx', 'gy')
- adjoint_temperature: float32 [192, 64, 128], P('gx', 'gy')
- grad_first_weight: float32 [19, 128], replicated
- grad_first_bias: float32 [128], replicated
- grad_second_weight: float32 [128, 128], replicated
- grad_second_bias: float32 [128], replicated
- grad_third_weight: float32 [128, 19], replicated
- grad_third_bias: float32 [19], replicated
The draws below stay inside these ranges and needn't reach their ends.
Inputs may be any that keep to these rules, and one draw needn't show every extreme that they name: `site_kind_code`: 0 marks a fluid cell, 1 a solid cell whose temperature is held, 2 a solid heater cell.
All inputs are finite; a program needn't handle non-finite values.
Results may differ from the reference program's by a relative error of at most 0.0003.
Values sent between devices are 32-bit elements; how exact they have to be, the bound alone decides.
No kernel may reach another device: no remote copies, remote signals or barrier semaphores. Data moves between devices by JAX's collectives and lax.ppermute only.
A program may use at most 64 MiB of HBM per device.

```python
import math
import jax
import jax.numpy as jnp
import numpy as np
from jax import lax

Q = 19
HID = 128
STEPS = 2
SITES_ALONG_Z = 128
SITES_ALONG_X = 192
SITES_ALONG_Y = 64


def draw_site_kind_code(key, part):
    picked = jax.random.randint(key, (SITES_ALONG_X, SITES_ALONG_Y, SITES_ALONG_Z), 0, 10)
    return jnp.where(picked == 0, 1, jnp.where(picked == 1, 2, 0)).astype(jnp.int32)


def steps_of(key, dims, split, low, largest):
    loudness = 1.0
    for dim, parts in split:
        steps = jax.random.uniform(jax.random.fold_in(jax.random.fold_in(key, 6), dim), (parts,), jnp.float32, low / len(split), largest / len(split))
        loudness = loudness * jnp.repeat(jnp.exp(steps), dims[dim] // parts).reshape((-1,) + (1,) * (len(dims) - 1 - dim))
    return loudness


def bell_draw(rng, shape, spread, most, pieces=(), held_as=jnp.bfloat16):
    gain = steps_of(rng, shape, pieces, -0.22, 0.18) if pieces else 1.0
    values = jax.random.normal(rng, shape, jnp.float32) * spread * gain
    return jnp.minimum(jnp.maximum(values, -most), most).astype(held_as)


def setup_inputs(seed: int = 0) -> dict:
    key_list = jax.random.split(jax.random.key(seed), 12)
    return {
        "distribution_values": jnp.clip(0.02 + 0.07000000402331352 * jax.random.uniform(key_list[0], (Q, SITES_ALONG_X, SITES_ALONG_Y, SITES_ALONG_Z), jnp.float32) ** steps_of(key_list[0], (Q, SITES_ALONG_X, SITES_ALONG_Y, SITES_ALONG_Z), ((1, 96), (2, 8)), -0.2, 0.2), 0.02, 0.09),
        "thermal_field": jnp.clip(jax.random.uniform(key_list[1], (SITES_ALONG_X, SITES_ALONG_Y, SITES_ALONG_Z), jnp.float32, -0.5, 0.5) * steps_of(key_list[1], (SITES_ALONG_X, SITES_ALONG_Y, SITES_ALONG_Z), ((0, 96), (1, 8)), -0.4, 0.0), -0.5, 0.5),
        "site_kind_code": draw_site_kind_code(jax.random.fold_in(key_list[11], 71), 0),
        "entry_level_matrix": jnp.clip(jax.random.uniform(key_list[3], (Q, HID), jnp.float32, -16.0, 16.0), -16.0, 16.0),
        "entry_level_offset": bell_draw(key_list[4], (HID,), 0.5, 3.0, (), jnp.float32),
        "inner_level_matrix": bell_draw(key_list[5], (HID, HID), HID ** -0.5, 0.5, (), jnp.float32),
        "inner_level_offset": bell_draw(key_list[6], (HID,), 0.5, 3.0, (), jnp.float32),
        "exit_level_matrix": bell_draw(key_list[7], (HID, Q), (16 * HID) ** -0.5, 0.125, (), jnp.float32),
        "exit_level_offset": bell_draw(key_list[8], (Q,), 0.05, 0.75, (), jnp.float32),
        "closing_density_adjoint": bell_draw(key_list[9], (Q, SITES_ALONG_X, SITES_ALONG_Y, SITES_ALONG_Z), 1.0, 6.0, ((1, 96), (2, 8)), jnp.float32),
        "closing_thermal_adjoint": bell_draw(key_list[10], (SITES_ALONG_X, SITES_ALONG_Y, SITES_ALONG_Z), 1.0, 6.0, ((0, 96), (1, 8)), jnp.float32),
    }


VELOCITIES = np.array([[0, 0, 0], [1, 0, 0], [-1, 0, 0], [0, 1, 0], [0, -1, 0], [0, 0, 1], [0, 0, -1], [1, 1, 0], [-1, -1, 0], [1, -1, 0], [-1, 1, 0], [1, 0, 1], [-1, 0, -1], [1, 0, -1], [-1, 0, 1], [0, 1, 1], [0, -1, -1], [0, 1, -1], [0, -1, 1]])
OPPOSITE = np.array([0, 2, 1, 4, 3, 6, 5, 8, 7, 10, 9, 12, 11, 14, 13, 16, 15, 18, 17])
LATTICE_WEIGHTS = np.array([1.0 / 3.0] + [1.0 / 18.0] * 6 + [1.0 / 36.0] * 12)
BUOYANCY = 0.3 * LATTICE_WEIGHTS * VELOCITIES[:, 2]
CONDUCTIVITY = 0.1
HOT_WALL = 0.5
COLD_WALL = -0.5
HEATER = 0.5
PRECISE_MODE = lax.Precision.HIGHEST
CONTRACT = (((0,), (0,)), ((), ()))

def propagation_offset(window, step_z):
    lead = [(0, 0)] * (window.ndim - 1)
    if step_z == 1:
        return jnp.pad(window[..., :-1], lead + [(1, 0)])
    if step_z == -1:
        return jnp.pad(window[..., 1:], lead + [(0, 1)])
    return window

def boundary(cells):
    depths = jnp.arange(cells)
    masks = []
    for i in range(19):
        step_z = int(VELOCITIES[i, 2])
        if step_z == 1:
            masks.append(depths == 0)
        elif step_z == -1:
            masks.append(depths == cells - 1)
        else:
            masks.append(depths < 0)
    return jnp.stack(masks).astype(jnp.float32)[:, None, None, :]

def collide(current_fields, current_thermal, site_kind_code, learned_coefficients):
    entry_level_matrix, entry_level_offset, inner_level_matrix, inner_level_offset, exit_level_matrix, exit_level_offset = learned_coefficients
    flattened = current_fields.reshape(19, -1)
    hidden_one = jnp.tanh(lax.dot_general(entry_level_matrix, flattened, CONTRACT, precision=PRECISE_MODE) + entry_level_offset[:, None])
    hidden_two = jnp.tanh(lax.dot_general(inner_level_matrix, hidden_one, CONTRACT, precision=PRECISE_MODE) + inner_level_offset[:, None])
    output = lax.dot_general(exit_level_matrix, hidden_two, CONTRACT, precision=PRECISE_MODE) + exit_level_offset[:, None]
    lifting = jnp.asarray(BUOYANCY, jnp.float32).reshape((19,) + (1,) * current_thermal.ndim)
    relaxed = current_fields + output.reshape(current_fields.shape) + lifting * current_thermal[None]
    bounced = current_fields[OPPOSITE]
    return jnp.where(site_kind_code[None] == 0, relaxed, bounced)

def motion_of(current_fields):
    lookup_table = jnp.asarray(VELOCITIES.T, jnp.float32)
    return jnp.tensordot(lookup_table, current_fields, axes=1, precision=PRECISE_MODE)

def depth_pad(heat_rim):
    span_along_x, span_along_y, discarded_outcome = heat_rim.shape
    bottom = jnp.full((span_along_x, span_along_y, 1), HOT_WALL, jnp.float32)
    upper = jnp.full((span_along_x, span_along_y, 1), COLD_WALL, jnp.float32)
    return jnp.concatenate([bottom, heat_rim, upper], axis=2)

def advance_temp(padded, current_thermal, motion, site_kind_code):
    span_along_x, span_along_y, span_along_z = current_thermal.shape
    summed = (1.0 - 6.0 * CONDUCTIVITY) * current_thermal
    for a in range(3):
        for s in (1, -1):
            anchor = [1, 1, 1]
            anchor[a] += s
            nearby = padded[anchor[0]:anchor[0] + span_along_x, anchor[1]:anchor[1] + span_along_y, anchor[2]:anchor[2] + span_along_z]
            summed = summed + (CONDUCTIVITY - 0.5 * s * motion[a]) * nearby
    return jnp.where(site_kind_code == 0, summed, jnp.where(site_kind_code == 1, current_thermal, HEATER))

def stream_pull(planes, orient):
    span_along_x = planes[0].shape[0] - 2
    span_along_y = planes[0].shape[1] - 2
    pulled = []
    for i in range(19):
        step_x = int(VELOCITIES[i, 0]) * orient
        step_y = int(VELOCITIES[i, 1]) * orient
        step_z = int(VELOCITIES[i, 2]) * orient
        window = planes[i][1 - step_x:1 - step_x + span_along_x, 1 - step_y:1 - step_y + span_along_y, :]
        pulled.append(propagation_offset(window, step_z))
    return jnp.stack(pulled)

def advance(current_fields, current_thermal, site_kind_code, learned_coefficients):

    def one_plane(items):
        return collide(items[0], items[1], items[2], learned_coefficients)
    post_collide = lax.map(jax.checkpoint(one_plane), (jnp.moveaxis(current_fields, 1, 0), current_thermal, site_kind_code))
    post_collide = jnp.moveaxis(post_collide, 0, 1)
    padded = jnp.pad(post_collide, ((0, 0), (1, 1), (1, 1), (0, 0)), mode='wrap')
    read = stream_pull([padded[i] for i in range(19)], 1) + boundary(current_fields.shape[-1]) * post_collide[OPPOSITE]
    heat_rim = jnp.pad(current_thermal, ((1, 1), (1, 1), (0, 0)), mode='wrap')
    heated = advance_temp(depth_pad(heat_rim), current_thermal, motion_of(current_fields), site_kind_code)
    return (read, heated)

def reference(distribution_values, thermal_field, site_kind_code, entry_level_matrix, entry_level_offset, inner_level_matrix, inner_level_offset, exit_level_matrix, exit_level_offset, closing_density_adjoint, closing_thermal_adjoint):

    def primal_pass(current_fields, current_thermal, learned_coefficients):
        for i in range(STEPS):
            current_fields, current_thermal = advance(current_fields, current_thermal, site_kind_code, learned_coefficients)
        return (current_fields, current_thermal)
    learned_coefficients = (entry_level_matrix, entry_level_offset, inner_level_matrix, inner_level_offset, exit_level_matrix, exit_level_offset)
    discarded_outcome, backpropagation_function = jax.vjp(primal_pass, distribution_values, thermal_field, learned_coefficients)
    density_adjoint, thermal_adjoint, adjoint_sequence = backpropagation_function((closing_density_adjoint, closing_thermal_adjoint))
    factor = 1.0 / math.sqrt(SITES_ALONG_X * SITES_ALONG_Y * SITES_ALONG_Z)
    return (density_adjoint, thermal_adjoint, adjoint_sequence[0] * factor, adjoint_sequence[1] * factor, adjoint_sequence[2] * factor, adjoint_sequence[3] * factor, adjoint_sequence[4] * factor, adjoint_sequence[5] * factor)
```

```python
import math

import jax
import jax.numpy as jnp
import numpy as np
from jax import lax
from jax.experimental import pallas as pl
from jax.experimental.pallas import tpu as pltpu
from jax.sharding import PartitionSpec as P

VELOCITIES = [
    (0, 0, 0), (1, 0, 0), (-1, 0, 0), (0, 1, 0), (0, -1, 0), (0, 0, 1), (0, 0, -1),
    (1, 1, 0), (-1, -1, 0), (1, -1, 0), (-1, 1, 0), (1, 0, 1), (-1, 0, -1), (1, 0, -1),
    (-1, 0, 1), (0, 1, 1), (0, -1, -1), (0, 1, -1), (0, -1, 1),
]
Q = 19
OPPOSITE = [VELOCITIES.index((-a, -b, -c)) for a, b, c in VELOCITIES]
WEIGHTS = [1.0 / 3.0] + [1.0 / 18.0] * 6 + [1.0 / 36.0] * 12
BUOYANCY = [float(np.float32(0.3 * w * c[2])) for w, c in zip(WEIGHTS, VELOCITIES)]
CONDUCTIVITY = 0.1
HOT_WALL = 0.5
COLD_WALL = -0.5
HEATER = 0.5
HID = 128
KP = 32
ROWS = 16
LANES = 128
CH = 512
PACK = 176
F32 = jnp.float32
BF16 = jnp.bfloat16


def moving(axis, sign, orient):
    return [i for i in range(Q) if VELOCITIES[i][axis] * orient == sign]


def diagonal(sx, sy, orient):
    return VELOCITIES.index((sx * orient, sy * orient, 0))


def split(x):
    hi = x.astype(BF16)
    lo = (x - hi.astype(F32)).astype(BF16)
    return hi, lo


def stacked(x):
    return jnp.concatenate(split(x), axis=0)


def nn(a, b):
    return lax.dot_general(a, b, (((1,), (0,)), ((), ())), preferred_element_type=F32)


def nt(a, b):
    return lax.dot_general(a, b, (((1,), (1,)), ((), ())), preferred_element_type=F32)


def left(w):
    hi, lo = split(w)
    return jnp.concatenate(
        [jnp.concatenate([hi, hi], axis=1), jnp.concatenate([lo, lo], axis=1)], axis=0
    )


def product(a, b, rows):
    d = nn(a, b)
    return d[:rows] + d[rows:]


def four_blocks(d, rows):
    return d[:rows, :HID] + d[:rows, HID:] + d[rows:, :HID] + d[rows:, HID:]


def lanes_of(shape):
    return lax.broadcasted_iota(jnp.int32, shape, 1)


def subs_of(shape):
    return lax.broadcasted_iota(jnp.int32, shape, 0)


def shift_z(v, step, fill):
    if step == 1:
        return jnp.where(lanes_of(v.shape) == 0, fill, pltpu.roll(v, 1, 1))
    return jnp.where(lanes_of(v.shape) == LANES - 1, fill, pltpu.roll(v, LANES - 1, 1))


def shift_y(v, step, row):
    if step == 1:
        return jnp.where(subs_of(v.shape) == 0, row, pltpu.roll(v, 1, 0))
    return jnp.where(subs_of(v.shape) == 7, row, pltpu.roll(v, 7, 0))


def tile(ref, i, x):
    k = i * ROWS + x * 8
    return ref[k : k + 8, :]


def transposed(w_ref, b_ref, pad_ref):
    pad_ref[...] = jnp.zeros((HID, HID), F32)
    pad_ref[0:Q, :] = w_ref[...]
    if b_ref is not None:
        pad_ref[Q : Q + 1, :] = b_ref[...]
    return pad_ref[...]


def column(b_ref, n, pad_ref):
    pad_ref[...] = jnp.zeros((HID, HID), F32)
    pad_ref[:, 0:n] = jnp.broadcast_to(b_ref[...], (HID, n))
    return jnp.transpose(pad_ref[...])


def across(ref, r0, rows):
    return jnp.concatenate(
        [ref[pl.ds(r0 + j, KP, stride=ROWS), :] for j in range(rows)], axis=1
    )


def back(ref, r0, value):
    for j in range(value.shape[1] // LANES):
        ref[pl.ds(r0 + j, KP, stride=ROWS), :] = value[:, j * LANES : (j + 1) * LANES]


def fill_features(s_ref, f_ref):
    s_ref[0 : Q * ROWS, :] = f_ref[...]
    s_ref[Q * ROWS : (Q + 1) * ROWS, :] = jnp.ones((ROWS, LANES), F32)
    s_ref[(Q + 1) * ROWS :, :] = jnp.zeros(((KP - Q - 1) * ROWS, LANES), F32)


def wide(b):
    return jnp.concatenate([b] * (CH // LANES), axis=1)


def put_messages(value, orient, xp, xm, yp, ym, at, row):
    for k, i in enumerate(moving(0, 1, orient)):
        xp[at + 8 * k : at + 8 * k + 8, :] = value(i, 1)
    for k, i in enumerate(moving(0, -1, orient)):
        xm[at + 8 * k : at + 8 * k + 8, :] = value(i, 0)
    for k, i in enumerate(moving(1, 1, orient)):
        for x in range(2):
            yp[row + 2 * k + x : row + 2 * k + x + 1, :] = value(i, x)[7:8]
    for k, i in enumerate(moving(1, -1, orient)):
        for x in range(2):
            ym[row + 2 * k + x : row + 2 * k + x + 1, :] = value(i, x)[0:1]


def put_corners(leftward, rightward, orient, xp, xm, row, at):
    for sx, to in ((1, xp), (-1, xm)):
        for k, (sy, come) in enumerate(((1, leftward), (-1, rightward))):
            j = row + 2 * moving(1, sy, orient).index(diagonal(sx, sy, orient)) + (sx == 1)
            to[at + k : at + k + 1, :] = come[j : j + 1, :]


def streamed(ref, halo, orient, i, x):
    below, above, leftward, rightward, at, row, corner = halo
    sx, sy, sz = (orient * c for c in VELOCITIES[i])
    xs = x - sx
    if xs in (0, 1):
        v = tile(ref, i, xs)
    else:
        k = at + 8 * moving(0, sx, orient).index(i)
        v = (below if sx == 1 else above)[k : k + 8, :]
    if sy:
        if xs in (0, 1):
            k = row + 2 * moving(1, sy, orient).index(i) + xs
            edge = (leftward if sy == 1 else rightward)[k : k + 1, :]
        else:
            k = corner + (sy == -1)
            edge = (below if sx == 1 else above)[k : k + 1, :]
        v = shift_y(v, sy, edge)
    if sz:
        v = shift_z(v, sz, tile(ref, OPPOSITE[i], x))
    return v


def motion(ref, x):
    us = []
    for a in range(3):
        total = None
        for i in range(Q):
            c = VELOCITIES[i][a]
            if c:
                v = tile(ref, i, x)
                total = (v if c == 1 else -v) if total is None else (total + v if c == 1 else total - v)
        us.append(total)
    return us


def warm_neighbours(t_ref, rims, x):
    below, above, leftward, rightward = rims
    t = [t_ref[0:8, :], t_ref[8:16, :]]
    lower = below if x == 0 else t[0]
    upper = t[1] if x == 0 else above
    return [
        (upper, lower),
        (shift_y(t[x], -1, rightward[x]), shift_y(t[x], 1, leftward[x])),
        (shift_z(t[x], -1, COLD_WALL), shift_z(t[x], 1, HOT_WALL)),
    ]


def flux(u, a, s, liquid):
    return (CONDUCTIVITY - (0.5 * s) * u[a]) * liquid


def heat_adjoint(us, liquids, theta, codes, flux_rims):
    below, above, leftward, rightward = flux_rims
    out = []
    for x in range(2):
        u, liquid = us[x], liquids[x]
        total = 0.4 * liquid + jnp.where(codes[x] == 1, theta[x], 0.0)
        total = total + (below if x == 0 else flux(us[0], 0, 1, liquids[0]))
        total = total + (flux(us[1], 0, -1, liquids[1]) if x == 0 else above)
        total = total + shift_y(flux(u, 1, 1, liquid), 1, leftward[x])
        total = total + shift_y(flux(u, 1, -1, liquid), -1, rightward[x])
        total = total + shift_z(flux(u, 2, 1, liquid), 1, 0.0)
        total = total + shift_z(flux(u, 2, -1, liquid), -1, 0.0)
        out.append(total)
    return out


def motion_adjoint(t_ref, rims, liquids):
    return [
        [-0.5 * liquids[x] * (plus - minus) for plus, minus in warm_neighbours(t_ref, rims, x)]
        for x in range(2)
    ]


def with_motion(value, ubar, i):
    for a in range(3):
        c = VELOCITIES[i][a]
        if c:
            value = value + ubar[a] if c == 1 else value - ubar[a]
    return value


def hidden(fx, a1, a2, b2):
    h1 = jnp.tanh(product(a1, fx, HID))
    h1x = stacked(h1)
    h2 = jnp.tanh(product(a2, h1x, HID) + b2)
    return h1, h1x, h2


def network_back(fx, h1, h1x, h2, d, w3b, w2b, w1b, acc2, acc1, acc3, accb, first):
    dx = stacked(d)
    p2 = product(w3b, dx, HID) * (1.0 - h2 * h2)
    px = stacked(p2)
    p1 = product(w2b, px, HID) * (1.0 - h1 * h1)
    qx = stacked(p1)
    df = product(w1b, qx, KP)
    parts = (
        (acc2, nt(h1x, px)),
        (acc1, nt(fx, jnp.concatenate([qx, px], axis=0))),
        (acc3, nt(dx, stacked(h2))),
        (accb, sum(d[:, j * LANES : (j + 1) * LANES] for j in range(CH // LANES))),
    )
    for ref, value in parts:
        if first:
            ref[...] = value
        else:
            ref[...] = ref[...] + value
    return df


def write_pack(pack, acc2, acc1, acc3, accb, pad_ref):
    pack[0:HID, :] = four_blocks(acc2[...], HID)
    d = acc1[...]
    w1 = four_blocks(d[:, : 2 * HID], KP)
    pack[HID : HID + 24, :] = w1[0:24]
    d3 = acc3[...]
    w3 = four_blocks(d3, KP)
    pack[HID + 24 : HID + 48, :] = w3[0:24]
    b2 = four_blocks(d[:, 2 * HID :], KP)[Q : Q + 1]
    pad_ref[...] = jnp.zeros((HID, HID), F32)
    pad_ref[0:KP, :] = accb[...]
    b3 = jnp.sum(jnp.transpose(pad_ref[...]), axis=0, keepdims=True)
    pack[HID + 21 : HID + 22, :] = b2
    pack[HID + 22 : HID + 23, :] = b3


def forward_kernel(
    f, t, code, adj, w1, b1, w2, b2, w3, b3,
    post, h1s, h2s, xp, xm, yp, ym,
    feat, outs, pad,
):
    put_messages(lambda i, x: tile(adj, i, x), -1, xp, xm, yp, ym, 48, 12)
    fill_features(feat, f)
    l1 = left_narrow(jnp.transpose(transposed(w1, b1, pad)))
    l2 = left(jnp.transpose(w2[...]))
    pad[...] = jnp.zeros((HID, HID), F32)
    pad[0:Q, :] = w3[...]
    l3 = left(pad[0:KP, :])
    b2t = wide(column(b2, HID, pad))
    b3t = wide(column(b3, Q, pad)[0:KP])
    n = CH // LANES
    for c in range(ROWS * LANES // CH):
        fx = stacked(across(feat, c * n, n))
        h1, h1x, h2 = hidden(fx, l1, l2, b2t)
        h1s[c] = h1
        h2s[c] = h2
        back(outs, c * n, product(l3, stacked(h2), KP) + b3t)
    fluid = code[...] == 0
    warm = t[...]
    for i in range(Q):
        k = i * ROWS
        relaxed = f[k : k + ROWS, :] + outs[k : k + ROWS, :]
        if BUOYANCY[i]:
            relaxed = relaxed + BUOYANCY[i] * warm
        o = OPPOSITE[i] * ROWS
        post[k : k + ROWS, :] = jnp.where(fluid, relaxed, f[o : o + ROWS, :])
    put_messages(lambda i, x: tile(post, i, x), 1, xp, xm, yp, ym, 0, 0)
    xp[40:48, :] = t[8:16, :]
    xm[40:48, :] = t[0:8, :]
    for x in range(2):
        yp[10 + x : 11 + x, :] = t[8 * x + 7 : 8 * x + 8, :]
        ym[10 + x : 11 + x, :] = t[8 * x : 8 * x + 1, :]


def left_narrow(w):
    hi, lo = split(w + pltpu.roll(w, KP, 1))
    return jnp.concatenate([hi, lo], axis=0)[:, : 2 * KP]


def rims_of(below, above, leftward, rightward, at, row):
    return (
        below[at : at + 8, :],
        above[at : at + 8, :],
        [leftward[row + x : row + x + 1, :] for x in range(2)],
        [rightward[row + x : row + x + 1, :] for x in range(2)],
    )


def stream_kernel(
    post, f, t, code, theta, below, above, leftward, rightward,
    f1, t1, xp, xm, yp, ym,
):
    halo = (below, above, leftward, rightward, 0, 0, 88)
    for i in range(Q):
        for x in range(2):
            k = i * ROWS + 8 * x
            f1[k : k + 8, :] = streamed(post, halo, 1, i, x)
    rims = rims_of(below, above, leftward, rightward, 40, 10)
    for x in range(2):
        u = motion(f, x)
        here = t[8 * x : 8 * x + 8, :]
        total = 0.4 * here
        for a, (plus, minus) in enumerate(warm_neighbours(t, rims, x)):
            total = total + (CONDUCTIVITY - 0.5 * u[a]) * plus
            total = total + (CONDUCTIVITY + 0.5 * u[a]) * minus
        kind = code[8 * x : 8 * x + 8, :]
        new = jnp.where(kind == 0, total, jnp.where(kind == 1, here, HEATER))
        t1[8 * x : 8 * x + 8, :] = new
        liquid = jnp.where(kind == 0, theta[8 * x : 8 * x + 8, :], 0.0)
        un = motion(f1, x)
        if x == 0:
            xm[0:8, :] = new
            xm[8:16, :] = flux(un, 0, -1, liquid)
        else:
            xp[0:8, :] = new
            xp[8:16, :] = flux(un, 0, 1, liquid)
        yp[x : x + 1, :] = new[7:8]
        yp[2 + x : 3 + x, :] = flux(un, 1, 1, liquid)[7:8]
        ym[x : x + 1, :] = new[0:1]
        ym[2 + x : 3 + x, :] = flux(un, 1, -1, liquid)[0:1]


def collision_gradient(adj, halo, code, grad, masked, lift):
    for x in range(2):
        fluid = code[8 * x : 8 * x + 8, :] == 0
        total = None
        for i in range(Q):
            k = i * ROWS + 8 * x
            g = streamed(adj, halo, -1, i, x)
            grad[k : k + 8, :] = g
            g = jnp.where(fluid, g, 0.0)
            masked[k : k + 8, :] = g
            if BUOYANCY[i]:
                total = BUOYANCY[i] * g if total is None else total + BUOYANCY[i] * g
        lift[8 * x : 8 * x + 8, :] = total
    masked[Q * ROWS :, :] = jnp.zeros(((KP - Q) * ROWS, LANES), F32)


def back_weights(w1, w2, w3, pad):
    pad[...] = jnp.zeros((HID, HID), F32)
    pad[0:Q, :] = w3[...]
    w3b = left_narrow(jnp.transpose(pad[...]))
    w2b = left(w2[...])
    pad[...] = jnp.zeros((HID, HID), F32)
    pad[0:Q, :] = w1[...]
    w1b = left(pad[0:KP, :])
    return w3b, w2b, w1b


def last_step_kernel(
    f, adj, below, above, leftward, rightward, code, w1, b1, w2, b2, w3,
    fbar, lift, pack,
    feat, grad, masked, dfs, pad, acc2, acc1, acc3, accb,
):
    halo = (below, above, leftward, rightward, 48, 12, 90)
    collision_gradient(adj, halo, code, grad, masked, lift)
    fill_features(feat, f)
    l1 = left_narrow(jnp.transpose(transposed(w1, b1, pad)))
    l2 = left(jnp.transpose(w2[...]))
    b2t = wide(column(b2, HID, pad))
    w3b, w2b, w1b = back_weights(w1, w2, w3, pad)
    n = CH // LANES
    for c in range(ROWS * LANES // CH):
        fx = stacked(across(feat, c * n, n))
        h1, h1x, h2 = hidden(fx, l1, l2, b2t)
        d = across(masked, c * n, n)
        df = network_back(fx, h1, h1x, h2, d, w3b, w2b, w1b, acc2, acc1, acc3, accb, c == 0)
        back(dfs, c * n, df)
    fluid = code[...] == 0
    for i in range(Q):
        k, o = i * ROWS, OPPOSITE[i] * ROWS
        fbar[k : k + ROWS, :] = jnp.where(
            fluid, grad[k : k + ROWS, :] + dfs[k : k + ROWS, :], grad[o : o + ROWS, :]
        )
    write_pack(pack, acc2, acc1, acc3, accb, pad)


def halves(ref):
    return [ref[0:8, :], ref[8:16, :]]


def join_kernel(
    fbar, lift, f1, t1, f0, theta, code, below, above, leftward, rightward,
    adj, theta1, xp, xm, yp, ym,
):
    codes, thetas = halves(code), halves(theta)
    liquids = [jnp.where(k == 0, v, 0.0) for k, v in zip(codes, thetas)]
    rims = rims_of(below, above, leftward, rightward, 0, 0)
    flux_rims = rims_of(below, above, leftward, rightward, 8, 2)
    ubar = motion_adjoint(t1, rims, liquids)
    for i in range(Q):
        for x in range(2):
            k = i * ROWS + 8 * x
            adj[k : k + 8, :] = with_motion(fbar[k : k + 8, :], ubar[x], i)
    new = heat_adjoint([motion(f1, x) for x in range(2)], liquids, thetas, codes, flux_rims)
    for x in range(2):
        value = new[x] + lift[8 * x : 8 * x + 8, :]
        theta1[8 * x : 8 * x + 8, :] = value
        liquid = jnp.where(codes[x] == 0, value, 0.0)
        u = motion(f0, x)
        if x == 0:
            xm[40:48, :] = flux(u, 0, -1, liquid)
        else:
            xp[40:48, :] = flux(u, 0, 1, liquid)
        yp[10 + x : 11 + x, :] = flux(u, 1, 1, liquid)[7:8]
        ym[10 + x : 11 + x, :] = flux(u, 1, -1, liquid)[0:1]
    put_messages(lambda i, x: tile(adj, i, x), -1, xp, xm, yp, ym, 0, 0)


def first_step_kernel(
    scale,
    f, t, theta, adj, below, above, leftward, rightward,
    tbelow, tabove, tleft, tright, code, h1s, h2s, w1, w2, w3, pack1,
    fbar, thetabar, pack,
    feat, grad, masked, dfs, pad, acc2, acc1, acc3, accb, lift, total,
):
    halo = (below, above, leftward, rightward, 0, 0, 48)
    collision_gradient(adj, halo, code, grad, masked, lift)
    fill_features(feat, f)
    w3b, w2b, w1b = back_weights(w1, w2, w3, pad)
    n = CH // LANES
    for c in range(ROWS * LANES // CH):
        fx = stacked(across(feat, c * n, n))
        h1 = h1s[c]
        d = across(masked, c * n, n)
        df = network_back(
            fx, h1, stacked(h1), h2s[c], d, w3b, w2b, w1b, acc2, acc1, acc3, accb, c == 0
        )
        back(dfs, c * n, df)
    write_pack(total, acc2, acc1, acc3, accb, pad)
    parts, part, _ = pack.shape
    total[PACK:, :] = jnp.zeros((parts * part - PACK, HID), F32)
    total[0:PACK, :] = (total[0:PACK, :] + pack1[...]) * scale
    for k in range(parts):
        pack[k] = total[k * part : (k + 1) * part, :]
    codes, thetas = halves(code), halves(theta)
    liquids = [jnp.where(k == 0, v, 0.0) for k, v in zip(codes, thetas)]
    rims = rims_of(tbelow, tabove, tleft, tright, 40, 10)
    flux_rims = rims_of(below, above, leftward, rightward, 40, 10)
    ubar = motion_adjoint(t, rims, liquids)
    new = heat_adjoint([motion(f, x) for x in range(2)], liquids, thetas, codes, flux_rims)
    for x in range(2):
        thetabar[8 * x : 8 * x + 8, :] = new[x] + lift[8 * x : 8 * x + 8, :]
        fluid = codes[x] == 0
        for i in range(Q):
            k, o = i * ROWS + 8 * x, OPPOSITE[i] * ROWS + 8 * x
            value = jnp.where(fluid, grad[k : k + 8, :] + dfs[k : k + 8, :], grad[o : o + 8, :])
            fbar[k : k + 8, :] = with_motion(value, ubar[x], i)


def struct(*shape):
    return jax.ShapeDtypeStruct(shape, F32)


def call(kernel, outs, scratch, name):
    return pl.pallas_call(
        kernel,
        out_shape=outs,
        scratch_shapes=[pltpu.VMEM(s, F32) for s in scratch],
        compiler_params=pltpu.CompilerParams(vmem_limit_bytes=40 * 1024 * 1024),
        name=name,
    )


FULL = (KP * ROWS, LANES)
POPS = struct(Q * ROWS, LANES)
WARM = struct(ROWS, LANES)


def shifted(value, axis, by):
    count = lax.axis_size(axis)
    return lax.ppermute(value, axis, [(s, (s + by) % count) for s in range(count)])


def along(axis, plus, minus):
    return shifted(plus, axis, 1), shifted(minus, axis, -1)


def edge_kernel(blocks, xp, xm, leftward, rightward, xp_out, xm_out):
    xp_out[...] = xp[...]
    xm_out[...] = xm[...]
    for orient, row, at in blocks:
        put_corners(leftward, rightward, orient, xp_out, xm_out, row, at)


def exchange(xp, xm, yp, ym, blocks):
    leftward, rightward = along("gy", yp, ym)
    xp, xm = call(
        lambda *refs: edge_kernel(blocks, *refs),
        [struct(*xp.shape), struct(*xm.shape)],
        [],
        "edge",
    )(xp, xm, leftward, rightward)
    below, above = along("gx", xp, xm)
    return below, above, leftward, rightward


def swapped(value, groups):
    return lax.all_to_all(
        value, ("gx", "gy"), 0, 0, axis_index_groups=groups, tiled=True
    )


def outer_of(nx):
    return nx // 24 if nx % 24 == 0 else (2 if nx % 2 == 0 else 1)


def groups_of(nx, ny):
    outer = outer_of(nx)
    at = np.arange(nx * ny).reshape(outer, nx // outer, ny)
    return (
        at.transpose(1, 0, 2).reshape(nx // outer, outer * ny).tolist(),
        at.transpose(0, 2, 1).reshape(outer * ny, nx // outer).tolist(),
    )


def total_kernel(parts, out):
    value = parts[0]
    for k in range(1, parts.shape[0]):
        value = value + parts[k]
    for k in range(out.shape[0]):
        out[k] = value


def summed(parts, copies):
    return call(total_kernel, struct(copies, *parts.shape[1:]), [], "total")(parts)


def reduced(pack):
    share, same = groups_of(lax.axis_size("gx"), lax.axis_size("gy"))
    part = summed(swapped(pack, share), len(same[0]))
    part = summed(swapped(part, same), len(share[0]))
    return swapped(part, share)


def unpack_kernel(parts, w1, b1, w2, b2, w3, b3, pack):
    count, part, _ = parts.shape
    for k in range(count):
        pack[k * part : (k + 1) * part, :] = parts[k]
    w2[...] = pack[0:HID, :]
    w1[...] = pack[HID : HID + Q, :]
    b1[...] = pack[HID + Q : HID + Q + 1, :]
    b2[...] = pack[HID + 21 : HID + 22, :]
    b3[...] = pack[HID + 22 : HID + 23, 0:Q]
    w3[...] = pack[HID + 24 : HID + 24 + Q, :]


def per_device(f, t, code, w1, b1, w2, b2, w3, b3, adj, theta):
    sx, sy, sz = t.shape
    cells = sx * lax.axis_size("gx") * sy * lax.axis_size("gy") * sz
    f, adj = f.reshape(Q * ROWS, LANES), adj.reshape(Q * ROWS, LANES)
    t, code, theta = (v.reshape(ROWS, LANES) for v in (t, code, theta))
    b1, b2, b3 = (v.reshape(1, -1) for v in (b1, b2, b3))
    w3 = w3.T
    chunks = struct(ROWS * LANES // CH, HID, CH)
    outs = call(
        forward_kernel,
        [POPS, chunks, chunks, struct(96, LANES), struct(96, LANES), struct(24, LANES), struct(24, LANES)],
        [FULL, FULL, (HID, HID)],
        "forward",
    )(f, t, code, adj, w1, b1, w2, b2, w3, b3)
    post, h1s, h2s = outs[:3]
    halo0 = exchange(*outs[3:], ((1, 0, 88), (-1, 12, 90)))
    f1, t1, *rim_messages = call(
        stream_kernel,
        [POPS, WARM, struct(16, LANES), struct(16, LANES), struct(8, LANES), struct(8, LANES)],
        [],
        "stream",
    )(post, f, t, code, theta, *halo0)
    left1, right1 = along("gy", *rim_messages[2:])
    rims1 = (*along("gx", *rim_messages[:2]), left1, right1)
    accs = [(2 * HID, 2 * HID), (2 * KP, 4 * HID), (2 * KP, 2 * HID), (KP, LANES)]
    fbar, lift, pack1 = call(
        last_step_kernel,
        [POPS, WARM, struct(PACK, HID)],
        [FULL, (Q * ROWS, LANES), FULL, FULL, (HID, HID), *accs],
        "last_step",
    )(f1, adj, *halo0, code, w1, b1, w2, b2, w3)
    adj1, theta1, *messages = call(
        join_kernel,
        [POPS, WARM, struct(56, LANES), struct(56, LANES), struct(16, LANES), struct(16, LANES)],
        [],
        "join",
    )(fbar, lift, f1, t1, f, theta, code, *rims1)
    halo1 = exchange(*messages, ((-1, 0, 48),))
    scale = 1.0 / math.sqrt(cells)
    parts = outer_of(lax.axis_size("gx")) * lax.axis_size("gy")
    part = -(-(PACK + 8) // parts)
    fbar0, theta0, pack = call(
        lambda *refs: first_step_kernel(scale, *refs),
        [POPS, WARM, struct(parts, part, HID)],
        [FULL, (Q * ROWS, LANES), FULL, FULL, (HID, HID), *accs, (ROWS, LANES), (parts * part, HID)],
        "first_step",
    )(f, t, theta1, adj1, *halo1, *halo0, code, h1s, h2s, w1, w2, w3, pack1)
    total = reduced(pack)
    g1, gb1, g2, gb2, g3, gb3 = call(
        unpack_kernel,
        [struct(Q, HID), struct(1, HID), struct(HID, HID), struct(1, HID), struct(Q, HID), struct(1, Q)],
        [(parts * part, HID)],
        "unpack",
    )(total)
    return (
        fbar0.reshape(Q, sx, sy, sz),
        theta0.reshape(sx, sy, sz),
        g1,
        gb1.reshape(HID),
        g2,
        gb2.reshape(HID),
        g3.T,
        gb3.reshape(Q),
    )


def solution(mesh):
    pops, cells = P(None, "gx", "gy", None), P("gx", "gy", None)
    return jax.shard_map(
        per_device,
        mesh=mesh,
        in_specs=(pops, cells, cells, P(), P(), P(), P(), P(), P(), pops, cells),
        out_specs=(pops, cells, P(), P(), P(), P(), P(), P()),
        check_vma=False,
    )
```

```python
import math

import jax
import jax.numpy as jnp
import numpy as np
from jax import lax
from jax.experimental import pallas as pl
from jax.experimental.pallas import tpu as pltpu
from jax.sharding import PartitionSpec as P

VELOCITIES = [
    (0, 0, 0), (1, 0, 0), (-1, 0, 0), (0, 1, 0), (0, -1, 0), (0, 0, 1), (0, 0, -1),
    (1, 1, 0), (-1, -1, 0), (1, -1, 0), (-1, 1, 0), (1, 0, 1), (-1, 0, -1), (1, 0, -1),
    (-1, 0, 1), (0, 1, 1), (0, -1, -1), (0, 1, -1), (0, -1, 1),
]
Q = 19
OPPOSITE = [VELOCITIES.index((-a, -b, -c)) for a, b, c in VELOCITIES]
WEIGHTS = [1.0 / 3.0] + [1.0 / 18.0] * 6 + [1.0 / 36.0] * 12
BUOYANCY = [float(np.float32(0.3 * w * c[2])) for w, c in zip(WEIGHTS, VELOCITIES)]
CONDUCTIVITY = 0.1
HOT_WALL = 0.5
COLD_WALL = -0.5
HEATER = 0.5
HID = 128
KP = 32
ROWS = 16
LANES = 128
CH = 512
PACK = 176
F32 = jnp.float32
BF16 = jnp.bfloat16


def moving(axis, sign, orient):
    return [i for i in range(Q) if VELOCITIES[i][axis] * orient == sign]


def diagonal(sx, sy, orient):
    return VELOCITIES.index((sx * orient, sy * orient, 0))


def split(x):
    hi = x.astype(BF16)
    lo = (x - hi.astype(F32)).astype(BF16)
    return hi, lo


def stacked(x):
    return jnp.concatenate(split(x), axis=0)


def nn(a, b):
    return lax.dot_general(a, b, (((1,), (0,)), ((), ())), preferred_element_type=F32)


def nt(a, b):
    return lax.dot_general(a, b, (((1,), (1,)), ((), ())), preferred_element_type=F32)


def left(w):
    hi, lo = split(w)
    return jnp.concatenate(
        [jnp.concatenate([hi, hi], axis=1), jnp.concatenate([lo, lo], axis=1)], axis=0
    )


def product(a, b, rows):
    d = nn(a, b)
    return d[:rows] + d[rows:]


def four_blocks(d, rows):
    return d[:rows, :HID] + d[:rows, HID:] + d[rows:, :HID] + d[rows:, HID:]


def lanes_of(shape):
    return lax.broadcasted_iota(jnp.int32, shape, 1)


def subs_of(shape):
    return lax.broadcasted_iota(jnp.int32, shape, 0)


def shift_z(v, step, fill):
    if step == 1:
        return jnp.where(lanes_of(v.shape) == 0, fill, pltpu.roll(v, 1, 1))
    return jnp.where(lanes_of(v.shape) == LANES - 1, fill, pltpu.roll(v, LANES - 1, 1))


def shift_y(v, step, row):
    if step == 1:
        return jnp.where(subs_of(v.shape) == 0, row, pltpu.roll(v, 1, 0))
    return jnp.where(subs_of(v.shape) == 7, row, pltpu.roll(v, 7, 0))


def tile(ref, i, x):
    k = i * ROWS + x * 8
    return ref[k : k + 8, :]


def transposed(w_ref, b_ref, pad_ref):
    pad_ref[...] = jnp.zeros((HID, HID), F32)
    pad_ref[0:Q, :] = w_ref[...]
    if b_ref is not None:
        pad_ref[Q : Q + 1, :] = b_ref[...]
    return pad_ref[...]


def column(b_ref, n, pad_ref):
    pad_ref[...] = jnp.zeros((HID, HID), F32)
    pad_ref[:, 0:n] = jnp.broadcast_to(b_ref[...], (HID, n))
    return jnp.transpose(pad_ref[...])


def across(ref, r0, rows):
    return jnp.concatenate(
        [ref[pl.ds(r0 + j, KP, stride=ROWS), :] for j in range(rows)], axis=1
    )


def back(ref, r0, value):
    for j in range(value.shape[1] // LANES):
        ref[pl.ds(r0 + j, KP, stride=ROWS), :] = value[:, j * LANES : (j + 1) * LANES]


def fill_features(s_ref, f_ref):
    s_ref[0 : Q * ROWS, :] = f_ref[...]
    s_ref[Q * ROWS : (Q + 1) * ROWS, :] = jnp.ones((ROWS, LANES), F32)
    s_ref[(Q + 1) * ROWS :, :] = jnp.zeros(((KP - Q - 1) * ROWS, LANES), F32)


def wide(b):
    return jnp.concatenate([b] * (CH // LANES), axis=1)


def put_messages(value, orient, xp, xm, yp, ym, at, row):
    for k, i in enumerate(moving(0, 1, orient)):
        xp[at + 8 * k : at + 8 * k + 8, :] = value(i, 1)
    for k, i in enumerate(moving(0, -1, orient)):
        xm[at + 8 * k : at + 8 * k + 8, :] = value(i, 0)
    for k, i in enumerate(moving(1, 1, orient)):
        for x in range(2):
            yp[row + 2 * k + x : row + 2 * k + x + 1, :] = value(i, x)[7:8]
    for k, i in enumerate(moving(1, -1, orient)):
        for x in range(2):
            ym[row + 2 * k + x : row + 2 * k + x + 1, :] = value(i, x)[0:1]


def put_corners(leftward, rightward, orient, xp, xm, row, at):
    for sx, to in ((1, xp), (-1, xm)):
        for k, (sy, come) in enumerate(((1, leftward), (-1, rightward))):
            j = row + 2 * moving(1, sy, orient).index(diagonal(sx, sy, orient)) + (sx == 1)
            to[at + k : at + k + 1, :] = come[j : j + 1, :]


def streamed(ref, halo, orient, i, x):
    below, above, leftward, rightward, at, row, corner = halo
    sx, sy, sz = (orient * c for c in VELOCITIES[i])
    xs = x - sx
    if xs in (0, 1):
        v = tile(ref, i, xs)
    else:
        k = at + 8 * moving(0, sx, orient).index(i)
        v = (below if sx == 1 else above)[k : k + 8, :]
    if sy:
        if xs in (0, 1):
            k = row + 2 * moving(1, sy, orient).index(i) + xs
            edge = (leftward if sy == 1 else rightward)[k : k + 1, :]
        else:
            k = corner + (sy == -1)
            edge = (below if sx == 1 else above)[k : k + 1, :]
        v = shift_y(v, sy, edge)
    if sz:
        v = shift_z(v, sz, tile(ref, OPPOSITE[i], x))
    return v


def motion(ref, x):
    us = []
    for a in range(3):
        total = None
        for i in range(Q):
            c = VELOCITIES[i][a]
            if c:
                v = tile(ref, i, x)
                total = (v if c == 1 else -v) if total is None else (total + v if c == 1 else total - v)
        us.append(total)
    return us


def warm_neighbours(t_ref, rims, x):
    below, above, leftward, rightward = rims
    t = [t_ref[0:8, :], t_ref[8:16, :]]
    lower = below if x == 0 else t[0]
    upper = t[1] if x == 0 else above
    return [
        (upper, lower),
        (shift_y(t[x], -1, rightward[x]), shift_y(t[x], 1, leftward[x])),
        (shift_z(t[x], -1, COLD_WALL), shift_z(t[x], 1, HOT_WALL)),
    ]


def flux(u, a, s, liquid):
    return (CONDUCTIVITY - (0.5 * s) * u[a]) * liquid


def heat_adjoint(us, liquids, theta, codes, flux_rims):
    below, above, leftward, rightward = flux_rims
    out = []
    for x in range(2):
        u, liquid = us[x], liquids[x]
        total = 0.4 * liquid + jnp.where(codes[x] == 1, theta[x], 0.0)
        total = total + (below if x == 0 else flux(us[0], 0, 1, liquids[0]))
        total = total + (flux(us[1], 0, -1, liquids[1]) if x == 0 else above)
        total = total + shift_y(flux(u, 1, 1, liquid), 1, leftward[x])
        total = total + shift_y(flux(u, 1, -1, liquid), -1, rightward[x])
        total = total + shift_z(flux(u, 2, 1, liquid), 1, 0.0)
        total = total + shift_z(flux(u, 2, -1, liquid), -1, 0.0)
        out.append(total)
    return out


def motion_adjoint(t_ref, rims, liquids):
    return [
        [-0.5 * liquids[x] * (plus - minus) for plus, minus in warm_neighbours(t_ref, rims, x)]
        for x in range(2)
    ]


def with_motion(value, ubar, i):
    for a in range(3):
        c = VELOCITIES[i][a]
        if c:
            value = value + ubar[a] if c == 1 else value - ubar[a]
    return value


def hidden(fx, a1, a2, b2):
    h1 = jnp.tanh(product(a1, fx, HID))
    h1x = stacked(h1)
    h2 = jnp.tanh(product(a2, h1x, HID) + b2)
    return h1, h1x, h2


def network_back(fx, h1, h1x, h2, d, w3b, w2b, w1b, acc2, acc1, acc3, accb, first):
    dx = stacked(d)
    p2 = product(w3b, dx, HID) * (1.0 - h2 * h2)
    px = stacked(p2)
    p1 = product(w2b, px, HID) * (1.0 - h1 * h1)
    qx = stacked(p1)
    df = product(w1b, qx, KP)
    parts = (
        (acc2, nt(h1x, px)),
        (acc1, nt(fx, jnp.concatenate([qx, px], axis=0))),
        (acc3, nt(dx, stacked(h2))),
        (accb, sum(d[:, j * LANES : (j + 1) * LANES] for j in range(CH // LANES))),
    )
    for ref, value in parts:
        if first:
            ref[...] = value
        else:
            ref[...] = ref[...] + value
    return df


def write_pack(pack, acc2, acc1, acc3, accb, pad_ref):
    pack[0:HID, :] = four_blocks(acc2[...], HID)
    d = acc1[...]
    w1 = four_blocks(d[:, : 2 * HID], KP)
    pack[HID : HID + 24, :] = w1[0:24]
    d3 = acc3[...]
    w3 = four_blocks(d3, KP)
    pack[HID + 24 : HID + 48, :] = w3[0:24]
    b2 = four_blocks(d[:, 2 * HID :], KP)[Q : Q + 1]
    pad_ref[...] = jnp.zeros((HID, HID), F32)
    pad_ref[0:KP, :] = accb[...]
    b3 = jnp.sum(jnp.transpose(pad_ref[...]), axis=0, keepdims=True)
    pack[HID + 21 : HID + 22, :] = b2
    pack[HID + 22 : HID + 23, :] = b3


def forward_kernel(
    f_in, t_in, code_in, adj_in, w1_in, b1_in, w2_in, b2_in, w3_in, b3_in,
    post, h1s, h2s, xp, xm, yp, ym,
    feat, outs, pad, f, t, code, adj, w1, b1, w2, b2, w3, b3, sems,
):
    ins = (w1_in, b1_in, w2_in, b2_in, w3_in, b3_in, f_in, t_in, code_in, adj_in)
    here = (w1, b1, w2, b2, w3, b3, f, t, code, adj)
    copies = [pltpu.make_async_copy(a, b, sems.at[k]) for k, (a, b) in enumerate(zip(ins, here))]
    for c in copies:
        c.start()
    for c in copies[:6]:
        c.wait()
    l1 = left_narrow(jnp.transpose(transposed(w1, b1, pad)))
    l2 = left(jnp.transpose(w2[...]))
    pad[...] = jnp.zeros((HID, HID), F32)
    pad[0:Q, :] = w3[...]
    l3 = left(pad[0:KP, :])
    b2t = wide(column(b2, HID, pad))
    b3t = wide(column(b3, Q, pad)[0:KP])
    copies[6].wait()
    fill_features(feat, f)
    n = CH // LANES
    for c in range(ROWS * LANES // CH):
        fx = stacked(across(feat, c * n, n))
        h1, h1x, h2 = hidden(fx, l1, l2, b2t)
        h1s[c] = h1
        h2s[c] = h2
        back(outs, c * n, product(l3, stacked(h2), KP) + b3t)
    for c in copies[7:]:
        c.wait()
    put_messages(lambda i, x: tile(adj, i, x), -1, xp, xm, yp, ym, 48, 12)
    fluid = code[...] == 0
    warm = t[...]
    for i in range(Q):
        k = i * ROWS
        relaxed = f[k : k + ROWS, :] + outs[k : k + ROWS, :]
        if BUOYANCY[i]:
            relaxed = relaxed + BUOYANCY[i] * warm
        o = OPPOSITE[i] * ROWS
        post[k : k + ROWS, :] = jnp.where(fluid, relaxed, f[o : o + ROWS, :])
    put_messages(lambda i, x: tile(post, i, x), 1, xp, xm, yp, ym, 0, 0)
    xp[40:48, :] = t[8:16, :]
    xm[40:48, :] = t[0:8, :]
    for x in range(2):
        yp[10 + x : 11 + x, :] = t[8 * x + 7 : 8 * x + 8, :]
        ym[10 + x : 11 + x, :] = t[8 * x : 8 * x + 1, :]


def left_narrow(w):
    hi, lo = split(w + pltpu.roll(w, KP, 1))
    return jnp.concatenate([hi, lo], axis=0)[:, : 2 * KP]


def rims_of(below, above, leftward, rightward, at, row):
    return (
        below[at : at + 8, :],
        above[at : at + 8, :],
        [leftward[row + x : row + x + 1, :] for x in range(2)],
        [rightward[row + x : row + x + 1, :] for x in range(2)],
    )


def stream_kernel(post, f, t, code, below, above, leftward, rightward, f1, t1):
    halo = (below, above, leftward, rightward, 0, 0, 88)
    for i in range(Q):
        for x in range(2):
            k = i * ROWS + 8 * x
            f1[k : k + 8, :] = streamed(post, halo, 1, i, x)
    rims = rims_of(below, above, leftward, rightward, 40, 10)
    for x in range(2):
        u = motion(f, x)
        here = t[8 * x : 8 * x + 8, :]
        total = 0.4 * here
        for a, (plus, minus) in enumerate(warm_neighbours(t, rims, x)):
            total = total + (CONDUCTIVITY - 0.5 * u[a]) * plus
            total = total + (CONDUCTIVITY + 0.5 * u[a]) * minus
        kind = code[8 * x : 8 * x + 8, :]
        t1[8 * x : 8 * x + 8, :] = jnp.where(
            kind == 0, total, jnp.where(kind == 1, here, HEATER)
        )


def collision_gradient(adj, halo, code, grad, masked, lift):
    for x in range(2):
        fluid = code[8 * x : 8 * x + 8, :] == 0
        total = None
        for i in range(Q):
            k = i * ROWS + 8 * x
            g = streamed(adj, halo, -1, i, x)
            grad[k : k + 8, :] = g
            g = jnp.where(fluid, g, 0.0)
            masked[k : k + 8, :] = g
            if BUOYANCY[i]:
                total = BUOYANCY[i] * g if total is None else total + BUOYANCY[i] * g
        lift[8 * x : 8 * x + 8, :] = total
    masked[Q * ROWS :, :] = jnp.zeros(((KP - Q) * ROWS, LANES), F32)


def back_weights(w1, w2, w3, pad):
    pad[...] = jnp.zeros((HID, HID), F32)
    pad[0:Q, :] = w3[...]
    w3b = left_narrow(jnp.transpose(pad[...]))
    w2b = left(w2[...])
    pad[...] = jnp.zeros((HID, HID), F32)
    pad[0:Q, :] = w1[...]
    w1b = left(pad[0:KP, :])
    return w3b, w2b, w1b


def last_step_kernel(
    f, adj, below, above, leftward, rightward, code, w1, b1, w2, b2, w3,
    fbar, lift, pack,
    feat, grad, masked, dfs, pad, acc2, acc1, acc3, accb,
):
    halo = (below, above, leftward, rightward, 48, 12, 90)
    collision_gradient(adj, halo, code, grad, masked, lift)
    fill_features(feat, f)
    l1 = left_narrow(jnp.transpose(transposed(w1, b1, pad)))
    l2 = left(jnp.transpose(w2[...]))
    b2t = wide(column(b2, HID, pad))
    w3b, w2b, w1b = back_weights(w1, w2, w3, pad)
    n = CH // LANES
    for c in range(ROWS * LANES // CH):
        fx = stacked(across(feat, c * n, n))
        h1, h1x, h2 = hidden(fx, l1, l2, b2t)
        d = across(masked, c * n, n)
        df = network_back(fx, h1, h1x, h2, d, w3b, w2b, w1b, acc2, acc1, acc3, accb, c == 0)
        back(dfs, c * n, df)
    fluid = code[...] == 0
    for i in range(Q):
        k, o = i * ROWS, OPPOSITE[i] * ROWS
        fbar[k : k + ROWS, :] = jnp.where(
            fluid, grad[k : k + ROWS, :] + dfs[k : k + ROWS, :], grad[o : o + ROWS, :]
        )
    write_pack(pack, acc2, acc1, acc3, accb, pad)


def halves(ref):
    return [ref[0:8, :], ref[8:16, :]]


def coefficient(u, a, s, kind):
    return jnp.where(kind == 0, CONDUCTIVITY - (0.5 * s) * u[a], 0.0)


def adjoint_parts(fbar, lift, f1, t1, theta, code, t_rims, flux_rims):
    codes, thetas = halves(code), halves(theta)
    liquids = [jnp.where(k == 0, v, 0.0) for k, v in zip(codes, thetas)]
    us = [motion(f1, x) for x in range(2)]
    ubar = motion_adjoint(t1, t_rims, liquids)
    warm = heat_adjoint(us, liquids, thetas, codes, flux_rims)
    warm = [v + w for v, w in zip(warm, halves(lift))]

    def adj(i, x):
        return with_motion(tile(fbar, i, x), ubar[x], i)

    return codes, liquids, us, adj, warm


def no_rims():
    blank, row = jnp.zeros((8, LANES), F32), jnp.zeros((1, LANES), F32)
    return blank, blank, [row, row], [row, row]


def rows_of(ref, at):
    return [ref[at + x : at + x + 1, :] for x in range(2)]


def along_y_kernel(fbar, lift, f1, t1, f0, theta, code, yp, ym):
    codes, liquids, us, adj, warm = adjoint_parts(
        fbar, lift, f1, t1, theta, code, no_rims(), no_rims()
    )
    ts = halves(t1)
    for s, e, out in ((1, 7, yp), (-1, 0, ym)):
        for x in range(2):
            u0 = motion(f0, x)
            parts = [adj(i, x) for i in moving(1, s, -1)]
            parts += [ts[x], flux(us[x], 1, s, liquids[x]), liquids[x], warm[x]]
            parts.append(coefficient(u0, 1, s, codes[x]))
            for k, v in enumerate(parts):
                out[2 * k + x : 2 * k + x + 1, :] = v[e : e + 1]
        out[20:21, :] = flux(us[1], 0, 1, liquids[1])[e : e + 1]
        out[21:22, :] = flux(us[0], 0, -1, liquids[0])[e : e + 1]


def along_x_kernel(
    fbar, lift, f1, t1, f0, theta, code, leftward, rightward, xp, xm, yl, yr
):
    zero, _, _, _ = no_rims()
    codes, liquids, us, adj, warm = adjoint_parts(
        fbar, lift, f1, t1, theta, code,
        (zero, zero, rows_of(leftward, 10), rows_of(rightward, 10)),
        (zero, zero, rows_of(leftward, 12), rows_of(rightward, 12)),
    )
    ts = halves(t1)
    for s, x, out in ((1, 1, xp), (-1, 0, xm)):
        parts = [adj(i, x) for i in moving(0, s, -1)]
        parts += [ts[x], liquids[x], warm[x]]
        parts.append(coefficient(motion(f0, x), 0, s, codes[x]))
        parts.append(flux(us[x], 0, s, liquids[x]))
        for k, v in enumerate(parts):
            out[8 * k : 8 * k + 8, :] = v
    for k, (s, e, come, out) in enumerate(((1, 0, leftward, yl), (-1, 7, rightward, yr))):
        t_come, flux_come, liquid, warm_come, factor = (
            rows_of(come, 10 + 2 * j) for j in range(5)
        )
        for x in range(2):
            for j in range(5):
                r = 2 * j + x
                out[r : r + 1, :] = (
                    come[r : r + 1, :] + 0.5 * liquid[x] * ts[x][e : e + 1]
                )
            done = warm_come[x] + flux(us[x], 1, -s, liquids[x])[e : e + 1]
            for j, v in enumerate((t_come[x], liquid[x], done, factor[x], flux_come[x])):
                r = 10 + 2 * j + x
                out[r : r + 1, :] = v
        for sx, x, to in ((1, 1, xp), (-1, 0, xm)):
            r = 2 * moving(1, s, -1).index(diagonal(sx, s, -1)) + x
            for j, v in enumerate(
                (out[r : r + 1, :], liquid[x], t_come[x], come[21 - x : 22 - x, :])
            ):
                to[80 + 4 * k + j : 81 + 4 * k + j, :] = v


def complete(
    fbar, lift, f1, t1, theta, code, below, above, yl, yr,
    adj1, warm1, hbelow, habove, hleft, hright,
):
    _, liquids, us, adj, warm = adjoint_parts(
        fbar, lift, f1, t1, theta, code,
        (below[40:48, :], above[40:48, :], rows_of(yl, 10), rows_of(yr, 10)),
        (below[72:80, :], above[72:80, :], rows_of(yl, 18), rows_of(yr, 18)),
    )
    ts = halves(t1)
    for x in range(2):
        warm1[8 * x : 8 * x + 8, :] = warm[x]
        for i in range(Q):
            k = i * ROWS + 8 * x
            adj1[k : k + 8, :] = adj(i, x)
    faces = []
    for s, x, come, out in ((1, 0, below, hbelow), (-1, 1, above, habove)):
        for k in range(5):
            out[8 * k : 8 * k + 8, :] = (
                come[8 * k : 8 * k + 8, :] + 0.5 * come[48:56, :] * ts[x]
            )
        for k, rows in enumerate((yl, yr)):
            j = 80 + 4 * k
            out[40 + k : 41 + k, :] = (
                come[j : j + 1, :] + 0.5 * come[j + 1 : j + 2, :] * rows[10 + x : 11 + x, :]
            )
        faces.append(come[64:72, :] * (come[56:64, :] + flux(us[x], 0, -s, liquids[x])))
    edges = []
    for k, (s, rows, out) in enumerate(((1, yl, hleft), (-1, yr, hright))):
        j = 80 + 4 * k
        out[0:10, :] = rows[0:10, :]
        edge = []
        for sx, x, come in ((1, 0, below), (-1, 1, above)):
            r = 2 * moving(1, s, -1).index(diagonal(sx, s, -1)) + x
            out[r : r + 1, :] = (
                rows[r : r + 1, :]
                - 0.5 * rows[12 + x : 13 + x, :] * come[j + 2 : j + 3, :]
            )
            edge.append(
                rows[16 + x : 17 + x, :]
                * (rows[14 + x : 15 + x, :] + come[j + 3 : j + 4, :])
            )
        edges.append(edge)
    return (*faces, *edges)


def halves(ref):
    return [ref[0:8, :], ref[8:16, :]]


def first_step_kernel(
    scale,
    fbar1, lift1, f1, t1, theta2, f, t, below, above, yl, yr,
    tbelow, tabove, tleft, tright, code, h1s, h2s, w1, w2, w3, pack1,
    fbar, thetabar, pack,
    feat, grad, masked, dfs, pad, acc2, acc1, acc3, accb, lift, total,
    adj, theta, hbelow, habove, hleft, hright,
):
    flux_rims = complete(
        fbar1, lift1, f1, t1, theta2, code, below, above, yl, yr,
        adj, theta, hbelow, habove, hleft, hright,
    )
    halo = (hbelow, habove, hleft, hright, 0, 0, 40)
    collision_gradient(adj, halo, code, grad, masked, lift)
    fill_features(feat, f)
    w3b, w2b, w1b = back_weights(w1, w2, w3, pad)
    n = CH // LANES
    for c in range(ROWS * LANES // CH):
        fx = stacked(across(feat, c * n, n))
        h1 = h1s[c]
        d = across(masked, c * n, n)
        df = network_back(
            fx, h1, stacked(h1), h2s[c], d, w3b, w2b, w1b, acc2, acc1, acc3, accb, c == 0
        )
        back(dfs, c * n, df)
    write_pack(total, acc2, acc1, acc3, accb, pad)
    parts, part, _ = pack.shape
    total[PACK:, :] = jnp.zeros((parts * part - PACK, HID), F32)
    total[0:PACK, :] = (total[0:PACK, :] + pack1[...]) * scale
    for k in range(parts):
        pack[k] = total[k * part : (k + 1) * part, :]
    codes, thetas = halves(code), halves(theta)
    liquids = [jnp.where(k == 0, v, 0.0) for k, v in zip(codes, thetas)]
    rims = rims_of(tbelow, tabove, tleft, tright, 40, 10)
    ubar = motion_adjoint(t, rims, liquids)
    new = heat_adjoint([motion(f, x) for x in range(2)], liquids, thetas, codes, flux_rims)
    for x in range(2):
        thetabar[8 * x : 8 * x + 8, :] = new[x] + lift[8 * x : 8 * x + 8, :]
        fluid = codes[x] == 0
        for i in range(Q):
            k, o = i * ROWS + 8 * x, OPPOSITE[i] * ROWS + 8 * x
            value = jnp.where(fluid, grad[k : k + 8, :] + dfs[k : k + 8, :], grad[o : o + 8, :])
            fbar[k : k + 8, :] = with_motion(value, ubar[x], i)


def struct(*shape):
    return jax.ShapeDtypeStruct(shape, F32)


def call(kernel, outs, scratch, name, more=(), **specs):
    return pl.pallas_call(
        kernel,
        out_shape=outs,
        scratch_shapes=[pltpu.VMEM(s, F32) for s in scratch] + list(more),
        **specs,
        compiler_params=pltpu.CompilerParams(vmem_limit_bytes=40 * 1024 * 1024),
        name=name,
    )


FULL = (KP * ROWS, LANES)
POPS = struct(Q * ROWS, LANES)
WARM = struct(ROWS, LANES)


def shifted(value, axis, by):
    count = lax.axis_size(axis)
    return lax.ppermute(value, axis, [(s, (s + by) % count) for s in range(count)])


def along(axis, plus, minus):
    return shifted(plus, axis, 1), shifted(minus, axis, -1)


def edge_kernel(blocks, xp, xm, leftward, rightward, xp_out, xm_out):
    xp_out[...] = xp[...]
    xm_out[...] = xm[...]
    for orient, row, at in blocks:
        put_corners(leftward, rightward, orient, xp_out, xm_out, row, at)


def exchange(xp, xm, yp, ym, blocks):
    leftward, rightward = along("gy", yp, ym)
    xp, xm = call(
        lambda *refs: edge_kernel(blocks, *refs),
        [struct(*xp.shape), struct(*xm.shape)],
        [],
        "edge",
    )(xp, xm, leftward, rightward)
    below, above = along("gx", xp, xm)
    return below, above, leftward, rightward


def swapped(value, groups):
    return lax.all_to_all(
        value, ("gx", "gy"), 0, 0, axis_index_groups=groups, tiled=True
    )


def outer_of(nx):
    return nx // 24 if nx % 24 == 0 else (2 if nx % 2 == 0 else 1)


def groups_of(nx, ny):
    outer = outer_of(nx)
    at = np.arange(nx * ny).reshape(outer, nx // outer, ny)
    return (
        at.transpose(1, 0, 2).reshape(nx // outer, outer * ny).tolist(),
        at.transpose(0, 2, 1).reshape(outer * ny, nx // outer).tolist(),
    )


def total_kernel(parts, out):
    value = parts[0]
    for k in range(1, parts.shape[0]):
        value = value + parts[k]
    for k in range(out.shape[0]):
        out[k] = value


def summed(parts, copies):
    return call(total_kernel, struct(copies, *parts.shape[1:]), [], "total")(parts)


def reduced(pack):
    share, same = groups_of(lax.axis_size("gx"), lax.axis_size("gy"))
    part = summed(swapped(pack, share), len(same[0]))
    part = summed(swapped(part, same), len(share[0]))
    return swapped(part, share)


def unpack_kernel(parts, w1, b1, w2, b2, w3, b3, pack):
    count, part, _ = parts.shape
    for k in range(count):
        pack[k * part : (k + 1) * part, :] = parts[k]
    w2[...] = pack[0:HID, :]
    w1[...] = pack[HID : HID + Q, :]
    b1[...] = pack[HID + Q : HID + Q + 1, :]
    b2[...] = pack[HID + 21 : HID + 22, :]
    b3[...] = pack[HID + 22 : HID + 23, 0:Q]
    w3[...] = pack[HID + 24 : HID + 24 + Q, :]


def per_device(f, t, code, w1, b1, w2, b2, w3, b3, adj, theta):
    sx, sy, sz = t.shape
    cells = sx * lax.axis_size("gx") * sy * lax.axis_size("gy") * sz
    f, adj = f.reshape(Q * ROWS, LANES), adj.reshape(Q * ROWS, LANES)
    t, code, theta = (v.reshape(ROWS, LANES) for v in (t, code, theta))
    b1, b2, b3 = (v.reshape(1, -1) for v in (b1, b2, b3))
    w3 = w3.T
    chunks = struct(ROWS * LANES // CH, HID, CH)
    outs = call(
        forward_kernel,
        [POPS, chunks, chunks, struct(96, LANES), struct(96, LANES), struct(24, LANES), struct(24, LANES)],
        [FULL, FULL, (HID, HID)],
        "forward",
        [pltpu.VMEM(v.shape, v.dtype) for v in (f, t, code, adj, w1, b1, w2, b2, w3, b3)]
        + [pltpu.SemaphoreType.DMA((10,))],
        in_specs=[pl.BlockSpec(memory_space=pltpu.HBM)] * 10,
    )(*(pltpu.with_memory_space_constraint(v, pltpu.HBM) for v in (f, t, code, adj, w1, b1, w2, b2, w3, b3)))
    post, h1s, h2s = outs[:3]
    halo0 = exchange(*outs[3:], ((1, 0, 88), (-1, 12, 90)))
    f1, t1 = call(stream_kernel, [POPS, WARM], [], "stream")(post, f, t, code, *halo0)
    accs = [(2 * HID, 2 * HID), (2 * KP, 4 * HID), (2 * KP, 2 * HID), (KP, LANES)]
    fbar, lift, pack1 = call(
        last_step_kernel,
        [POPS, WARM, struct(PACK, HID)],
        [FULL, (Q * ROWS, LANES), FULL, FULL, (HID, HID), *accs],
        "last_step",
    )(f1, adj, *halo0, code, w1, b1, w2, b2, w3)
    known = (fbar, lift, f1, t1, f, theta, code)
    yp, ym = call(along_y_kernel, [struct(24, LANES)] * 2, [], "along_y")(*known)
    come = along("gy", yp, ym)
    xp, xm, yl, yr = call(
        along_x_kernel, [struct(88, LANES)] * 2 + [struct(24, LANES)] * 2, [], "along_x"
    )(*known, *come)
    faces = along("gx", xp, xm)
    scale = 1.0 / math.sqrt(cells)
    parts = outer_of(lax.axis_size("gx")) * lax.axis_size("gy")
    part = -(-(PACK + 8) // parts)
    fbar0, theta0, pack = call(
        lambda *refs: first_step_kernel(scale, *refs),
        [POPS, WARM, struct(parts, part, HID)],
        [FULL, (Q * ROWS, LANES), FULL, FULL, (HID, HID), *accs, (ROWS, LANES), (parts * part, HID),
         (Q * ROWS, LANES), (ROWS, LANES), (48, LANES), (48, LANES), (16, LANES), (16, LANES)],
        "first_step",
    )(fbar, lift, f1, t1, theta, f, t, *faces, yl, yr, *halo0, code, h1s, h2s, w1, w2, w3, pack1)
    total = reduced(pack)
    g1, gb1, g2, gb2, g3, gb3 = call(
        unpack_kernel,
        [struct(Q, HID), struct(1, HID), struct(HID, HID), struct(1, HID), struct(Q, HID), struct(1, Q)],
        [(parts * part, HID)],
        "unpack",
    )(total)
    return (
        fbar0.reshape(Q, sx, sy, sz),
        theta0.reshape(sx, sy, sz),
        g1,
        gb1.reshape(HID),
        g2,
        gb2.reshape(HID),
        g3.T,
        gb3.reshape(Q),
    )


def solution(mesh):
    pops, cells = P(None, "gx", "gy", None), P("gx", "gy", None)
    return jax.shard_map(
        per_device,
        mesh=mesh,
        in_specs=(pops, cells, cells, P(), P(), P(), P(), P(), P(), pops, cells),
        out_specs=(pops, cells, P(), P(), P(), P(), P(), P()),
        check_vma=False,
    )
```

```python
import math

import jax
import jax.numpy as jnp
import numpy as np
from jax import lax
from jax.experimental import pallas as pl
from jax.experimental.pallas import tpu as pltpu
from jax.sharding import PartitionSpec as P

VELOCITIES = [
    (0, 0, 0), (1, 0, 0), (-1, 0, 0), (0, 1, 0), (0, -1, 0), (0, 0, 1), (0, 0, -1),
    (1, 1, 0), (-1, -1, 0), (1, -1, 0), (-1, 1, 0), (1, 0, 1), (-1, 0, -1), (1, 0, -1),
    (-1, 0, 1), (0, 1, 1), (0, -1, -1), (0, 1, -1), (0, -1, 1),
]
Q = 19
OPPOSITE = [VELOCITIES.index((-a, -b, -c)) for a, b, c in VELOCITIES]
WEIGHTS = [1.0 / 3.0] + [1.0 / 18.0] * 6 + [1.0 / 36.0] * 12
BUOYANCY = [float(np.float32(0.3 * w * c[2])) for w, c in zip(WEIGHTS, VELOCITIES)]
CONDUCTIVITY = 0.1
HOT_WALL = 0.5
COLD_WALL = -0.5
HEATER = 0.5
HID = 128
KP = 32
ROWS = 16
LANES = 128
CH = 512
PACK = 176
F32 = jnp.float32
BF16 = jnp.bfloat16


def moving(axis, sign, orient):
    return [i for i in range(Q) if VELOCITIES[i][axis] * orient == sign]


def diagonal(sx, sy, orient):
    return VELOCITIES.index((sx * orient, sy * orient, 0))


def split(x):
    hi = x.astype(BF16)
    lo = (x - hi.astype(F32)).astype(BF16)
    return hi, lo


def stacked(x):
    return jnp.concatenate(split(x), axis=0)


def nn(a, b):
    return lax.dot_general(a, b, (((1,), (0,)), ((), ())), preferred_element_type=F32)


def nt(a, b):
    return lax.dot_general(a, b, (((1,), (1,)), ((), ())), preferred_element_type=F32)


def left(w):
    hi, lo = split(w)
    return jnp.concatenate(
        [jnp.concatenate([hi, hi], axis=1), jnp.concatenate([lo, lo], axis=1)], axis=0
    )


def product(a, b, rows):
    d = nn(a, b)
    return d[:rows] + d[rows:]


def four_blocks(d, rows):
    return d[:rows, :HID] + d[:rows, HID:] + d[rows:, :HID] + d[rows:, HID:]


def lanes_of(shape):
    return lax.broadcasted_iota(jnp.int32, shape, 1)


def subs_of(shape):
    return lax.broadcasted_iota(jnp.int32, shape, 0)


def shift_z(v, step, fill):
    if step == 1:
        return jnp.where(lanes_of(v.shape) == 0, fill, pltpu.roll(v, 1, 1))
    return jnp.where(lanes_of(v.shape) == LANES - 1, fill, pltpu.roll(v, LANES - 1, 1))


def shift_y(v, step, row):
    if step == 1:
        return jnp.where(subs_of(v.shape) == 0, row, pltpu.roll(v, 1, 0))
    return jnp.where(subs_of(v.shape) == 7, row, pltpu.roll(v, 7, 0))


def tile(ref, i, x):
    if isinstance(ref, tuple):
        return ref[x][8 * i : 8 * i + 8, :]
    k = i * ROWS + x * 8
    return ref[k : k + 8, :]


def halves(ref):
    if isinstance(ref, tuple):
        return [ref[0][...], ref[1][...]]
    return [ref[0:8, :], ref[8:16, :]]


def transposed(w_ref, b_ref, pad_ref):
    pad_ref[...] = jnp.zeros((HID, HID), F32)
    pad_ref[0:Q, :] = w_ref[...]
    if b_ref is not None:
        pad_ref[Q : Q + 1, :] = b_ref[...]
    return pad_ref[...]


def column(b_ref, n, pad_ref):
    pad_ref[...] = jnp.zeros((HID, HID), F32)
    pad_ref[:, 0:n] = jnp.broadcast_to(b_ref[...], (HID, n))
    return jnp.transpose(pad_ref[...])


def across(ref, c):
    n, step = CH // LANES, ref.shape[0] // KP
    return jnp.concatenate(
        [ref[pl.ds(c * n + j, KP, stride=step), :] for j in range(n)], axis=1
    )


def back(ref, c, value):
    n, step = CH // LANES, ref.shape[0] // KP
    for j in range(n):
        ref[pl.ds(c * n + j, KP, stride=step), :] = value[:, j * LANES : (j + 1) * LANES]


def fill_features(s_ref, f_ref):
    rows = s_ref.shape[0] // KP
    s_ref[0 : Q * rows, :] = f_ref[...]
    s_ref[Q * rows : (Q + 1) * rows, :] = jnp.ones((rows, LANES), F32)
    s_ref[(Q + 1) * rows :, :] = jnp.zeros(((KP - Q - 1) * rows, LANES), F32)


def wide(b):
    return jnp.concatenate([b] * (CH // LANES), axis=1)


def put_messages(value, orient, xp, xm, yp, ym, at, row):
    for k, i in enumerate(moving(0, 1, orient)):
        xp[at + 8 * k : at + 8 * k + 8, :] = value(i, 1)
    for k, i in enumerate(moving(0, -1, orient)):
        xm[at + 8 * k : at + 8 * k + 8, :] = value(i, 0)
    for k, i in enumerate(moving(1, 1, orient)):
        for x in range(2):
            yp[row + 2 * k + x : row + 2 * k + x + 1, :] = value(i, x)[7:8]
    for k, i in enumerate(moving(1, -1, orient)):
        for x in range(2):
            ym[row + 2 * k + x : row + 2 * k + x + 1, :] = value(i, x)[0:1]


def put_corners(leftward, rightward, orient, xp, xm, row, at):
    for sx, to in ((1, xp), (-1, xm)):
        for k, (sy, come) in enumerate(((1, leftward), (-1, rightward))):
            j = row + 2 * moving(1, sy, orient).index(diagonal(sx, sy, orient)) + (sx == 1)
            to[at + k : at + k + 1, :] = come[j : j + 1, :]


def streamed(ref, halo, orient, i, x):
    below, above, leftward, rightward, at, row, corner = halo
    sx, sy, sz = (orient * c for c in VELOCITIES[i])
    xs = x - sx
    if xs in (0, 1):
        v = tile(ref, i, xs)
    else:
        k = at + 8 * moving(0, sx, orient).index(i)
        v = (below if sx == 1 else above)[k : k + 8, :]
    if sy:
        if xs in (0, 1):
            k = row + 2 * moving(1, sy, orient).index(i) + xs
            edge = (leftward if sy == 1 else rightward)[k : k + 1, :]
        else:
            k = corner + (sy == -1)
            edge = (below if sx == 1 else above)[k : k + 1, :]
        v = shift_y(v, sy, edge)
    if sz:
        v = shift_z(v, sz, tile(ref, OPPOSITE[i], x))
    return v


def motion(ref, x):
    us = []
    for a in range(3):
        total = None
        for i in range(Q):
            c = VELOCITIES[i][a]
            if c:
                v = tile(ref, i, x)
                total = (v if c == 1 else -v) if total is None else (total + v if c == 1 else total - v)
        us.append(total)
    return us


def warm_neighbours(t_ref, rims, x):
    below, above, leftward, rightward = rims
    t = halves(t_ref)
    lower = below if x == 0 else t[0]
    upper = t[1] if x == 0 else above
    return [
        (upper, lower),
        (shift_y(t[x], -1, rightward[x]), shift_y(t[x], 1, leftward[x])),
        (shift_z(t[x], -1, COLD_WALL), shift_z(t[x], 1, HOT_WALL)),
    ]


def flux(u, a, s, liquid):
    return (CONDUCTIVITY - (0.5 * s) * u[a]) * liquid


def heat_adjoint(us, liquids, theta, codes, flux_rims):
    below, above, leftward, rightward = flux_rims
    out = []
    for x in range(2):
        u, liquid = us[x], liquids[x]
        total = 0.4 * liquid + jnp.where(codes[x] == 1, theta[x], 0.0)
        total = total + (below if x == 0 else flux(us[0], 0, 1, liquids[0]))
        total = total + (flux(us[1], 0, -1, liquids[1]) if x == 0 else above)
        total = total + shift_y(flux(u, 1, 1, liquid), 1, leftward[x])
        total = total + shift_y(flux(u, 1, -1, liquid), -1, rightward[x])
        total = total + shift_z(flux(u, 2, 1, liquid), 1, 0.0)
        total = total + shift_z(flux(u, 2, -1, liquid), -1, 0.0)
        out.append(total)
    return out


def motion_adjoint(t_ref, rims, liquids):
    return [
        [-0.5 * liquids[x] * (plus - minus) for plus, minus in warm_neighbours(t_ref, rims, x)]
        for x in range(2)
    ]


def with_motion(value, ubar, i):
    for a in range(3):
        c = VELOCITIES[i][a]
        if c:
            value = value + ubar[a] if c == 1 else value - ubar[a]
    return value


def hidden(fx, a1, a2, b2):
    h1 = jnp.tanh(product(a1, fx, HID))
    h1x = stacked(h1)
    h2 = jnp.tanh(product(a2, h1x, HID) + b2)
    return h1, h1x, h2


def network_back(h1, h2, d, w3b, w2b, w1b):
    dx = stacked(d)
    px = stacked(product(w3b, dx, HID) * (1.0 - h2 * h2))
    qx = stacked(product(w2b, px, HID) * (1.0 - h1 * h1))
    return product(w1b, qx, KP), dx, px, qx


def folded(d):
    return sum(d[:, j * LANES : (j + 1) * LANES] for j in range(CH // LANES))


def gather(accs, values, first):
    for ref, value in zip(accs, values):
        ref[...] = value if first else ref[...] + value


def weight_products(fx, h1x, h2x, dx, px, qx):
    return nt(h1x, px), nt(fx, jnp.concatenate([qx, px], axis=0)), nt(dx, h2x)


def write_pack(pack, acc2, acc1, acc3, accb, pad_ref):
    pack[0:HID, :] = four_blocks(acc2[...], HID)
    d = acc1[...]
    w1 = four_blocks(d[:, : 2 * HID], KP)
    pack[HID : HID + 24, :] = w1[0:24]
    d3 = acc3[...]
    w3 = four_blocks(d3, KP)
    pack[HID + 24 : HID + 48, :] = w3[0:24]
    b2 = four_blocks(d[:, 2 * HID :], KP)[Q : Q + 1]
    pad_ref[...] = jnp.zeros((HID, HID), F32)
    pad_ref[0:KP, :] = accb[...]
    b3 = jnp.sum(jnp.transpose(pad_ref[...]), axis=0, keepdims=True)
    pack[HID + 21 : HID + 22, :] = b2
    pack[HID + 22 : HID + 23, :] = b3


def forward_kernel(
    f_in, t_in, code_in, adj_in, w1_in, b1_in, w2_in, b2_in, w3_in, b3_in,
    post, h1s, h2s, xp, xm, yp, ym,
    feat, outs, pad, f, t, code, adj, w1, b1, w2, b2, w3, b3, sems,
):
    ins = (w1_in, b1_in, w2_in, b2_in, w3_in, b3_in, f_in, t_in, code_in, adj_in)
    here = (w1, b1, w2, b2, w3, b3, f, t, code, adj)
    copies = [pltpu.make_async_copy(a, b, sems.at[k]) for k, (a, b) in enumerate(zip(ins, here))]
    for c in copies:
        c.start()
    for c in copies[:6]:
        c.wait()
    l1 = left_narrow(jnp.transpose(transposed(w1, b1, pad)))
    l2 = left(jnp.transpose(w2[...]))
    pad[...] = jnp.zeros((HID, HID), F32)
    pad[0:Q, :] = w3[...]
    l3 = left(pad[0:KP, :])
    b2t = wide(column(b2, HID, pad))
    b3t = wide(column(b3, Q, pad)[0:KP])
    copies[6].wait()
    fill_features(feat, f)
    for c in range(ROWS * LANES // CH):
        fx = stacked(across(feat, c))
        h1, h1x, h2 = hidden(fx, l1, l2, b2t)
        h1s[c] = h1
        h2s[c] = h2
        back(outs, c, product(l3, stacked(h2), KP) + b3t)
    for c in copies[7:]:
        c.wait()
    put_messages(lambda i, x: tile(adj, i, x), -1, xp, xm, yp, ym, 48, 12)
    fluid = code[...] == 0
    warm = t[...]
    for i in range(Q):
        k = i * ROWS
        relaxed = f[k : k + ROWS, :] + outs[k : k + ROWS, :]
        if BUOYANCY[i]:
            relaxed = relaxed + BUOYANCY[i] * warm
        o = OPPOSITE[i] * ROWS
        post[k : k + ROWS, :] = jnp.where(fluid, relaxed, f[o : o + ROWS, :])
    put_messages(lambda i, x: tile(post, i, x), 1, xp, xm, yp, ym, 0, 0)
    xp[40:48, :] = t[8:16, :]
    xm[40:48, :] = t[0:8, :]
    for x in range(2):
        yp[10 + x : 11 + x, :] = t[8 * x + 7 : 8 * x + 8, :]
        ym[10 + x : 11 + x, :] = t[8 * x : 8 * x + 1, :]


def left_narrow(w):
    hi, lo = split(w + pltpu.roll(w, KP, 1))
    return jnp.concatenate([hi, lo], axis=0)[:, : 2 * KP]


def rims_of(below, above, leftward, rightward, at, row):
    return (
        below[at : at + 8, :],
        above[at : at + 8, :],
        [leftward[row + x : row + x + 1, :] for x in range(2)],
        [rightward[row + x : row + x + 1, :] for x in range(2)],
    )


def collision_gradient(adj, halo, code, grad, masked, lift):
    for x in range(2):
        fluid = code[8 * x : 8 * x + 8, :] == 0
        total = None
        for i in range(Q):
            k = i * ROWS + 8 * x
            g = streamed(adj, halo, -1, i, x)
            grad[k : k + 8, :] = g
            g = jnp.where(fluid, g, 0.0)
            masked[k : k + 8, :] = g
            if BUOYANCY[i]:
                total = BUOYANCY[i] * g if total is None else total + BUOYANCY[i] * g
        lift[8 * x : 8 * x + 8, :] = total
    masked[Q * ROWS :, :] = jnp.zeros(((KP - Q) * ROWS, LANES), F32)


def back_weights(w1, w2, w3, pad):
    pad[...] = jnp.zeros((HID, HID), F32)
    pad[0:Q, :] = w3[...]
    w3b = left_narrow(jnp.transpose(pad[...]))
    w2b = left(w2[...])
    pad[...] = jnp.zeros((HID, HID), F32)
    pad[0:Q, :] = w1[...]
    w1b = left(pad[0:KP, :])
    return w3b, w2b, w1b


def middle_kernel(
    x, post, f, t, code, adj, face, leftward, rightward, w1, b1, w2, b2, w3,
    f1, t1, fbar, lift, accb, fxs, h1xs, h2xs, dxs, pxs, qxs,
    feat, grad, masked, dfs, pad,
):
    kind = code[8 * x : 8 * x + 8, :]
    fluid = kind == 0
    halo = (face, face, leftward, rightward, 0, 0, 88)
    adj_halo = (face, face, leftward, rightward, 48, 12, 90)
    warmth = None
    for i in range(Q):
        k = 8 * i
        f1[k : k + 8, :] = streamed(post, halo, 1, i, x)
        g = streamed(adj, adj_halo, -1, i, x)
        grad[k : k + 8, :] = g
        g = jnp.where(fluid, g, 0.0)
        masked[k : k + 8, :] = g
        if BUOYANCY[i]:
            warmth = BUOYANCY[i] * g if warmth is None else warmth + BUOYANCY[i] * g
    lift[...] = warmth
    masked[8 * Q :, :] = jnp.zeros(((KP - Q) * 8, LANES), F32)
    u = motion(f, x)
    here = t[8 * x : 8 * x + 8, :]
    total = 0.4 * here
    rims = rims_of(face, face, leftward, rightward, 40, 10)
    for a, (plus, minus) in enumerate(warm_neighbours(t, rims, x)):
        total = total + (CONDUCTIVITY - 0.5 * u[a]) * plus
        total = total + (CONDUCTIVITY + 0.5 * u[a]) * minus
    t1[...] = jnp.where(fluid, total, jnp.where(kind == 1, here, HEATER))
    fill_features(feat, f1)
    l1 = left_narrow(jnp.transpose(transposed(w1, b1, pad)))
    l2 = left(jnp.transpose(w2[...]))
    b2t = wide(column(b2, HID, pad))
    w3b, w2b, w1b = back_weights(w1, w2, w3, pad)
    for c in range(8 * LANES // CH):
        fx = stacked(across(feat, c))
        h1, h1x, h2 = hidden(fx, l1, l2, b2t)
        d = across(masked, c)
        df, dx, px, qx = network_back(h1, h2, d, w3b, w2b, w1b)
        gather((accb,), (folded(d),), c == 0)
        back(dfs, c, df)
        fxs[c], h1xs[c], h2xs[c] = fx, h1x, stacked(h2)
        dxs[c], pxs[c], qxs[c] = dx, px, qx
    for i in range(Q):
        k, o = 8 * i, 8 * OPPOSITE[i]
        fbar[k : k + 8, :] = jnp.where(
            fluid, grad[k : k + 8, :] + dfs[k : k + 8, :], grad[o : o + 8, :]
        )


def weights_kernel(*refs):
    first, second, (_, pack, pad, accb, *accs) = refs[:7], refs[7:14], refs[14:]
    accb[...] = first[0][...] + second[0][...]
    for plane in (first, second):
        for c in range(plane[1].shape[0]):
            values = weight_products(*(v[c] for v in plane[1:]))
            gather(accs, values, plane is first and c == 0)
    write_pack(pack, *accs, accb, pad)


def coefficient(u, a, s, kind):
    return jnp.where(kind == 0, CONDUCTIVITY - (0.5 * s) * u[a], 0.0)


def adjoint_parts(fbar, lift, f1, t1, theta, code, t_rims, flux_rims):
    codes, thetas = halves(code), halves(theta)
    liquids = [jnp.where(k == 0, v, 0.0) for k, v in zip(codes, thetas)]
    us = [motion(f1, x) for x in range(2)]
    ubar = motion_adjoint(t1, t_rims, liquids)
    warm = heat_adjoint(us, liquids, thetas, codes, flux_rims)
    warm = [v + w for v, w in zip(warm, halves(lift))]

    def adj(i, x):
        return with_motion(tile(fbar, i, x), ubar[x], i)

    return codes, liquids, us, adj, warm


def no_rims():
    blank, row = jnp.zeros((8, LANES), F32), jnp.zeros((1, LANES), F32)
    return blank, blank, [row, row], [row, row]


def rows_of(ref, at):
    return [ref[at + x : at + x + 1, :] for x in range(2)]


def paired(refs):
    return [tuple(refs[2 * k : 2 * k + 2]) for k in range(4)]


def along_y_kernel(*refs):
    fbar, lift, f1, t1 = paired(refs)
    f0, theta, code, yp, ym = refs[8:]
    codes, liquids, us, adj, warm = adjoint_parts(
        fbar, lift, f1, t1, theta, code, no_rims(), no_rims()
    )
    ts = halves(t1)
    for s, e, out in ((1, 7, yp), (-1, 0, ym)):
        for x in range(2):
            u0 = motion(f0, x)
            parts = [adj(i, x) for i in moving(1, s, -1)]
            parts += [ts[x], flux(us[x], 1, s, liquids[x]), liquids[x], warm[x]]
            parts.append(coefficient(u0, 1, s, codes[x]))
            for k, v in enumerate(parts):
                out[2 * k + x : 2 * k + x + 1, :] = v[e : e + 1]
        out[20:21, :] = flux(us[1], 0, 1, liquids[1])[e : e + 1]
        out[21:22, :] = flux(us[0], 0, -1, liquids[0])[e : e + 1]


def along_x_kernel(*refs):
    fbar, lift, f1, t1 = paired(refs)
    f0, theta, code, leftward, rightward, xp, xm, yl, yr = refs[8:]
    zero, _, _, _ = no_rims()
    codes, liquids, us, adj, warm = adjoint_parts(
        fbar, lift, f1, t1, theta, code,
        (zero, zero, rows_of(leftward, 10), rows_of(rightward, 10)),
        (zero, zero, rows_of(leftward, 12), rows_of(rightward, 12)),
    )
    ts = halves(t1)
    for s, x, out in ((1, 1, xp), (-1, 0, xm)):
        parts = [adj(i, x) for i in moving(0, s, -1)]
        parts += [ts[x], liquids[x], warm[x]]
        parts.append(coefficient(motion(f0, x), 0, s, codes[x]))
        parts.append(flux(us[x], 0, s, liquids[x]))
        for k, v in enumerate(parts):
            out[8 * k : 8 * k + 8, :] = v
    for k, (s, e, come, out) in enumerate(((1, 0, leftward, yl), (-1, 7, rightward, yr))):
        t_come, flux_come, liquid, warm_come, factor = (
            rows_of(come, 10 + 2 * j) for j in range(5)
        )
        for x in range(2):
            for j in range(5):
                r = 2 * j + x
                out[r : r + 1, :] = (
                    come[r : r + 1, :] + 0.5 * liquid[x] * ts[x][e : e + 1]
                )
            done = warm_come[x] + flux(us[x], 1, -s, liquids[x])[e : e + 1]
            for j, v in enumerate((t_come[x], liquid[x], done, factor[x], flux_come[x])):
                r = 10 + 2 * j + x
                out[r : r + 1, :] = v
        for sx, x, to in ((1, 1, xp), (-1, 0, xm)):
            r = 2 * moving(1, s, -1).index(diagonal(sx, s, -1)) + x
            for j, v in enumerate(
                (out[r : r + 1, :], liquid[x], t_come[x], come[21 - x : 22 - x, :])
            ):
                to[80 + 4 * k + j : 81 + 4 * k + j, :] = v


def complete(
    fbar, lift, f1, t1, theta, code, below, above, yl, yr,
    adj1, warm1, hbelow, habove, hleft, hright,
):
    _, liquids, us, adj, warm = adjoint_parts(
        fbar, lift, f1, t1, theta, code,
        (below[40:48, :], above[40:48, :], rows_of(yl, 10), rows_of(yr, 10)),
        (below[72:80, :], above[72:80, :], rows_of(yl, 18), rows_of(yr, 18)),
    )
    ts = halves(t1)
    for x in range(2):
        warm1[8 * x : 8 * x + 8, :] = warm[x]
        for i in range(Q):
            k = i * ROWS + 8 * x
            adj1[k : k + 8, :] = adj(i, x)
    faces = []
    for s, x, come, out in ((1, 0, below, hbelow), (-1, 1, above, habove)):
        for k in range(5):
            out[8 * k : 8 * k + 8, :] = (
                come[8 * k : 8 * k + 8, :] + 0.5 * come[48:56, :] * ts[x]
            )
        for k, rows in enumerate((yl, yr)):
            j = 80 + 4 * k
            out[40 + k : 41 + k, :] = (
                come[j : j + 1, :] + 0.5 * come[j + 1 : j + 2, :] * rows[10 + x : 11 + x, :]
            )
        faces.append(come[64:72, :] * (come[56:64, :] + flux(us[x], 0, -s, liquids[x])))
    edges = []
    for k, (s, rows, out) in enumerate(((1, yl, hleft), (-1, yr, hright))):
        j = 80 + 4 * k
        out[0:10, :] = rows[0:10, :]
        edge = []
        for sx, x, come in ((1, 0, below), (-1, 1, above)):
            r = 2 * moving(1, s, -1).index(diagonal(sx, s, -1)) + x
            out[r : r + 1, :] = (
                rows[r : r + 1, :]
                - 0.5 * rows[12 + x : 13 + x, :] * come[j + 2 : j + 3, :]
            )
            edge.append(
                rows[16 + x : 17 + x, :]
                * (rows[14 + x : 15 + x, :] + come[j + 3 : j + 4, :])
            )
        edges.append(edge)
    return (*faces, *edges)


def first_step_kernel(
    scale, known,
    theta2, f, t, below, above, yl, yr,
    tbelow, tabove, tleft, tright, code, h1s, h2s, w1, w2, w3, pack1,
    fbar, thetabar, pack,
    feat, grad, masked, dfs, pad, acc2, acc1, acc3, accb, lift, total,
    adj, theta, hbelow, habove, hleft, hright,
):
    flux_rims = complete(
        *paired(known), theta2, code, below, above, yl, yr,
        adj, theta, hbelow, habove, hleft, hright,
    )
    halo = (hbelow, habove, hleft, hright, 0, 0, 40)
    collision_gradient(adj, halo, code, grad, masked, lift)
    fill_features(feat, f)
    w3b, w2b, w1b = back_weights(w1, w2, w3, pad)
    for c in range(ROWS * LANES // CH):
        fx, h1, h2, d = stacked(across(feat, c)), h1s[c], h2s[c], across(masked, c)
        df, dx, px, qx = network_back(h1, h2, d, w3b, w2b, w1b)
        values = weight_products(fx, stacked(h1), stacked(h2), dx, px, qx)
        gather((acc2, acc1, acc3, accb), (*values, folded(d)), c == 0)
        back(dfs, c, df)
    write_pack(total, acc2, acc1, acc3, accb, pad)
    parts, part, _ = pack.shape
    total[PACK:, :] = jnp.zeros((parts * part - PACK, HID), F32)
    total[0:PACK, :] = (total[0:PACK, :] + pack1[...]) * scale
    for k in range(parts):
        pack[k] = total[k * part : (k + 1) * part, :]
    codes, thetas = halves(code), halves(theta)
    liquids = [jnp.where(k == 0, v, 0.0) for k, v in zip(codes, thetas)]
    rims = rims_of(tbelow, tabove, tleft, tright, 40, 10)
    ubar = motion_adjoint(t, rims, liquids)
    new = heat_adjoint([motion(f, x) for x in range(2)], liquids, thetas, codes, flux_rims)
    for x in range(2):
        thetabar[8 * x : 8 * x + 8, :] = new[x] + lift[8 * x : 8 * x + 8, :]
        fluid = codes[x] == 0
        for i in range(Q):
            k, o = i * ROWS + 8 * x, OPPOSITE[i] * ROWS + 8 * x
            value = jnp.where(fluid, grad[k : k + 8, :] + dfs[k : k + 8, :], grad[o : o + 8, :])
            fbar[k : k + 8, :] = with_motion(value, ubar[x], i)


def struct(*shape):
    return jax.ShapeDtypeStruct(shape, F32)


def call(kernel, outs, scratch, name, more=(), **specs):
    return pl.pallas_call(
        kernel,
        out_shape=outs,
        scratch_shapes=[pltpu.VMEM(s, F32) for s in scratch] + list(more),
        **specs,
        compiler_params=pltpu.CompilerParams(vmem_limit_bytes=40 * 1024 * 1024),
        name=name,
    )


FULL = (KP * ROWS, LANES)
POPS = struct(Q * ROWS, LANES)
WARM = struct(ROWS, LANES)


def shifted(value, axis, by):
    count = lax.axis_size(axis)
    return lax.ppermute(value, axis, [(s, (s + by) % count) for s in range(count)])


def along(axis, plus, minus):
    return shifted(plus, axis, 1), shifted(minus, axis, -1)


def edge_kernel(blocks, xp, xm, leftward, rightward, xp_out, xm_out):
    xp_out[...] = xp[...]
    xm_out[...] = xm[...]
    for orient, row, at in blocks:
        put_corners(leftward, rightward, orient, xp_out, xm_out, row, at)


def exchange(xp, xm, yp, ym, blocks):
    leftward, rightward = along("gy", yp, ym)
    xp, xm = call(
        lambda *refs: edge_kernel(blocks, *refs),
        [struct(*xp.shape), struct(*xm.shape)],
        [],
        "edge",
    )(xp, xm, leftward, rightward)
    below, above = along("gx", xp, xm)
    return below, above, leftward, rightward


def swapped(value, groups):
    return lax.all_to_all(
        value, ("gx", "gy"), 0, 0, axis_index_groups=groups, tiled=True
    )


def outer_of(nx):
    return nx // 24 if nx % 24 == 0 else (2 if nx % 2 == 0 else 1)


def groups_of(nx, ny):
    outer = outer_of(nx)
    at = np.arange(nx * ny).reshape(outer, nx // outer, ny)
    return (
        at.transpose(1, 0, 2).reshape(nx // outer, outer * ny).tolist(),
        at.transpose(0, 2, 1).reshape(outer * ny, nx // outer).tolist(),
    )


def total_kernel(parts, out):
    value = parts[0]
    for k in range(1, parts.shape[0]):
        value = value + parts[k]
    for k in range(out.shape[0]):
        out[k] = value


def summed(parts, copies):
    return call(total_kernel, struct(copies, *parts.shape[1:]), [], "total")(parts)


def reduced(pack):
    share, same = groups_of(lax.axis_size("gx"), lax.axis_size("gy"))
    part = summed(swapped(pack, share), len(same[0]))
    part = summed(swapped(part, same), len(share[0]))
    return swapped(part, share)


def unpack_kernel(parts, w1, b1, w2, b2, w3, b3, pack):
    count, part, _ = parts.shape
    for k in range(count):
        pack[k * part : (k + 1) * part, :] = parts[k]
    w2[...] = pack[0:HID, :]
    w1[...] = pack[HID : HID + Q, :]
    b1[...] = pack[HID + Q : HID + Q + 1, :]
    b2[...] = pack[HID + 21 : HID + 22, :]
    b3[...] = pack[HID + 22 : HID + 23, 0:Q]
    w3[...] = pack[HID + 24 : HID + 24 + Q, :]


def per_device(f, t, code, w1, b1, w2, b2, w3, b3, adj, theta):
    sx, sy, sz = t.shape
    cells = sx * lax.axis_size("gx") * sy * lax.axis_size("gy") * sz
    f, adj = f.reshape(Q * ROWS, LANES), adj.reshape(Q * ROWS, LANES)
    t, code, theta = (v.reshape(ROWS, LANES) for v in (t, code, theta))
    b1, b2, b3 = (v.reshape(1, -1) for v in (b1, b2, b3))
    w3 = w3.T
    chunks = struct(ROWS * LANES // CH, HID, CH)
    outs = call(
        forward_kernel,
        [POPS, chunks, chunks, struct(96, LANES), struct(96, LANES), struct(24, LANES), struct(24, LANES)],
        [FULL, FULL, (HID, HID)],
        "forward",
        [pltpu.VMEM(v.shape, v.dtype) for v in (f, t, code, adj, w1, b1, w2, b2, w3, b3)]
        + [pltpu.SemaphoreType.DMA((10,))],
        in_specs=[pl.BlockSpec(memory_space=pltpu.HBM)] * 10,
    )(*(pltpu.with_memory_space_constraint(v, pltpu.HBM) for v in (f, t, code, adj, w1, b1, w2, b2, w3, b3)))
    post, h1s, h2s = outs[:3]
    halo0 = exchange(*outs[3:], ((1, 0, 88), (-1, 12, 90)))
    accs = [(2 * HID, 2 * HID), (2 * KP, 4 * HID), (2 * KP, 2 * HID), (KP, LANES)]
    plane, half = struct(8 * Q, LANES), struct(8, LANES)
    small, large = (
        jax.ShapeDtypeStruct((8 * LANES // CH, 2 * n, CH), BF16) for n in (KP, HID)
    )
    below, above, *sides = halo0
    planes = [
        call(
            lambda *refs, x=x: middle_kernel(x, *refs),
            [plane, half, plane, half, struct(KP, LANES), small, large, large, small, large, large],
            [(8 * KP, LANES), (8 * Q, LANES), (8 * KP, LANES), (8 * KP, LANES), (HID, HID)],
            "middle",
        )(post, f, t, code, adj, face, *sides, w1, b1, w2, b2, w3)
        for x, face in enumerate((below, above))
    ]
    parts = [planes[x][k] for k in (2, 3, 0, 1) for x in range(2)]
    known = (*parts, f, theta, code)
    yp, ym = call(along_y_kernel, [struct(24, LANES)] * 2, [], "along_y")(*known)
    come = along("gy", yp, ym)
    xp, xm, yl, yr = call(
        along_x_kernel, [struct(88, LANES)] * 2 + [struct(24, LANES)] * 2, [], "along_x"
    )(*known, *come)
    faces = along("gx", xp, xm)
    pack1 = call(
        weights_kernel,
        struct(PACK, HID),
        [(HID, HID), (KP, LANES), *accs[:3]],
        "weights",
        in_specs=[pl.BlockSpec(memory_space=pltpu.VMEM)] * 14 + [pl.BlockSpec(memory_space=pl.ANY)],
    )(*planes[0][4:], *planes[1][4:], xp)
    scale = 1.0 / math.sqrt(cells)
    shares = outer_of(lax.axis_size("gx")) * lax.axis_size("gy")
    part = -(-(PACK + 8) // shares)
    fbar0, theta0, pack = call(
        lambda *refs: first_step_kernel(scale, refs[:8], *refs[8:]),
        [POPS, WARM, struct(shares, part, HID)],
        [FULL, (Q * ROWS, LANES), FULL, FULL, (HID, HID), *accs, (ROWS, LANES), (shares * part, HID),
         (Q * ROWS, LANES), (ROWS, LANES), (48, LANES), (48, LANES), (16, LANES), (16, LANES)],
        "first_step",
    )(*parts, theta, f, t, *faces, yl, yr, *halo0, code, h1s, h2s, w1, w2, w3, pack1)
    total = reduced(pack)
    g1, gb1, g2, gb2, g3, gb3 = call(
        unpack_kernel,
        [struct(Q, HID), struct(1, HID), struct(HID, HID), struct(1, HID), struct(Q, HID), struct(1, Q)],
        [(shares * part, HID)],
        "unpack",
    )(total)
    return (
        fbar0.reshape(Q, sx, sy, sz),
        theta0.reshape(sx, sy, sz),
        g1,
        gb1.reshape(HID),
        g2,
        gb2.reshape(HID),
        g3.T,
        gb3.reshape(Q),
    )


def solution(mesh):
    pops, cells = P(None, "gx", "gy", None), P("gx", "gy", None)
    return jax.shard_map(
        per_device,
        mesh=mesh,
        in_specs=(pops, cells, cells, P(), P(), P(), P(), P(), P(), pops, cells),
        out_specs=(pops, cells, P(), P(), P(), P(), P(), P()),
        check_vma=False,
    )
```

```python
import math

import jax
import jax.numpy as jnp
import numpy as np
from jax import lax
from jax.experimental import pallas as pl
from jax.experimental.pallas import tpu as pltpu
from jax.sharding import PartitionSpec as P

VELOCITIES = [
    (0, 0, 0), (1, 0, 0), (-1, 0, 0), (0, 1, 0), (0, -1, 0), (0, 0, 1), (0, 0, -1),
    (1, 1, 0), (-1, -1, 0), (1, -1, 0), (-1, 1, 0), (1, 0, 1), (-1, 0, -1), (1, 0, -1),
    (-1, 0, 1), (0, 1, 1), (0, -1, -1), (0, 1, -1), (0, -1, 1),
]
Q = 19
OPPOSITE = [VELOCITIES.index((-a, -b, -c)) for a, b, c in VELOCITIES]
WEIGHTS = [1.0 / 3.0] + [1.0 / 18.0] * 6 + [1.0 / 36.0] * 12
BUOYANCY = [float(np.float32(0.3 * w * c[2])) for w, c in zip(WEIGHTS, VELOCITIES)]
CONDUCTIVITY = 0.1
HOT_WALL = 0.5
COLD_WALL = -0.5
HEATER = 0.5
HID = 128
KP = 32
ROWS = 16
LANES = 128
CH = 512
PACK = 176
F32 = jnp.float32
BF16 = jnp.bfloat16


def moving(axis, sign, orient):
    return [i for i in range(Q) if VELOCITIES[i][axis] * orient == sign]


def diagonal(sx, sy, orient):
    return VELOCITIES.index((sx * orient, sy * orient, 0))


def split(x):
    hi = x.astype(BF16)
    lo = (x - hi.astype(F32)).astype(BF16)
    return hi, lo


def stacked(x):
    return jnp.concatenate(split(x), axis=0)


def nn(a, b):
    return lax.dot_general(a, b, (((1,), (0,)), ((), ())), preferred_element_type=F32)


def nt(a, b):
    return lax.dot_general(a, b, (((1,), (1,)), ((), ())), preferred_element_type=F32)


def left(w):
    hi, lo = split(w)
    return jnp.concatenate(
        [jnp.concatenate([hi, hi], axis=1), jnp.concatenate([lo, lo], axis=1)], axis=0
    )


def product(a, b, rows):
    d = nn(a, b)
    return d[:rows] + d[rows:]


def four_blocks(d, rows):
    return d[:rows, :HID] + d[:rows, HID:] + d[rows:, :HID] + d[rows:, HID:]


def lanes_of(shape):
    return lax.broadcasted_iota(jnp.int32, shape, 1)


def subs_of(shape):
    return lax.broadcasted_iota(jnp.int32, shape, 0)


def shift_z(v, step, fill):
    if step == 1:
        return jnp.where(lanes_of(v.shape) == 0, fill, pltpu.roll(v, 1, 1))
    return jnp.where(lanes_of(v.shape) == LANES - 1, fill, pltpu.roll(v, LANES - 1, 1))


def shift_y(v, step, row):
    if step == 1:
        return jnp.where(subs_of(v.shape) == 0, row, pltpu.roll(v, 1, 0))
    return jnp.where(subs_of(v.shape) == 7, row, pltpu.roll(v, 7, 0))


def tile(ref, i, x):
    if isinstance(ref, tuple):
        return ref[x][8 * i : 8 * i + 8, :]
    k = i * ROWS + x * 8
    return ref[k : k + 8, :]


def halves(ref):
    if isinstance(ref, tuple):
        return [ref[0][...], ref[1][...]]
    return [ref[0:8, :], ref[8:16, :]]


def transposed(w_ref, b_ref, pad_ref):
    pad_ref[...] = jnp.zeros((HID, HID), F32)
    pad_ref[0:Q, :] = w_ref[...]
    if b_ref is not None:
        pad_ref[Q : Q + 1, :] = b_ref[...]
    return pad_ref[...]


def column(b_ref, n, pad_ref):
    pad_ref[...] = jnp.zeros((HID, HID), F32)
    pad_ref[:, 0:n] = jnp.broadcast_to(b_ref[...], (HID, n))
    return jnp.transpose(pad_ref[...])


def rows_in(ref, c):
    n, step = CH // LANES, ref.shape[0] // KP
    order = range(step) if step != ROWS else [0, 7, 8, 15, *range(1, 7), *range(9, 15)]
    return order[c * n : (c + 1) * n], step


def across(ref, c):
    rows, step = rows_in(ref, c)
    return jnp.concatenate([ref[pl.ds(r, KP, stride=step), :] for r in rows], axis=1)


def back(ref, c, value):
    rows, step = rows_in(ref, c)
    for j, r in enumerate(rows):
        ref[pl.ds(r, KP, stride=step), :] = value[:, j * LANES : (j + 1) * LANES]


def fill_features(s_ref, f_ref):
    rows = s_ref.shape[0] // KP
    s_ref[0 : Q * rows, :] = f_ref[...]
    s_ref[Q * rows : (Q + 1) * rows, :] = jnp.ones((rows, LANES), F32)
    s_ref[(Q + 1) * rows :, :] = jnp.zeros(((KP - Q - 1) * rows, LANES), F32)


def wide(b):
    return jnp.concatenate([b] * (CH // LANES), axis=1)


def put_x(value, orient, xp, xm, at):
    for k, i in enumerate(moving(0, 1, orient)):
        xp[at + 8 * k : at + 8 * k + 8, :] = value(i, 1)
    for k, i in enumerate(moving(0, -1, orient)):
        xm[at + 8 * k : at + 8 * k + 8, :] = value(i, 0)


def put_y(value, orient, yp, ym, row):
    for k, i in enumerate(moving(1, 1, orient)):
        for x in range(2):
            yp[row + 2 * k + x : row + 2 * k + x + 1, :] = value(i, x)[7:8]
    for k, i in enumerate(moving(1, -1, orient)):
        for x in range(2):
            ym[row + 2 * k + x : row + 2 * k + x + 1, :] = value(i, x)[0:1]


def put_corners(leftward, rightward, orient, xp, xm, row, at):
    for sx, to in ((1, xp), (-1, xm)):
        for k, (sy, come) in enumerate(((1, leftward), (-1, rightward))):
            j = row + 2 * moving(1, sy, orient).index(diagonal(sx, sy, orient)) + (sx == 1)
            to[at + k : at + k + 1, :] = come[j : j + 1, :]


def streamed(ref, halo, orient, i, x):
    below, above, leftward, rightward, at, row, corner = halo
    sx, sy, sz = (orient * c for c in VELOCITIES[i])
    xs = x - sx
    if xs in (0, 1):
        v = tile(ref, i, xs)
    else:
        k = at + 8 * moving(0, sx, orient).index(i)
        v = (below if sx == 1 else above)[k : k + 8, :]
    if sy:
        if xs in (0, 1):
            k = row + 2 * moving(1, sy, orient).index(i) + xs
            edge = (leftward if sy == 1 else rightward)[k : k + 1, :]
        else:
            k = corner + (sy == -1)
            edge = (below if sx == 1 else above)[k : k + 1, :]
        v = shift_y(v, sy, edge)
    if sz:
        v = shift_z(v, sz, tile(ref, OPPOSITE[i], x))
    return v


def motion(ref, x):
    us = []
    for a in range(3):
        total = None
        for i in range(Q):
            c = VELOCITIES[i][a]
            if c:
                v = tile(ref, i, x)
                total = (v if c == 1 else -v) if total is None else (total + v if c == 1 else total - v)
        us.append(total)
    return us


def warm_neighbours(t_ref, rims, x):
    below, above, leftward, rightward = rims
    t = halves(t_ref)
    lower = below if x == 0 else t[0]
    upper = t[1] if x == 0 else above
    return [
        (upper, lower),
        (shift_y(t[x], -1, rightward[x]), shift_y(t[x], 1, leftward[x])),
        (shift_z(t[x], -1, COLD_WALL), shift_z(t[x], 1, HOT_WALL)),
    ]


def flux(u, a, s, liquid):
    return (CONDUCTIVITY - (0.5 * s) * u[a]) * liquid


def heat_adjoint(us, liquids, theta, codes, flux_rims):
    below, above, leftward, rightward = flux_rims
    out = []
    for x in range(2):
        u, liquid = us[x], liquids[x]
        total = 0.4 * liquid + jnp.where(codes[x] == 1, theta[x], 0.0)
        total = total + (below if x == 0 else flux(us[0], 0, 1, liquids[0]))
        total = total + (flux(us[1], 0, -1, liquids[1]) if x == 0 else above)
        total = total + shift_y(flux(u, 1, 1, liquid), 1, leftward[x])
        total = total + shift_y(flux(u, 1, -1, liquid), -1, rightward[x])
        total = total + shift_z(flux(u, 2, 1, liquid), 1, 0.0)
        total = total + shift_z(flux(u, 2, -1, liquid), -1, 0.0)
        out.append(total)
    return out


def motion_adjoint(t_ref, rims, liquids):
    return [
        [-0.5 * liquids[x] * (plus - minus) for plus, minus in warm_neighbours(t_ref, rims, x)]
        for x in range(2)
    ]


def with_motion(value, ubar, i):
    for a in range(3):
        c = VELOCITIES[i][a]
        if c:
            value = value + ubar[a] if c == 1 else value - ubar[a]
    return value


def hidden(fx, a1, a2, b2):
    h1 = jnp.tanh(product(a1, fx, HID))
    h1x = stacked(h1)
    h2 = jnp.tanh(product(a2, h1x, HID) + b2)
    return h1, h1x, h2


def network_back(s1, s2, d, w3b, w2b, w1b):
    dx = stacked(d)
    px = stacked(product(w3b, dx, HID) * s2)
    qx = stacked(product(w2b, px, HID) * s1)
    return product(w1b, qx, KP), dx, px, qx


def folded(d):
    return sum(d[:, j * LANES : (j + 1) * LANES] for j in range(CH // LANES))


def gather(accs, values, first):
    for ref, value in zip(accs, values):
        ref[...] = value if first else ref[...] + value


def weight_products(fx, h1x, h2x, dx, px, qx):
    return nt(h1x, px), nt(fx, jnp.concatenate([qx, px], axis=0)), nt(dx, h2x)


def write_pack(pack, acc2, acc1, acc3, accb, pad_ref):
    pack[0:HID, :] = four_blocks(acc2[...], HID)
    d = acc1[...]
    w1 = four_blocks(d[:, : 2 * HID], KP)
    pack[HID : HID + 24, :] = w1[0:24]
    d3 = acc3[...]
    w3 = four_blocks(d3, KP)
    pack[HID + 24 : HID + 48, :] = w3[0:24]
    b2 = four_blocks(d[:, 2 * HID :], KP)[Q : Q + 1]
    pad_ref[...] = jnp.zeros((HID, HID), F32)
    pad_ref[0:KP, :] = accb[...]
    b3 = jnp.sum(jnp.transpose(pad_ref[...]), axis=0, keepdims=True)
    pack[HID + 21 : HID + 22, :] = b2
    pack[HID + 22 : HID + 23, :] = b3


def collided(f, t, code, outs, i):
    k = i * ROWS
    relaxed = f[k : k + ROWS, :] + outs[k : k + ROWS, :]
    if BUOYANCY[i]:
        relaxed = relaxed + BUOYANCY[i] * t[...]
    o = OPPOSITE[i] * ROWS
    return jnp.where(code[...] == 0, relaxed, f[o : o + ROWS, :])


def forward_chunk(feat, c, l1, l2, l3, b2t, b3t):
    h1, _, h2 = hidden(stacked(across(feat, c)), l1, l2, b2t)
    return h1, h2, product(l3, stacked(h2), KP) + b3t


def edge_rows_kernel(
    w1_in, b1_in, w2_in, b2_in, w3_in, b3_in, f_in, t_in, code_in, adj_in, theta_in,
    w1, w2, w3, f, t, code, adj, theta, l1, l2, l3, b2t, b3t, h1s, h2s, out0, yp, ym,
    feat, outs, pad, b1, b2, b3, sems,
):
    ins = (w1_in, b1_in, w2_in, b2_in, w3_in, b3_in, f_in, t_in, code_in, adj_in, theta_in)
    here = (w1, b1, w2, b2, w3, b3, f, t, code, adj, theta)
    copies = [pltpu.make_async_copy(a, b, sems.at[k]) for k, (a, b) in enumerate(zip(ins, here))]
    for c in copies:
        c.start()
    for c in copies[:6]:
        c.wait()
    l1[...] = left_narrow(jnp.transpose(transposed(w1, b1, pad)))
    l2[...] = left(jnp.transpose(w2[...]))
    pad[...] = jnp.zeros((HID, HID), F32)
    pad[0:Q, :] = w3[...]
    l3[...] = left(pad[0:KP, :])
    b2t[...] = wide(column(b2, HID, pad))
    b3t[...] = wide(column(b3, Q, pad)[0:KP])
    copies[6].wait()
    fill_features(feat, f)
    h1, h2, out = forward_chunk(feat, 0, l1[...], l2[...], l3[...], b2t[...], b3t[...])
    h1s[0], h2s[0], out0[...] = h1, h2, out
    outs[...] = jnp.zeros(outs.shape, F32)
    back(outs, 0, out)
    for c in copies[7:]:
        c.wait()
    put_y(lambda i, x: tile(adj, i, x), -1, yp, ym, 12)

    def value(i, x):
        return collided(f, t, code, outs, i)[8 * x : 8 * x + 8]

    put_y(value, 1, yp, ym, 0)
    for x in range(2):
        yp[10 + x : 11 + x, :] = t[8 * x + 7 : 8 * x + 8, :]
        ym[10 + x : 11 + x, :] = t[8 * x : 8 * x + 1, :]


def other_rows_kernel(
    f, t, code, adj, l1, l2, l3, b2t, b3t, out0,
    post, h1s, h2s, xp, xm,
    feat, outs,
):
    fill_features(feat, f)
    back(outs, 0, out0[...])
    for c in range(1, ROWS * LANES // CH):
        h1, h2, out = forward_chunk(feat, c, l1[...], l2[...], l3[...], b2t[...], b3t[...])
        h1s[c - 1], h2s[c - 1] = h1, h2
        back(outs, c, out)
    for i in range(Q):
        post[i * ROWS : (i + 1) * ROWS, :] = collided(f, t, code, outs, i)
    put_x(lambda i, x: tile(adj, i, x), -1, xp, xm, 48)
    put_x(lambda i, x: tile(post, i, x), 1, xp, xm, 0)
    xp[40:48, :] = t[8:16, :]
    xm[40:48, :] = t[0:8, :]


def prepare_kernel(
    f, h1a, h2a, h1b, h2b, w1, w2, w3, _,
    w3b, w2b, w1b, fxs, h1xs, h2xs, s1, s2,
    feat, pad,
):
    w3b[...], w2b[...], w1b[...] = back_weights(w1, w2, w3, pad)
    fill_features(feat, f)
    for c in range(ROWS * LANES // CH):
        h1, h2 = (h1a[0], h2a[0]) if c == 0 else (h1b[c - 1], h2b[c - 1])
        fxs[c], h1xs[c], h2xs[c] = stacked(across(feat, c)), stacked(h1), stacked(h2)
        s1[c], s2[c] = 1.0 - h1 * h1, 1.0 - h2 * h2


def left_narrow(w):
    hi, lo = split(w + pltpu.roll(w, KP, 1))
    return jnp.concatenate([hi, lo], axis=0)[:, : 2 * KP]


def rims_of(below, above, leftward, rightward, at, row):
    return (
        below[at : at + 8, :],
        above[at : at + 8, :],
        [leftward[row + x : row + x + 1, :] for x in range(2)],
        [rightward[row + x : row + x + 1, :] for x in range(2)],
    )


def collision_gradient(adj, halo, code, grad, masked, lift):
    for x in range(2):
        fluid = code[8 * x : 8 * x + 8, :] == 0
        total = None
        for i in range(Q):
            k = i * ROWS + 8 * x
            g = streamed(adj, halo, -1, i, x)
            grad[k : k + 8, :] = g
            g = jnp.where(fluid, g, 0.0)
            masked[k : k + 8, :] = g
            if BUOYANCY[i]:
                total = BUOYANCY[i] * g if total is None else total + BUOYANCY[i] * g
        lift[8 * x : 8 * x + 8, :] = total
    masked[Q * ROWS :, :] = jnp.zeros(((KP - Q) * ROWS, LANES), F32)


def back_weights(w1, w2, w3, pad):
    pad[...] = jnp.zeros((HID, HID), F32)
    pad[0:Q, :] = w3[...]
    w3b = left_narrow(jnp.transpose(pad[...]))
    w2b = left(w2[...])
    pad[...] = jnp.zeros((HID, HID), F32)
    pad[0:Q, :] = w1[...]
    w1b = left(pad[0:KP, :])
    return w3b, w2b, w1b


def middle_kernel(
    x, post, f, t, code, adj, face, leftward, rightward, l1, l2, b2t, w3b, w2b, w1b,
    f1, t1, fbar, lift, accb, fxs, h1xs, h2xs, dxs, pxs, qxs,
    feat, grad, masked, dfs,
):
    kind = code[8 * x : 8 * x + 8, :]
    fluid = kind == 0
    halo = (face, face, leftward, rightward, 0, 0, 88)
    adj_halo = (face, face, leftward, rightward, 48, 12, 90)
    warmth = None
    for i in range(Q):
        k = 8 * i
        f1[k : k + 8, :] = streamed(post, halo, 1, i, x)
        g = streamed(adj, adj_halo, -1, i, x)
        grad[k : k + 8, :] = g
        g = jnp.where(fluid, g, 0.0)
        masked[k : k + 8, :] = g
        if BUOYANCY[i]:
            warmth = BUOYANCY[i] * g if warmth is None else warmth + BUOYANCY[i] * g
    lift[...] = warmth
    masked[8 * Q :, :] = jnp.zeros(((KP - Q) * 8, LANES), F32)
    u = motion(f, x)
    here = t[8 * x : 8 * x + 8, :]
    total = 0.4 * here
    rims = rims_of(face, face, leftward, rightward, 40, 10)
    for a, (plus, minus) in enumerate(warm_neighbours(t, rims, x)):
        total = total + (CONDUCTIVITY - 0.5 * u[a]) * plus
        total = total + (CONDUCTIVITY + 0.5 * u[a]) * minus
    t1[...] = jnp.where(fluid, total, jnp.where(kind == 1, here, HEATER))
    fill_features(feat, f1)
    for c in range(8 * LANES // CH):
        fx = stacked(across(feat, c))
        h1, h1x, h2 = hidden(fx, l1[...], l2[...], b2t[...])
        d = across(masked, c)
        df, dx, px, qx = network_back(
            1.0 - h1 * h1, 1.0 - h2 * h2, d, w3b[...], w2b[...], w1b[...]
        )
        gather((accb,), (folded(d),), c == 0)
        back(dfs, c, df)
        fxs[c], h1xs[c], h2xs[c] = fx, h1x, stacked(h2)
        dxs[c], pxs[c], qxs[c] = dx, px, qx
    for i in range(Q):
        k, o = 8 * i, 8 * OPPOSITE[i]
        fbar[k : k + 8, :] = jnp.where(
            fluid, grad[k : k + 8, :] + dfs[k : k + 8, :], grad[o : o + 8, :]
        )


def weights_kernel(*refs):
    first, second, (_, pack, pad, accb, *accs) = refs[:7], refs[7:14], refs[14:]
    accb[...] = first[0][...] + second[0][...]
    for plane in (first, second):
        for c in range(plane[1].shape[0]):
            values = weight_products(*(v[c] for v in plane[1:]))
            gather(accs, values, plane is first and c == 0)
    write_pack(pack, *accs, accb, pad)


def coefficient(u, a, s, kind):
    return jnp.where(kind == 0, CONDUCTIVITY - (0.5 * s) * u[a], 0.0)


def adjoint_parts(fbar, lift, f1, t1, theta, code, t_rims, flux_rims):
    codes, thetas = halves(code), halves(theta)
    liquids = [jnp.where(k == 0, v, 0.0) for k, v in zip(codes, thetas)]
    us = [motion(f1, x) for x in range(2)]
    ubar = motion_adjoint(t1, t_rims, liquids)
    warm = heat_adjoint(us, liquids, thetas, codes, flux_rims)
    warm = [v + w for v, w in zip(warm, halves(lift))]

    def adj(i, x):
        return with_motion(tile(fbar, i, x), ubar[x], i)

    return codes, liquids, us, adj, warm


def no_rims():
    blank, row = jnp.zeros((8, LANES), F32), jnp.zeros((1, LANES), F32)
    return blank, blank, [row, row], [row, row]


def rows_of(ref, at):
    return [ref[at + x : at + x + 1, :] for x in range(2)]


def paired(refs):
    return [tuple(refs[2 * k : 2 * k + 2]) for k in range(4)]


def along_y_kernel(*refs):
    fbar, lift, f1, t1 = paired(refs)
    f0, theta, code, yp, ym = refs[8:]
    codes, liquids, us, adj, warm = adjoint_parts(
        fbar, lift, f1, t1, theta, code, no_rims(), no_rims()
    )
    ts = halves(t1)
    for s, e, out in ((1, 7, yp), (-1, 0, ym)):
        for x in range(2):
            u0 = motion(f0, x)
            parts = [adj(i, x) for i in moving(1, s, -1)]
            parts += [ts[x], flux(us[x], 1, s, liquids[x]), liquids[x], warm[x]]
            parts.append(coefficient(u0, 1, s, codes[x]))
            for k, v in enumerate(parts):
                out[2 * k + x : 2 * k + x + 1, :] = v[e : e + 1]
        out[20:21, :] = flux(us[1], 0, 1, liquids[1])[e : e + 1]
        out[21:22, :] = flux(us[0], 0, -1, liquids[0])[e : e + 1]


def along_x_kernel(*refs):
    fbar, lift, f1, t1 = paired(refs)
    f0, theta, code, leftward, rightward, xp, xm, yl, yr = refs[8:]
    zero, _, _, _ = no_rims()
    codes, liquids, us, adj, warm = adjoint_parts(
        fbar, lift, f1, t1, theta, code,
        (zero, zero, rows_of(leftward, 10), rows_of(rightward, 10)),
        (zero, zero, rows_of(leftward, 12), rows_of(rightward, 12)),
    )
    ts = halves(t1)
    for s, x, out in ((1, 1, xp), (-1, 0, xm)):
        parts = [adj(i, x) for i in moving(0, s, -1)]
        parts += [ts[x], liquids[x], warm[x]]
        parts.append(coefficient(motion(f0, x), 0, s, codes[x]))
        parts.append(flux(us[x], 0, s, liquids[x]))
        for k, v in enumerate(parts):
            out[8 * k : 8 * k + 8, :] = v
    for k, (s, e, come, out) in enumerate(((1, 0, leftward, yl), (-1, 7, rightward, yr))):
        t_come, flux_come, liquid, warm_come, factor = (
            rows_of(come, 10 + 2 * j) for j in range(5)
        )
        for x in range(2):
            for j in range(5):
                r = 2 * j + x
                out[r : r + 1, :] = (
                    come[r : r + 1, :] + 0.5 * liquid[x] * ts[x][e : e + 1]
                )
            done = warm_come[x] + flux(us[x], 1, -s, liquids[x])[e : e + 1]
            for j, v in enumerate((t_come[x], liquid[x], done, factor[x], flux_come[x])):
                r = 10 + 2 * j + x
                out[r : r + 1, :] = v
        for sx, x, to in ((1, 1, xp), (-1, 0, xm)):
            r = 2 * moving(1, s, -1).index(diagonal(sx, s, -1)) + x
            for j, v in enumerate(
                (out[r : r + 1, :], liquid[x], t_come[x], come[21 - x : 22 - x, :])
            ):
                to[80 + 4 * k + j : 81 + 4 * k + j, :] = v


def complete(
    fbar, lift, f1, t1, theta, code, below, above, yl, yr,
    adj1, warm1, hbelow, habove, hleft, hright,
):
    _, liquids, us, adj, warm = adjoint_parts(
        fbar, lift, f1, t1, theta, code,
        (below[40:48, :], above[40:48, :], rows_of(yl, 10), rows_of(yr, 10)),
        (below[72:80, :], above[72:80, :], rows_of(yl, 18), rows_of(yr, 18)),
    )
    ts = halves(t1)
    for x in range(2):
        warm1[8 * x : 8 * x + 8, :] = warm[x]
        for i in range(Q):
            k = i * ROWS + 8 * x
            adj1[k : k + 8, :] = adj(i, x)
    faces = []
    for s, x, come, out in ((1, 0, below, hbelow), (-1, 1, above, habove)):
        for k in range(5):
            out[8 * k : 8 * k + 8, :] = (
                come[8 * k : 8 * k + 8, :] + 0.5 * come[48:56, :] * ts[x]
            )
        for k, rows in enumerate((yl, yr)):
            j = 80 + 4 * k
            out[40 + k : 41 + k, :] = (
                come[j : j + 1, :] + 0.5 * come[j + 1 : j + 2, :] * rows[10 + x : 11 + x, :]
            )
        faces.append(come[64:72, :] * (come[56:64, :] + flux(us[x], 0, -s, liquids[x])))
    edges = []
    for k, (s, rows, out) in enumerate(((1, yl, hleft), (-1, yr, hright))):
        j = 80 + 4 * k
        out[0:10, :] = rows[0:10, :]
        edge = []
        for sx, x, come in ((1, 0, below), (-1, 1, above)):
            r = 2 * moving(1, s, -1).index(diagonal(sx, s, -1)) + x
            out[r : r + 1, :] = (
                rows[r : r + 1, :]
                - 0.5 * rows[12 + x : 13 + x, :] * come[j + 2 : j + 3, :]
            )
            edge.append(
                rows[16 + x : 17 + x, :]
                * (rows[14 + x : 15 + x, :] + come[j + 3 : j + 4, :])
            )
        edges.append(edge)
    return (*faces, *edges)


def first_step_kernel(
    scale, known,
    theta2, f, t, below, above, yl, yr,
    tbelow, tabove, tleft, tright, code, w3b, w2b, w1b, fxs, h1xs, h2xs, s1, s2, pack1,
    fbar, thetabar, pack,
    grad, masked, dfs, pad, acc2, acc1, acc3, accb, lift, total,
    adj, theta, hbelow, habove, hleft, hright,
):
    flux_rims = complete(
        *paired(known), theta2, code, below, above, yl, yr,
        adj, theta, hbelow, habove, hleft, hright,
    )
    halo = (hbelow, habove, hleft, hright, 0, 0, 40)
    collision_gradient(adj, halo, code, grad, masked, lift)
    for c in range(ROWS * LANES // CH):
        d = across(masked, c)
        df, dx, px, qx = network_back(s1[c], s2[c], d, w3b[...], w2b[...], w1b[...])
        values = weight_products(fxs[c], h1xs[c], h2xs[c], dx, px, qx)
        gather((acc2, acc1, acc3, accb), (*values, folded(d)), c == 0)
        back(dfs, c, df)
    write_pack(total, acc2, acc1, acc3, accb, pad)
    parts, part, _ = pack.shape
    total[PACK:, :] = jnp.zeros((parts * part - PACK, HID), F32)
    total[0:PACK, :] = (total[0:PACK, :] + pack1[...]) * scale
    for k in range(parts):
        pack[k] = total[k * part : (k + 1) * part, :]
    codes, thetas = halves(code), halves(theta)
    liquids = [jnp.where(k == 0, v, 0.0) for k, v in zip(codes, thetas)]
    rims = rims_of(tbelow, tabove, tleft, tright, 40, 10)
    ubar = motion_adjoint(t, rims, liquids)
    new = heat_adjoint([motion(f, x) for x in range(2)], liquids, thetas, codes, flux_rims)
    for x in range(2):
        thetabar[8 * x : 8 * x + 8, :] = new[x] + lift[8 * x : 8 * x + 8, :]
        fluid = codes[x] == 0
        for i in range(Q):
            k, o = i * ROWS + 8 * x, OPPOSITE[i] * ROWS + 8 * x
            value = jnp.where(fluid, grad[k : k + 8, :] + dfs[k : k + 8, :], grad[o : o + 8, :])
            fbar[k : k + 8, :] = with_motion(value, ubar[x], i)


def struct(*shape):
    return jax.ShapeDtypeStruct(shape, F32)


def call(kernel, outs, scratch, name, more=(), **specs):
    return pl.pallas_call(
        kernel,
        out_shape=outs,
        scratch_shapes=[pltpu.VMEM(s, F32) for s in scratch] + list(more),
        **specs,
        compiler_params=pltpu.CompilerParams(vmem_limit_bytes=40 * 1024 * 1024),
        name=name,
    )


FULL = (KP * ROWS, LANES)
POPS = struct(Q * ROWS, LANES)
WARM = struct(ROWS, LANES)


def shifted(value, axis, by):
    count = lax.axis_size(axis)
    return lax.ppermute(value, axis, [(s, (s + by) % count) for s in range(count)])


def along(axis, plus, minus):
    return shifted(plus, axis, 1), shifted(minus, axis, -1)


def edge_kernel(blocks, xp, xm, leftward, rightward, xp_out, xm_out):
    xp_out[...] = xp[...]
    xm_out[...] = xm[...]
    for orient, row, at in blocks:
        put_corners(leftward, rightward, orient, xp_out, xm_out, row, at)


def swapped(value, groups):
    return lax.all_to_all(
        value, ("gx", "gy"), 0, 0, axis_index_groups=groups, tiled=True
    )


def factors_of(nx):
    near = 2 if nx % 2 == 0 else 1
    far = nx // 24 if nx % 24 == 0 else 1
    return far, nx // (far * near), near


def shares_of(nx, ny):
    far, _, near = factors_of(nx)
    return far * near * ny


def groups_of(nx, ny):
    far, mid, near = factors_of(nx)
    at = np.arange(nx * ny).reshape(far, mid, near, ny)
    return (
        at.transpose(1, 0, 2, 3).reshape(mid, -1).tolist(),
        at.transpose(0, 2, 3, 1).reshape(-1, mid).tolist(),
    )


def total_kernel(parts, out):
    value = parts[0]
    for k in range(1, parts.shape[0]):
        value = value + parts[k]
    for k in range(out.shape[0]):
        out[k] = value


def summed(parts, copies):
    return call(total_kernel, struct(copies, *parts.shape[1:]), [], "total")(parts)


def reduced(pack):
    share, same = groups_of(lax.axis_size("gx"), lax.axis_size("gy"))
    part = summed(swapped(pack, share), len(same[0]))
    part = summed(swapped(part, same), len(share[0]))
    return swapped(part, share)


def unpack_kernel(parts, w1, b1, w2, b2, w3, b3, pack):
    count, part, _ = parts.shape
    for k in range(count):
        pack[k * part : (k + 1) * part, :] = parts[k]
    w2[...] = pack[0:HID, :]
    w1[...] = pack[HID : HID + Q, :]
    b1[...] = pack[HID + Q : HID + Q + 1, :]
    b2[...] = pack[HID + 21 : HID + 22, :]
    b3[...] = pack[HID + 22 : HID + 23, 0:Q]
    w3[...] = pack[HID + 24 : HID + 24 + Q, :]


def per_device(f, t, code, w1, b1, w2, b2, w3, b3, adj, theta):
    sx, sy, sz = t.shape
    cells = sx * lax.axis_size("gx") * sy * lax.axis_size("gy") * sz
    f, adj = f.reshape(Q * ROWS, LANES), adj.reshape(Q * ROWS, LANES)
    t, code, theta = (v.reshape(ROWS, LANES) for v in (t, code, theta))
    b1, b2, b3 = (v.reshape(1, -1) for v in (b1, b2, b3))
    w3 = w3.T
    ins = (w1, b1, w2, b2, w3, b3, f, t, code, adj, theta)
    like = [jax.ShapeDtypeStruct(v.shape, v.dtype) for v in ins]
    held = [v for k, v in enumerate(like) if k not in (1, 3, 5)]
    count = ROWS * LANES // CH

    def narrow(*shape):
        return jax.ShapeDtypeStruct(shape, BF16)

    outs = call(
        edge_rows_kernel,
        [*held, narrow(2 * HID, 2 * KP), narrow(2 * HID, 2 * HID), narrow(2 * KP, 2 * HID),
         struct(HID, CH), struct(KP, CH), struct(1, HID, CH), struct(1, HID, CH),
         struct(KP, CH), struct(24, LANES), struct(24, LANES)],
        [FULL, FULL, (HID, HID)],
        "edge_rows",
        [pltpu.VMEM(v.shape, v.dtype) for v in (b1, b2, b3)] + [pltpu.SemaphoreType.DMA((11,))],
        in_specs=[pl.BlockSpec(memory_space=pltpu.HBM)] * 11,
    )(*(pltpu.with_memory_space_constraint(v, pltpu.HBM) for v in ins))
    w1, w2, w3, f, t, code, adj, theta, l1, l2, l3, b2t, b3t, h1a, h2a, out0, yp, ym = outs
    sides = along("gy", yp, ym)
    post, h1b, h2b, xp, xm = call(
        other_rows_kernel,
        [POPS, *[struct(count - 1, HID, CH)] * 2, struct(96, LANES), struct(96, LANES)],
        [FULL, FULL],
        "other_rows",
    )(f, t, code, adj, l1, l2, l3, b2t, b3t, out0)
    blocks = ((1, 0, 88), (-1, 12, 90))
    xp, xm = call(
        lambda *refs: edge_kernel(blocks, *refs), [struct(96, LANES)] * 2, [], "corners"
    )(xp, xm, *sides)
    below, above = along("gx", xp, xm)
    halo0 = (below, above, *sides)
    w3b, w2b, w1b, *kept = call(
        prepare_kernel,
        [narrow(2 * HID, 2 * KP), narrow(2 * HID, 2 * HID), narrow(2 * KP, 2 * HID),
         narrow(count, 2 * KP, CH), *[narrow(count, 2 * HID, CH)] * 2, *[struct(count, HID, CH)] * 2],
        [FULL, (HID, HID)],
        "prepare",
        in_specs=[pl.BlockSpec(memory_space=pltpu.VMEM)] * 8 + [pl.BlockSpec(memory_space=pl.ANY)],
    )(f, h1a, h2a, h1b, h2b, w1, w2, w3, xp)
    accs = [(2 * HID, 2 * HID), (2 * KP, 4 * HID), (2 * KP, 2 * HID), (KP, LANES)]
    plane, half = struct(8 * Q, LANES), struct(8, LANES)
    small, large = (
        jax.ShapeDtypeStruct((8 * LANES // CH, 2 * n, CH), BF16) for n in (KP, HID)
    )
    planes = [
        call(
            lambda *refs, x=x: middle_kernel(x, *refs),
            [plane, half, plane, half, struct(KP, LANES), small, large, large, small, large, large],
            [(8 * KP, LANES), (8 * Q, LANES), (8 * KP, LANES), (8 * KP, LANES)],
            "middle",
        )(post, f, t, code, adj, face, *sides, l1, l2, b2t, w3b, w2b, w1b)
        for x, face in enumerate((below, above))
    ]
    parts = [planes[x][k] for k in (2, 3, 0, 1) for x in range(2)]
    known = (*parts, f, theta, code)
    yp, ym = call(along_y_kernel, [struct(24, LANES)] * 2, [], "along_y")(*known)
    come = along("gy", yp, ym)
    xp, xm, yl, yr = call(
        along_x_kernel, [struct(88, LANES)] * 2 + [struct(24, LANES)] * 2, [], "along_x"
    )(*known, *come)
    faces = along("gx", xp, xm)
    pack1 = call(
        weights_kernel,
        struct(PACK, HID),
        [(HID, HID), (KP, LANES), *accs[:3]],
        "weights",
        in_specs=[pl.BlockSpec(memory_space=pltpu.VMEM)] * 14 + [pl.BlockSpec(memory_space=pl.ANY)],
    )(*planes[0][4:], *planes[1][4:], xp)
    scale = 1.0 / math.sqrt(cells)
    shares = shares_of(lax.axis_size("gx"), lax.axis_size("gy"))
    part = -(-(PACK + 8) // shares)
    fbar0, theta0, pack = call(
        lambda *refs: first_step_kernel(scale, refs[:8], *refs[8:]),
        [POPS, WARM, struct(shares, part, HID)],
        [(Q * ROWS, LANES), FULL, FULL, (HID, HID), *accs, (ROWS, LANES), (shares * part, HID),
         (Q * ROWS, LANES), (ROWS, LANES), (48, LANES), (48, LANES), (16, LANES), (16, LANES)],
        "first_step",
    )(*parts, theta, f, t, *faces, yl, yr, *halo0, code, w3b, w2b, w1b, *kept, pack1)
    total = reduced(pack)
    g1, gb1, g2, gb2, g3, gb3 = call(
        unpack_kernel,
        [struct(Q, HID), struct(1, HID), struct(HID, HID), struct(1, HID), struct(Q, HID), struct(1, Q)],
        [(shares * part, HID)],
        "unpack",
    )(total)
    return (
        fbar0.reshape(Q, sx, sy, sz),
        theta0.reshape(sx, sy, sz),
        g1,
        gb1.reshape(HID),
        g2,
        gb2.reshape(HID),
        g3.T,
        gb3.reshape(Q),
    )


def solution(mesh):
    pops, cells = P(None, "gx", "gy", None), P("gx", "gy", None)
    return jax.shard_map(
        per_device,
        mesh=mesh,
        in_specs=(pops, cells, cells, P(), P(), P(), P(), P(), P(), pops, cells),
        out_specs=(pops, cells, P(), P(), P(), P(), P(), P()),
        check_vma=False,
    )
```

```python
import math

import jax
import jax.numpy as jnp
import numpy as np
from jax import lax
from jax.experimental import pallas as pl
from jax.experimental.pallas import tpu as pltpu
from jax.sharding import PartitionSpec as P

VELOCITIES = [
    (0, 0, 0), (1, 0, 0), (-1, 0, 0), (0, 1, 0), (0, -1, 0), (0, 0, 1), (0, 0, -1),
    (1, 1, 0), (-1, -1, 0), (1, -1, 0), (-1, 1, 0), (1, 0, 1), (-1, 0, -1), (1, 0, -1),
    (-1, 0, 1), (0, 1, 1), (0, -1, -1), (0, 1, -1), (0, -1, 1),
]
Q = 19
OPPOSITE = [VELOCITIES.index((-a, -b, -c)) for a, b, c in VELOCITIES]
WEIGHTS = [1.0 / 3.0] + [1.0 / 18.0] * 6 + [1.0 / 36.0] * 12
BUOYANCY = [float(np.float32(0.3 * w * c[2])) for w, c in zip(WEIGHTS, VELOCITIES)]
CONDUCTIVITY = 0.1
HOT_WALL = 0.5
COLD_WALL = -0.5
HEATER = 0.5
HID = 128
KP = 32
ROWS = 16
LANES = 128
CH = 512
PACK = 176
F32 = jnp.float32
BF16 = jnp.bfloat16


def moving(axis, sign, orient):
    return [i for i in range(Q) if VELOCITIES[i][axis] * orient == sign]


def diagonal(sx, sy, orient):
    return VELOCITIES.index((sx * orient, sy * orient, 0))


def split(x):
    hi = x.astype(BF16)
    lo = (x - hi.astype(F32)).astype(BF16)
    return hi, lo


def stacked(x):
    return jnp.concatenate(split(x), axis=0)


def nn(a, b):
    return lax.dot_general(a, b, (((1,), (0,)), ((), ())), preferred_element_type=F32)


def nt(a, b):
    return lax.dot_general(a, b, (((1,), (1,)), ((), ())), preferred_element_type=F32)


def left(w):
    hi, lo = split(w)
    return jnp.concatenate(
        [jnp.concatenate([hi, hi], axis=1), jnp.concatenate([lo, lo], axis=1)], axis=0
    )


def product(a, b, rows):
    d = nn(a, b)
    return d[:rows] + d[rows:]


def four_blocks(d, rows):
    return d[:rows, :HID] + d[:rows, HID:] + d[rows:, :HID] + d[rows:, HID:]


def lanes_of(shape):
    return lax.broadcasted_iota(jnp.int32, shape, 1)


def subs_of(shape):
    return lax.broadcasted_iota(jnp.int32, shape, 0)


def shift_z(v, step, fill):
    if step == 1:
        return jnp.where(lanes_of(v.shape) == 0, fill, pltpu.roll(v, 1, 1))
    return jnp.where(lanes_of(v.shape) == LANES - 1, fill, pltpu.roll(v, LANES - 1, 1))


def shift_y(v, step, row):
    if step == 1:
        return jnp.where(subs_of(v.shape) == 0, row, pltpu.roll(v, 1, 0))
    return jnp.where(subs_of(v.shape) == 7, row, pltpu.roll(v, 7, 0))


def tile(ref, i, x):
    if isinstance(ref, tuple):
        return ref[x][8 * i : 8 * i + 8, :]
    k = i * ROWS + x * 8
    return ref[k : k + 8, :]


def halves(ref):
    if isinstance(ref, tuple):
        return [ref[0][...], ref[1][...]]
    return [ref[0:8, :], ref[8:16, :]]


def transposed(w_ref, b_ref, pad_ref):
    pad_ref[...] = jnp.zeros((HID, HID), F32)
    pad_ref[0:Q, :] = w_ref[...]
    if b_ref is not None:
        pad_ref[Q : Q + 1, :] = b_ref[...]
    return pad_ref[...]


def column(b_ref, n, pad_ref):
    pad_ref[...] = jnp.zeros((HID, HID), F32)
    pad_ref[:, 0:n] = jnp.broadcast_to(b_ref[...], (HID, n))
    return jnp.transpose(pad_ref[...])


def rows_in(ref, c):
    n, step = CH // LANES, ref.shape[0] // KP
    order = range(step) if step != ROWS else [0, 7, 8, 15, *range(1, 7), *range(9, 15)]
    return order[c * n : (c + 1) * n], step


def across(ref, c):
    rows, step = rows_in(ref, c)
    return jnp.concatenate([ref[pl.ds(r, KP, stride=step), :] for r in rows], axis=1)


def back(ref, c, value):
    rows, step = rows_in(ref, c)
    for j, r in enumerate(rows):
        ref[pl.ds(r, KP, stride=step), :] = value[:, j * LANES : (j + 1) * LANES]


def fill_features(s_ref, f_ref):
    rows = s_ref.shape[0] // KP
    s_ref[0 : Q * rows, :] = f_ref[...]
    s_ref[Q * rows : (Q + 1) * rows, :] = jnp.ones((rows, LANES), F32)
    s_ref[(Q + 1) * rows :, :] = jnp.zeros(((KP - Q - 1) * rows, LANES), F32)


def wide(b):
    return jnp.concatenate([b] * (CH // LANES), axis=1)


def put_x(value, orient, xp, xm, at):
    for k, i in enumerate(moving(0, 1, orient)):
        xp[at + 8 * k : at + 8 * k + 8, :] = value(i, 1)
    for k, i in enumerate(moving(0, -1, orient)):
        xm[at + 8 * k : at + 8 * k + 8, :] = value(i, 0)


def put_y(value, orient, yp, ym, row):
    for k, i in enumerate(moving(1, 1, orient)):
        for x in range(2):
            yp[row + 2 * k + x : row + 2 * k + x + 1, :] = value(i, x)[7:8]
    for k, i in enumerate(moving(1, -1, orient)):
        for x in range(2):
            ym[row + 2 * k + x : row + 2 * k + x + 1, :] = value(i, x)[0:1]


def put_corners(leftward, rightward, orient, xp, xm, row, at):
    for sx, to in ((1, xp), (-1, xm)):
        for k, (sy, come) in enumerate(((1, leftward), (-1, rightward))):
            j = row + 2 * moving(1, sy, orient).index(diagonal(sx, sy, orient)) + (sx == 1)
            to[at + k : at + k + 1, :] = come[j : j + 1, :]


def streamed(ref, halo, orient, i, x):
    below, above, leftward, rightward, at, row, corner = halo
    sx, sy, sz = (orient * c for c in VELOCITIES[i])
    xs = x - sx
    if xs in (0, 1):
        v = tile(ref, i, xs)
    else:
        k = at + 8 * moving(0, sx, orient).index(i)
        v = (below if sx == 1 else above)[k : k + 8, :]
    if sy:
        if xs in (0, 1):
            k = row + 2 * moving(1, sy, orient).index(i) + xs
            edge = (leftward if sy == 1 else rightward)[k : k + 1, :]
        else:
            k = corner + (sy == -1)
            edge = (below if sx == 1 else above)[k : k + 1, :]
        v = shift_y(v, sy, edge)
    if sz:
        v = shift_z(v, sz, tile(ref, OPPOSITE[i], x))
    return v


def motion(ref, x):
    us = []
    for a in range(3):
        total = None
        for i in range(Q):
            c = VELOCITIES[i][a]
            if c:
                v = tile(ref, i, x)
                total = (v if c == 1 else -v) if total is None else (total + v if c == 1 else total - v)
        us.append(total)
    return us


def warm_neighbours(t_ref, rims, x):
    below, above, leftward, rightward = rims
    t = halves(t_ref)
    lower = below if x == 0 else t[0]
    upper = t[1] if x == 0 else above
    return [
        (upper, lower),
        (shift_y(t[x], -1, rightward[x]), shift_y(t[x], 1, leftward[x])),
        (shift_z(t[x], -1, COLD_WALL), shift_z(t[x], 1, HOT_WALL)),
    ]


def flux(u, a, s, liquid):
    return (CONDUCTIVITY - (0.5 * s) * u[a]) * liquid


def heat_adjoint(us, liquids, theta, codes, flux_rims):
    below, above, leftward, rightward = flux_rims
    out = []
    for x in range(2):
        u, liquid = us[x], liquids[x]
        total = 0.4 * liquid + jnp.where(codes[x] == 1, theta[x], 0.0)
        total = total + (below if x == 0 else flux(us[0], 0, 1, liquids[0]))
        total = total + (flux(us[1], 0, -1, liquids[1]) if x == 0 else above)
        total = total + shift_y(flux(u, 1, 1, liquid), 1, leftward[x])
        total = total + shift_y(flux(u, 1, -1, liquid), -1, rightward[x])
        total = total + shift_z(flux(u, 2, 1, liquid), 1, 0.0)
        total = total + shift_z(flux(u, 2, -1, liquid), -1, 0.0)
        out.append(total)
    return out


def motion_adjoint(t_ref, rims, liquids):
    return [
        [-0.5 * liquids[x] * (plus - minus) for plus, minus in warm_neighbours(t_ref, rims, x)]
        for x in range(2)
    ]


def with_motion(value, ubar, i):
    for a in range(3):
        c = VELOCITIES[i][a]
        if c:
            value = value + ubar[a] if c == 1 else value - ubar[a]
    return value


def hidden(fx, a1, a2, b2):
    h1 = jnp.tanh(product(a1, fx, HID))
    h1x = stacked(h1)
    h2 = jnp.tanh(product(a2, h1x, HID) + b2)
    return h1, h1x, h2


def network_back(s1, s2, d, w3b, w2b, w1b):
    dx = stacked(d)
    p = product(w3b, dx, HID) * s2
    px = stacked(p)
    qx = stacked(product(w2b, px, HID) * s1)
    return product(w1b, qx, KP), (folded(d), folded(p)), dx, px, qx


def folded(d):
    return sum(d[:, j * LANES : (j + 1) * LANES] for j in range(CH // LANES))


def gather(accs, values, first):
    for ref, value in zip(accs, values):
        ref[...] = value if first else ref[...] + value


def weight_products(fx, h1x, h2x, dx, px, qx):
    return nt(h1x, px), nt(fx, qx), nt(dx, h2x)


def write_pack(pack, acc2, acc1, acc3, accb, accp, pad_ref):
    pack[0:HID, :] = four_blocks(acc2[...], HID)
    pack[HID : HID + 24, :] = four_blocks(acc1[...], KP)[0:24]
    pack[HID + 24 : HID + 48, :] = four_blocks(acc3[...], KP)[0:24]
    pad_ref[...] = jnp.zeros((HID, HID), F32)
    pad_ref[0:KP, :] = accb[...]
    for k, sums in ((21, accp[...]), (22, pad_ref[...])):
        row = jnp.sum(jnp.transpose(sums), axis=0, keepdims=True)
        pack[HID + k : HID + k + 1, :] = row


def collided(f, t, code, outs, i):
    k = i * ROWS
    relaxed = f[k : k + ROWS, :] + outs[k : k + ROWS, :]
    if BUOYANCY[i]:
        relaxed = relaxed + BUOYANCY[i] * t[...]
    o = OPPOSITE[i] * ROWS
    return jnp.where(code[...] == 0, relaxed, f[o : o + ROWS, :])


def forward_chunk(feat, c, l1, l2, l3, b2t, b3t):
    h1, _, h2 = hidden(stacked(across(feat, c)), l1, l2, b2t)
    return h1, h2, product(l3, stacked(h2), KP) + b3t


def edge_rows_kernel(
    w1_in, b1_in, w2_in, b2_in, w3_in, b3_in, f_in, t_in, code_in, adj_in, theta_in,
    w1, w2, w3, f, t, code, adj, theta, l1, l2, l3, b2t, b3t, h1s, h2s, out0, yp, ym,
    feat, outs, pad, b1, b2, b3, sems,
):
    ins = (w1_in, b1_in, w2_in, b2_in, w3_in, b3_in, f_in, t_in, code_in, adj_in, theta_in)
    here = (w1, b1, w2, b2, w3, b3, f, t, code, adj, theta)
    copies = [pltpu.make_async_copy(a, b, sems.at[k]) for k, (a, b) in enumerate(zip(ins, here))]
    for c in copies:
        c.start()
    for c in copies[:6]:
        c.wait()
    l1[...] = left_narrow(jnp.transpose(transposed(w1, b1, pad)))
    l2[...] = left(jnp.transpose(w2[...]))
    pad[...] = jnp.zeros((HID, HID), F32)
    pad[0:Q, :] = w3[...]
    l3[...] = left(pad[0:KP, :])
    b2t[...] = wide(column(b2, HID, pad))
    b3t[...] = wide(column(b3, Q, pad)[0:KP])
    copies[6].wait()
    fill_features(feat, f)
    h1, h2, out = forward_chunk(feat, 0, l1[...], l2[...], l3[...], b2t[...], b3t[...])
    h1s[0], h2s[0], out0[...] = h1, h2, out
    outs[...] = jnp.zeros(outs.shape, F32)
    back(outs, 0, out)
    for c in copies[7:]:
        c.wait()
    put_y(lambda i, x: tile(adj, i, x), -1, yp, ym, 12)

    def value(i, x):
        return collided(f, t, code, outs, i)[8 * x : 8 * x + 8]

    put_y(value, 1, yp, ym, 0)
    for x in range(2):
        yp[10 + x : 11 + x, :] = t[8 * x + 7 : 8 * x + 8, :]
        ym[10 + x : 11 + x, :] = t[8 * x : 8 * x + 1, :]


def other_rows_kernel(
    f, t, code, adj, l1, l2, l3, b2t, b3t, out0, w1, w2, w3,
    post, h1s, h2s, xp, xm, w3b, w2b, w1b,
    feat, outs, pad,
):
    w3b[...], w2b[...], w1b[...] = back_weights(w1, w2, w3, pad)
    fill_features(feat, f)
    back(outs, 0, out0[...])
    for c in range(1, ROWS * LANES // CH):
        h1, h2, out = forward_chunk(feat, c, l1[...], l2[...], l3[...], b2t[...], b3t[...])
        h1s[c - 1], h2s[c - 1] = h1, h2
        back(outs, c, out)
    for i in range(Q):
        post[i * ROWS : (i + 1) * ROWS, :] = collided(f, t, code, outs, i)
    put_x(lambda i, x: tile(adj, i, x), -1, xp, xm, 48)
    put_x(lambda i, x: tile(post, i, x), 1, xp, xm, 0)
    xp[40:48, :] = t[8:16, :]
    xm[40:48, :] = t[0:8, :]


def prepare_kernel(
    f, h1a, h2a, h1b, h2b, _,
    fxs, h1xs, h2xs, s1, s2,
    feat,
):
    fill_features(feat, f)
    for c in range(ROWS * LANES // CH):
        h1, h2 = (h1a[0], h2a[0]) if c == 0 else (h1b[c - 1], h2b[c - 1])
        fxs[c], h1xs[c], h2xs[c] = stacked(across(feat, c)), stacked(h1), stacked(h2)
        s1[c], s2[c] = 1.0 - h1 * h1, 1.0 - h2 * h2


def left_narrow(w):
    hi, lo = split(w + pltpu.roll(w, KP, 1))
    return jnp.concatenate([hi, lo], axis=0)[:, : 2 * KP]


def rims_of(below, above, leftward, rightward, at, row):
    return (
        below[at : at + 8, :],
        above[at : at + 8, :],
        [leftward[row + x : row + x + 1, :] for x in range(2)],
        [rightward[row + x : row + x + 1, :] for x in range(2)],
    )


def collision_gradient(adj, halo, code, grad, masked, lift):
    for x in range(2):
        fluid = code[8 * x : 8 * x + 8, :] == 0
        total = None
        for i in range(Q):
            k = i * ROWS + 8 * x
            g = streamed(adj, halo, -1, i, x)
            grad[k : k + 8, :] = g
            g = jnp.where(fluid, g, 0.0)
            masked[k : k + 8, :] = g
            if BUOYANCY[i]:
                total = BUOYANCY[i] * g if total is None else total + BUOYANCY[i] * g
        lift[8 * x : 8 * x + 8, :] = total
    masked[Q * ROWS :, :] = jnp.zeros(((KP - Q) * ROWS, LANES), F32)


def back_weights(w1, w2, w3, pad):
    pad[...] = jnp.zeros((HID, HID), F32)
    pad[0:Q, :] = w3[...]
    w3b = left_narrow(jnp.transpose(pad[...]))
    w2b = left(w2[...])
    pad[...] = jnp.zeros((HID, HID), F32)
    pad[0:Q, :] = w1[...]
    w1b = left(pad[0:KP, :])
    return w3b, w2b, w1b


def middle_kernel(
    x, post, f, t, code, adj, face, leftward, rightward, l1, l2, b2t, w3b, w2b, w1b,
    f1, t1, fbar, lift, accb, accp, fxs, h1xs, h2s, dxs, pxs, qxs,
    feat, grad, masked, dfs,
):
    kind = code[8 * x : 8 * x + 8, :]
    fluid = kind == 0
    halo = (face, face, leftward, rightward, 0, 0, 88)
    adj_halo = (face, face, leftward, rightward, 48, 12, 90)
    warmth = None
    for i in range(Q):
        k = 8 * i
        f1[k : k + 8, :] = streamed(post, halo, 1, i, x)
        g = streamed(adj, adj_halo, -1, i, x)
        grad[k : k + 8, :] = g
        g = jnp.where(fluid, g, 0.0)
        masked[k : k + 8, :] = g
        if BUOYANCY[i]:
            warmth = BUOYANCY[i] * g if warmth is None else warmth + BUOYANCY[i] * g
    lift[...] = warmth
    masked[8 * Q :, :] = jnp.zeros(((KP - Q) * 8, LANES), F32)
    u = motion(f, x)
    here = t[8 * x : 8 * x + 8, :]
    total = 0.4 * here
    rims = rims_of(face, face, leftward, rightward, 40, 10)
    for a, (plus, minus) in enumerate(warm_neighbours(t, rims, x)):
        total = total + (CONDUCTIVITY - 0.5 * u[a]) * plus
        total = total + (CONDUCTIVITY + 0.5 * u[a]) * minus
    t1[...] = jnp.where(fluid, total, jnp.where(kind == 1, here, HEATER))
    fill_features(feat, f1)
    for c in range(8 * LANES // CH):
        fx = stacked(across(feat, c))
        h1, h1x, h2 = hidden(fx, l1[...], l2[...], b2t[...])
        d = across(masked, c)
        df, sums, dx, px, qx = network_back(
            1.0 - h1 * h1, 1.0 - h2 * h2, d, w3b[...], w2b[...], w1b[...]
        )
        gather((accb, accp), sums, c == 0)
        back(dfs, c, df)
        fxs[c], h1xs[c], h2s[c] = fx, h1x, h2
        dxs[c], pxs[c], qxs[c] = dx, px, qx
    for i in range(Q):
        k, o = 8 * i, 8 * OPPOSITE[i]
        fbar[k : k + 8, :] = jnp.where(
            fluid, grad[k : k + 8, :] + dfs[k : k + 8, :], grad[o : o + 8, :]
        )


def weights_kernel(*refs):
    first, second, (_, pack, pad, accb, accp, *accs) = refs[:8], refs[8:16], refs[16:]
    accb[...] = first[0][...] + second[0][...]
    accp[...] = first[1][...] + second[1][...]
    for plane in (first, second):
        for c in range(plane[2].shape[0]):
            fx, h1x, h2, dx, px, qx = (v[c] for v in plane[2:])
            values = weight_products(fx, h1x, stacked(h2), dx, px, qx)
            gather(accs, values, plane is first and c == 0)
    write_pack(pack, *accs, accb, accp, pad)


def coefficient(u, a, s, kind):
    return jnp.where(kind == 0, CONDUCTIVITY - (0.5 * s) * u[a], 0.0)


def adjoint_parts(fbar, lift, f1, t1, theta, code, t_rims, flux_rims):
    codes, thetas = halves(code), halves(theta)
    liquids = [jnp.where(k == 0, v, 0.0) for k, v in zip(codes, thetas)]
    us = [motion(f1, x) for x in range(2)]
    ubar = motion_adjoint(t1, t_rims, liquids)
    warm = heat_adjoint(us, liquids, thetas, codes, flux_rims)
    warm = [v + w for v, w in zip(warm, halves(lift))]

    def adj(i, x):
        return with_motion(tile(fbar, i, x), ubar[x], i)

    return codes, liquids, us, adj, warm


def no_rims():
    blank, row = jnp.zeros((8, LANES), F32), jnp.zeros((1, LANES), F32)
    return blank, blank, [row, row], [row, row]


def rows_of(ref, at):
    return [ref[at + x : at + x + 1, :] for x in range(2)]


def paired(refs):
    return [tuple(refs[2 * k : 2 * k + 2]) for k in range(4)]


def along_y_kernel(*refs):
    fbar, lift, f1, t1 = paired(refs)
    f0, theta, code, yp, ym = refs[8:]
    codes, liquids, us, adj, warm = adjoint_parts(
        fbar, lift, f1, t1, theta, code, no_rims(), no_rims()
    )
    ts = halves(t1)
    for s, e, out in ((1, 7, yp), (-1, 0, ym)):
        for x in range(2):
            u0 = motion(f0, x)
            parts = [adj(i, x) for i in moving(1, s, -1)]
            parts += [ts[x], flux(us[x], 1, s, liquids[x]), liquids[x], warm[x]]
            parts.append(coefficient(u0, 1, s, codes[x]))
            for k, v in enumerate(parts):
                out[2 * k + x : 2 * k + x + 1, :] = v[e : e + 1]
        out[20:21, :] = flux(us[1], 0, 1, liquids[1])[e : e + 1]
        out[21:22, :] = flux(us[0], 0, -1, liquids[0])[e : e + 1]


def along_x_kernel(*refs):
    fbar, lift, f1, t1 = paired(refs)
    f0, theta, code, leftward, rightward, xp, xm, yl, yr = refs[8:]
    zero, _, _, _ = no_rims()
    codes, liquids, us, adj, warm = adjoint_parts(
        fbar, lift, f1, t1, theta, code,
        (zero, zero, rows_of(leftward, 10), rows_of(rightward, 10)),
        (zero, zero, rows_of(leftward, 12), rows_of(rightward, 12)),
    )
    ts = halves(t1)
    for s, x, out in ((1, 1, xp), (-1, 0, xm)):
        parts = [adj(i, x) for i in moving(0, s, -1)]
        parts += [ts[x], liquids[x], warm[x]]
        parts.append(coefficient(motion(f0, x), 0, s, codes[x]))
        parts.append(flux(us[x], 0, s, liquids[x]))
        for k, v in enumerate(parts):
            out[8 * k : 8 * k + 8, :] = v
    for k, (s, e, come, out) in enumerate(((1, 0, leftward, yl), (-1, 7, rightward, yr))):
        t_come, flux_come, liquid, warm_come, factor = (
            rows_of(come, 10 + 2 * j) for j in range(5)
        )
        for x in range(2):
            for j in range(5):
                r = 2 * j + x
                out[r : r + 1, :] = (
                    come[r : r + 1, :] + 0.5 * liquid[x] * ts[x][e : e + 1]
                )
            done = warm_come[x] + flux(us[x], 1, -s, liquids[x])[e : e + 1]
            for j, v in enumerate((t_come[x], liquid[x], done, factor[x], flux_come[x])):
                r = 10 + 2 * j + x
                out[r : r + 1, :] = v
        for sx, x, to in ((1, 1, xp), (-1, 0, xm)):
            r = 2 * moving(1, s, -1).index(diagonal(sx, s, -1)) + x
            for j, v in enumerate(
                (out[r : r + 1, :], liquid[x], t_come[x], come[21 - x : 22 - x, :])
            ):
                to[80 + 4 * k + j : 81 + 4 * k + j, :] = v


def complete(
    fbar, lift, f1, t1, theta, code, below, above, yl, yr,
    adj1, warm1, hbelow, habove, hleft, hright,
):
    _, liquids, us, adj, warm = adjoint_parts(
        fbar, lift, f1, t1, theta, code,
        (below[40:48, :], above[40:48, :], rows_of(yl, 10), rows_of(yr, 10)),
        (below[72:80, :], above[72:80, :], rows_of(yl, 18), rows_of(yr, 18)),
    )
    ts = halves(t1)
    for x in range(2):
        warm1[8 * x : 8 * x + 8, :] = warm[x]
        for i in range(Q):
            k = i * ROWS + 8 * x
            adj1[k : k + 8, :] = adj(i, x)
    faces = []
    for s, x, come, out in ((1, 0, below, hbelow), (-1, 1, above, habove)):
        for k in range(5):
            out[8 * k : 8 * k + 8, :] = (
                come[8 * k : 8 * k + 8, :] + 0.5 * come[48:56, :] * ts[x]
            )
        for k, rows in enumerate((yl, yr)):
            j = 80 + 4 * k
            out[40 + k : 41 + k, :] = (
                come[j : j + 1, :] + 0.5 * come[j + 1 : j + 2, :] * rows[10 + x : 11 + x, :]
            )
        faces.append(come[64:72, :] * (come[56:64, :] + flux(us[x], 0, -s, liquids[x])))
    edges = []
    for k, (s, rows, out) in enumerate(((1, yl, hleft), (-1, yr, hright))):
        j = 80 + 4 * k
        out[0:10, :] = rows[0:10, :]
        edge = []
        for sx, x, come in ((1, 0, below), (-1, 1, above)):
            r = 2 * moving(1, s, -1).index(diagonal(sx, s, -1)) + x
            out[r : r + 1, :] = (
                rows[r : r + 1, :]
                - 0.5 * rows[12 + x : 13 + x, :] * come[j + 2 : j + 3, :]
            )
            edge.append(
                rows[16 + x : 17 + x, :]
                * (rows[14 + x : 15 + x, :] + come[j + 3 : j + 4, :])
            )
        edges.append(edge)
    return (*faces, *edges)


def first_step_kernel(
    scale, known,
    theta2, f, t, below, above, yl, yr,
    tbelow, tabove, tleft, tright, code, w3b, w2b, w1b, fxs, h1xs, h2xs, s1, s2, pack1,
    fbar, thetabar, pack,
    grad, masked, dfs, pad, acc2, acc1, acc3, accb, accp, lift, total,
    adj, theta, hbelow, habove, hleft, hright,
):
    flux_rims = complete(
        *paired(known), theta2, code, below, above, yl, yr,
        adj, theta, hbelow, habove, hleft, hright,
    )
    halo = (hbelow, habove, hleft, hright, 0, 0, 40)
    collision_gradient(adj, halo, code, grad, masked, lift)
    for c in range(ROWS * LANES // CH):
        d = across(masked, c)
        df, sums, dx, px, qx = network_back(s1[c], s2[c], d, w3b[...], w2b[...], w1b[...])
        values = weight_products(fxs[c], h1xs[c], h2xs[c], dx, px, qx)
        gather((acc2, acc1, acc3, accb, accp), (*values, *sums), c == 0)
        back(dfs, c, df)
    write_pack(total, acc2, acc1, acc3, accb, accp, pad)
    parts, part, _ = pack.shape
    total[PACK:, :] = jnp.zeros((parts * part - PACK, HID), F32)
    total[0:PACK, :] = (total[0:PACK, :] + pack1[...]) * scale
    for k in range(parts):
        pack[k] = total[k * part : (k + 1) * part, :]
    codes, thetas = halves(code), halves(theta)
    liquids = [jnp.where(k == 0, v, 0.0) for k, v in zip(codes, thetas)]
    rims = rims_of(tbelow, tabove, tleft, tright, 40, 10)
    ubar = motion_adjoint(t, rims, liquids)
    new = heat_adjoint([motion(f, x) for x in range(2)], liquids, thetas, codes, flux_rims)
    for x in range(2):
        thetabar[8 * x : 8 * x + 8, :] = new[x] + lift[8 * x : 8 * x + 8, :]
        fluid = codes[x] == 0
        for i in range(Q):
            k, o = i * ROWS + 8 * x, OPPOSITE[i] * ROWS + 8 * x
            value = jnp.where(fluid, grad[k : k + 8, :] + dfs[k : k + 8, :], grad[o : o + 8, :])
            fbar[k : k + 8, :] = with_motion(value, ubar[x], i)


def struct(*shape):
    return jax.ShapeDtypeStruct(shape, F32)


def call(kernel, outs, scratch, name, more=(), **specs):
    return pl.pallas_call(
        kernel,
        out_shape=outs,
        scratch_shapes=[pltpu.VMEM(s, F32) for s in scratch] + list(more),
        **specs,
        compiler_params=pltpu.CompilerParams(vmem_limit_bytes=40 * 1024 * 1024),
        name=name,
    )


FULL = (KP * ROWS, LANES)
POPS = struct(Q * ROWS, LANES)
WARM = struct(ROWS, LANES)


def shifted(value, axis, by):
    count = lax.axis_size(axis)
    return lax.ppermute(value, axis, [(s, (s + by) % count) for s in range(count)])


def along(axis, plus, minus):
    return shifted(plus, axis, 1), shifted(minus, axis, -1)


def edge_kernel(blocks, xp, xm, leftward, rightward, xp_out, xm_out):
    xp_out[...] = xp[...]
    xm_out[...] = xm[...]
    for orient, row, at in blocks:
        put_corners(leftward, rightward, orient, xp_out, xm_out, row, at)


def swapped(value, groups):
    return lax.all_to_all(
        value, ("gx", "gy"), 0, 0, axis_index_groups=groups, tiled=True
    )


def factors_of(nx):
    near = 2 if nx % 2 == 0 else 1
    far = nx // 24 if nx % 24 == 0 else 1
    return far, nx // (far * near), near


def shares_of(nx, ny):
    far, _, near = factors_of(nx)
    return far * near * ny


def groups_of(nx, ny):
    far, mid, near = factors_of(nx)
    at = np.arange(nx * ny).reshape(far, mid, near, ny)
    return (
        at.transpose(1, 0, 2, 3).reshape(mid, -1).tolist(),
        at.transpose(0, 2, 3, 1).reshape(-1, mid).tolist(),
    )


def total_kernel(parts, out):
    value = parts[0]
    for k in range(1, parts.shape[0]):
        value = value + parts[k]
    for k in range(out.shape[0]):
        out[k] = value


def summed(parts, copies):
    return call(total_kernel, struct(copies, *parts.shape[1:]), [], "total")(parts)


def reduced(pack):
    share, same = groups_of(lax.axis_size("gx"), lax.axis_size("gy"))
    part = summed(swapped(pack, share), len(same[0]))
    part = summed(swapped(part, same), len(share[0]))
    return swapped(part, share)


def unpack_kernel(parts, w1, b1, w2, b2, w3, b3, pack):
    count, part, _ = parts.shape
    for k in range(count):
        pack[k * part : (k + 1) * part, :] = parts[k]
    w2[...] = pack[0:HID, :]
    w1[...] = pack[HID : HID + Q, :]
    b1[...] = pack[HID + Q : HID + Q + 1, :]
    b2[...] = pack[HID + 21 : HID + 22, :]
    b3[...] = pack[HID + 22 : HID + 23, 0:Q]
    w3[...] = pack[HID + 24 : HID + 24 + Q, :]


def per_device(f, t, code, w1, b1, w2, b2, w3, b3, adj, theta):
    sx, sy, sz = t.shape
    cells = sx * lax.axis_size("gx") * sy * lax.axis_size("gy") * sz
    f, adj = f.reshape(Q * ROWS, LANES), adj.reshape(Q * ROWS, LANES)
    t, code, theta = (v.reshape(ROWS, LANES) for v in (t, code, theta))
    b1, b2, b3 = (v.reshape(1, -1) for v in (b1, b2, b3))
    w3 = w3.T
    ins = (w1, b1, w2, b2, w3, b3, f, t, code, adj, theta)
    like = [jax.ShapeDtypeStruct(v.shape, v.dtype) for v in ins]
    held = [v for k, v in enumerate(like) if k not in (1, 3, 5)]
    count = ROWS * LANES // CH

    def narrow(*shape):
        return jax.ShapeDtypeStruct(shape, BF16)

    outs = call(
        edge_rows_kernel,
        [*held, narrow(2 * HID, 2 * KP), narrow(2 * HID, 2 * HID), narrow(2 * KP, 2 * HID),
         struct(HID, CH), struct(KP, CH), struct(1, HID, CH), struct(1, HID, CH),
         struct(KP, CH), struct(24, LANES), struct(24, LANES)],
        [FULL, FULL, (HID, HID)],
        "edge_rows",
        [pltpu.VMEM(v.shape, v.dtype) for v in (b1, b2, b3)] + [pltpu.SemaphoreType.DMA((11,))],
        in_specs=[pl.BlockSpec(memory_space=pltpu.HBM)] * 11,
    )(*(pltpu.with_memory_space_constraint(v, pltpu.HBM) for v in ins))
    w1, w2, w3, f, t, code, adj, theta, l1, l2, l3, b2t, b3t, h1a, h2a, out0, yp, ym = outs
    sides = along("gy", yp, ym)
    post, h1b, h2b, xp, xm, w3b, w2b, w1b = call(
        other_rows_kernel,
        [POPS, *[struct(count - 1, HID, CH)] * 2, struct(96, LANES), struct(96, LANES),
         narrow(2 * HID, 2 * KP), narrow(2 * HID, 2 * HID), narrow(2 * KP, 2 * HID)],
        [FULL, FULL, (HID, HID)],
        "other_rows",
    )(f, t, code, adj, l1, l2, l3, b2t, b3t, out0, w1, w2, w3)
    blocks = ((1, 0, 88), (-1, 12, 90))
    xp, xm = call(
        lambda *refs: edge_kernel(blocks, *refs), [struct(96, LANES)] * 2, [], "corners"
    )(xp, xm, *sides)
    below, above = along("gx", xp, xm)
    halo0 = (below, above, *sides)
    accs = [(2 * HID, 2 * HID), (2 * KP, 2 * HID), (2 * KP, 2 * HID), (KP, LANES), (HID, LANES)]
    plane, half = struct(8 * Q, LANES), struct(8, LANES)
    small, large = (
        jax.ShapeDtypeStruct((8 * LANES // CH, 2 * n, CH), BF16) for n in (KP, HID)
    )
    planes = [
        call(
            lambda *refs, x=x: middle_kernel(x, *refs),
            [plane, half, plane, half, struct(KP, LANES), struct(HID, LANES), small, large,
             struct(8 * LANES // CH, HID, CH), small, large, large],
            [(8 * KP, LANES), (8 * Q, LANES), (8 * KP, LANES), (8 * KP, LANES)],
            "middle",
        )(post, f, t, code, adj, face, *sides, l1, l2, b2t, w3b, w2b, w1b)
        for x, face in enumerate((below, above))
    ]
    parts = [planes[x][k] for k in (2, 3, 0, 1) for x in range(2)]
    known = (*parts, f, theta, code)
    yp, ym = call(along_y_kernel, [struct(24, LANES)] * 2, [], "along_y")(*known)
    come = along("gy", yp, ym)
    xp, xm, yl, yr = call(
        along_x_kernel, [struct(88, LANES)] * 2 + [struct(24, LANES)] * 2, [], "along_x"
    )(*known, *come)
    faces = along("gx", xp, xm)
    kept = call(
        prepare_kernel,
        [narrow(count, 2 * KP, CH), *[narrow(count, 2 * HID, CH)] * 2, *[struct(count, HID, CH)] * 2],
        [FULL],
        "prepare",
        in_specs=[pl.BlockSpec(memory_space=pltpu.VMEM)] * 5 + [pl.BlockSpec(memory_space=pl.ANY)],
    )(f, h1a, h2a, h1b, h2b, xp)
    pack1 = call(
        weights_kernel,
        struct(PACK, HID),
        [(HID, HID), *accs[3:], *accs[:3]],
        "weights",
        in_specs=[pl.BlockSpec(memory_space=pltpu.VMEM)] * 16 + [pl.BlockSpec(memory_space=pl.ANY)],
    )(*planes[0][4:], *planes[1][4:], xp)
    scale = 1.0 / math.sqrt(cells)
    shares = shares_of(lax.axis_size("gx"), lax.axis_size("gy"))
    part = -(-(PACK + 8) // shares)
    fbar0, theta0, pack = call(
        lambda *refs: first_step_kernel(scale, refs[:8], *refs[8:]),
        [POPS, WARM, struct(shares, part, HID)],
        [(Q * ROWS, LANES), FULL, FULL, (HID, HID), *accs, (ROWS, LANES), (shares * part, HID),
         (Q * ROWS, LANES), (ROWS, LANES), (48, LANES), (48, LANES), (16, LANES), (16, LANES)],
        "first_step",
    )(*parts, theta, f, t, *faces, yl, yr, *halo0, code, w3b, w2b, w1b, *kept, pack1)
    total = reduced(pack)
    g1, gb1, g2, gb2, g3, gb3 = call(
        unpack_kernel,
        [struct(Q, HID), struct(1, HID), struct(HID, HID), struct(1, HID), struct(Q, HID), struct(1, Q)],
        [(shares * part, HID)],
        "unpack",
    )(total)
    return (
        fbar0.reshape(Q, sx, sy, sz),
        theta0.reshape(sx, sy, sz),
        g1,
        gb1.reshape(HID),
        g2,
        gb2.reshape(HID),
        g3.T,
        gb3.reshape(Q),
    )


def solution(mesh):
    pops, cells = P(None, "gx", "gy", None), P("gx", "gy", None)
    return jax.shard_map(
        per_device,
        mesh=mesh,
        in_specs=(pops, cells, cells, P(), P(), P(), P(), P(), P(), pops, cells),
        out_specs=(pops, cells, P(), P(), P(), P(), P(), P()),
        check_vma=False,
    )
```

```python
import math

import jax
import jax.numpy as jnp
import numpy as np
from jax import lax
from jax.experimental import pallas as pl
from jax.experimental.pallas import tpu as pltpu
from jax.sharding import PartitionSpec as P

VELOCITIES = [
    (0, 0, 0), (1, 0, 0), (-1, 0, 0), (0, 1, 0), (0, -1, 0), (0, 0, 1), (0, 0, -1),
    (1, 1, 0), (-1, -1, 0), (1, -1, 0), (-1, 1, 0), (1, 0, 1), (-1, 0, -1), (1, 0, -1),
    (-1, 0, 1), (0, 1, 1), (0, -1, -1), (0, 1, -1), (0, -1, 1),
]
Q = 19
OPPOSITE = [VELOCITIES.index((-a, -b, -c)) for a, b, c in VELOCITIES]
WEIGHTS = [1.0 / 3.0] + [1.0 / 18.0] * 6 + [1.0 / 36.0] * 12
BUOYANCY = [float(np.float32(0.3 * w * c[2])) for w, c in zip(WEIGHTS, VELOCITIES)]
CONDUCTIVITY = 0.1
HOT_WALL = 0.5
COLD_WALL = -0.5
HEATER = 0.5
HID = 128
KP = 32
ROWS = 16
LANES = 128
CH = 1024
PACK = 176
F32 = jnp.float32
BF16 = jnp.bfloat16


def moving(axis, sign, orient):
    return [i for i in range(Q) if VELOCITIES[i][axis] * orient == sign]


def diagonal(sx, sy, orient):
    return VELOCITIES.index((sx * orient, sy * orient, 0))


def split(x):
    hi = x.astype(BF16)
    lo = (x - hi.astype(F32)).astype(BF16)
    return hi, lo


def stacked(x):
    return jnp.concatenate(split(x), axis=0)


def nn(a, b):
    return lax.dot_general(a, b, (((1,), (0,)), ((), ())), preferred_element_type=F32)


def nt(a, b):
    return lax.dot_general(a, b, (((1,), (1,)), ((), ())), preferred_element_type=F32)


def left(w):
    hi, lo = split(w)
    return jnp.concatenate(
        [jnp.concatenate([hi, hi], axis=1), jnp.concatenate([lo, lo], axis=1)], axis=0
    )


def product(a, b, rows):
    d = nn(a, b)
    return d[:rows] + d[rows:]


def four_blocks(d, rows):
    return d[:rows, :HID] + d[:rows, HID:] + d[rows:, :HID] + d[rows:, HID:]


def lanes_of(shape):
    return lax.broadcasted_iota(jnp.int32, shape, 1)


def subs_of(shape):
    return lax.broadcasted_iota(jnp.int32, shape, 0)


def shift_z(v, step, fill):
    if step == 1:
        return jnp.where(lanes_of(v.shape) == 0, fill, pltpu.roll(v, 1, 1))
    return jnp.where(lanes_of(v.shape) == LANES - 1, fill, pltpu.roll(v, LANES - 1, 1))


def shift_y(v, step, row):
    if step == 1:
        return jnp.where(subs_of(v.shape) == 0, row, pltpu.roll(v, 1, 0))
    return jnp.where(subs_of(v.shape) == 7, row, pltpu.roll(v, 7, 0))


def tile(ref, i, x):
    if isinstance(ref, tuple):
        return ref[x][8 * i : 8 * i + 8, :]
    k = i * ROWS + x * 8
    return ref[k : k + 8, :]


def halves(ref):
    if isinstance(ref, tuple):
        return [ref[0][...], ref[1][...]]
    return [ref[0:8, :], ref[8:16, :]]


def transposed(w_ref, b_ref, pad_ref):
    pad_ref[...] = jnp.zeros((HID, HID), F32)
    pad_ref[0:Q, :] = w_ref[...]
    if b_ref is not None:
        pad_ref[Q : Q + 1, :] = b_ref[...]
    return pad_ref[...]


def column(b_ref, n, pad_ref):
    pad_ref[...] = jnp.zeros((HID, HID), F32)
    pad_ref[:, 0:n] = jnp.broadcast_to(b_ref[...], (HID, n))
    return jnp.transpose(pad_ref[...])


def rows_in(ref, c):
    n, step = CH // LANES, ref.shape[0] // KP
    order = range(step) if step != ROWS else [0, 7, 8, 15, *range(1, 7), *range(9, 15)]
    return order[c * n : (c + 1) * n], step


def across(ref, c):
    rows, step = rows_in(ref, c)
    return jnp.concatenate([ref[pl.ds(r, KP, stride=step), :] for r in rows], axis=1)


def back(ref, c, value):
    rows, step = rows_in(ref, c)
    for j, r in enumerate(rows):
        ref[pl.ds(r, KP, stride=step), :] = value[:, j * LANES : (j + 1) * LANES]


def fill_features(s_ref, f_ref):
    rows = s_ref.shape[0] // KP
    s_ref[0 : Q * rows, :] = f_ref[...]
    s_ref[Q * rows : (Q + 1) * rows, :] = jnp.ones((rows, LANES), F32)
    s_ref[(Q + 1) * rows :, :] = jnp.zeros(((KP - Q - 1) * rows, LANES), F32)


def wide(b):
    return jnp.concatenate([b] * (CH // LANES), axis=1)


def put_x(value, orient, xp, xm, at):
    for k, i in enumerate(moving(0, 1, orient)):
        xp[at + 8 * k : at + 8 * k + 8, :] = value(i, 1)
    for k, i in enumerate(moving(0, -1, orient)):
        xm[at + 8 * k : at + 8 * k + 8, :] = value(i, 0)


def put_y(value, orient, yp, ym, row):
    for k, i in enumerate(moving(1, 1, orient)):
        for x in range(2):
            yp[row + 2 * k + x : row + 2 * k + x + 1, :] = value(i, x)[7:8]
    for k, i in enumerate(moving(1, -1, orient)):
        for x in range(2):
            ym[row + 2 * k + x : row + 2 * k + x + 1, :] = value(i, x)[0:1]


def put_corners(leftward, rightward, orient, xp, xm, row, at):
    for sx, to in ((1, xp), (-1, xm)):
        for k, (sy, come) in enumerate(((1, leftward), (-1, rightward))):
            j = row + 2 * moving(1, sy, orient).index(diagonal(sx, sy, orient)) + (sx == 1)
            to[at + k : at + k + 1, :] = come[j : j + 1, :]


def streamed(ref, halo, orient, i, x):
    below, above, leftward, rightward, at, row, corner = halo
    sx, sy, sz = (orient * c for c in VELOCITIES[i])
    xs = x - sx
    if xs in (0, 1):
        v = tile(ref, i, xs)
    else:
        k = at + 8 * moving(0, sx, orient).index(i)
        v = (below if sx == 1 else above)[k : k + 8, :]
    if sy:
        if xs in (0, 1):
            k = row + 2 * moving(1, sy, orient).index(i) + xs
            edge = (leftward if sy == 1 else rightward)[k : k + 1, :]
        else:
            k = corner + (sy == -1)
            edge = (below if sx == 1 else above)[k : k + 1, :]
        v = shift_y(v, sy, edge)
    if sz:
        v = shift_z(v, sz, tile(ref, OPPOSITE[i], x))
    return v


def motion(ref, x):
    us = []
    for a in range(3):
        total = None
        for i in range(Q):
            c = VELOCITIES[i][a]
            if c:
                v = tile(ref, i, x)
                total = (v if c == 1 else -v) if total is None else (total + v if c == 1 else total - v)
        us.append(total)
    return us


def warm_neighbours(t_ref, rims, x):
    below, above, leftward, rightward = rims
    t = halves(t_ref)
    lower = below if x == 0 else t[0]
    upper = t[1] if x == 0 else above
    return [
        (upper, lower),
        (shift_y(t[x], -1, rightward[x]), shift_y(t[x], 1, leftward[x])),
        (shift_z(t[x], -1, COLD_WALL), shift_z(t[x], 1, HOT_WALL)),
    ]


def flux(u, a, s, liquid):
    return (CONDUCTIVITY - (0.5 * s) * u[a]) * liquid


def heat_adjoint(us, liquids, theta, codes, flux_rims):
    below, above, leftward, rightward = flux_rims
    out = []
    for x in range(2):
        u, liquid = us[x], liquids[x]
        total = 0.4 * liquid + jnp.where(codes[x] == 1, theta[x], 0.0)
        total = total + (below if x == 0 else flux(us[0], 0, 1, liquids[0]))
        total = total + (flux(us[1], 0, -1, liquids[1]) if x == 0 else above)
        total = total + shift_y(flux(u, 1, 1, liquid), 1, leftward[x])
        total = total + shift_y(flux(u, 1, -1, liquid), -1, rightward[x])
        total = total + shift_z(flux(u, 2, 1, liquid), 1, 0.0)
        total = total + shift_z(flux(u, 2, -1, liquid), -1, 0.0)
        out.append(total)
    return out


def motion_adjoint(t_ref, rims, liquids):
    return [
        [-0.5 * liquids[x] * (plus - minus) for plus, minus in warm_neighbours(t_ref, rims, x)]
        for x in range(2)
    ]


def with_motion(value, ubar, i):
    for a in range(3):
        c = VELOCITIES[i][a]
        if c:
            value = value + ubar[a] if c == 1 else value - ubar[a]
    return value


def hidden(fx, a1, a2, b2):
    h1 = jnp.tanh(product(a1, fx, HID))
    h1x = stacked(h1)
    h2 = jnp.tanh(product(a2, h1x, HID) + b2)
    return h1, h1x, h2


def network_back(s1, s2, d, w3b, w2b, w1b):
    dx = stacked(d)
    p = product(w3b, dx, HID) * s2
    px = stacked(p)
    qx = stacked(product(w2b, px, HID) * s1)
    return product(w1b, qx, KP), (folded(d), folded(p)), dx, px, qx


def folded(d):
    return sum(d[:, j * LANES : (j + 1) * LANES] for j in range(CH // LANES))


def gather(accs, values, first):
    for ref, value in zip(accs, values):
        ref[...] = value if first else ref[...] + value


def weight_products(fx, h1x, h2x, dx, px, qx):
    return nt(h1x, px), nt(fx, qx), nt(dx, h2x)


def write_pack(pack, acc2, acc1, acc3, accb, accp, pad_ref):
    pack[0:HID, :] = four_blocks(acc2[...], HID)
    pack[HID : HID + 24, :] = four_blocks(acc1[...], KP)[0:24]
    pack[HID + 24 : HID + 48, :] = four_blocks(acc3[...], KP)[0:24]
    pad_ref[...] = jnp.zeros((HID, HID), F32)
    pad_ref[0:KP, :] = accb[...]
    for k, sums in ((21, accp[...]), (22, pad_ref[...])):
        row = jnp.sum(jnp.transpose(sums), axis=0, keepdims=True)
        pack[HID + k : HID + k + 1, :] = row


def collided(f, t, code, outs, i):
    k = i * ROWS
    relaxed = f[k : k + ROWS, :] + outs[k : k + ROWS, :]
    if BUOYANCY[i]:
        relaxed = relaxed + BUOYANCY[i] * t[...]
    o = OPPOSITE[i] * ROWS
    return jnp.where(code[...] == 0, relaxed, f[o : o + ROWS, :])


def forward_chunk(feat, c, l1, l2, l3, b2t, b3t):
    h1, _, h2 = hidden(stacked(across(feat, c)), l1, l2, b2t)
    return h1, h2, product(l3, stacked(h2), KP) + b3t


def edge_rows_kernel(
    w1_in, b1_in, w2_in, b2_in, w3_in, b3_in, f_in, t_in, code_in, adj_in, theta_in,
    w1, w2, w3, f, t, code, adj, theta, l1, l2, l3, b2t, b3t, h1s, h2s, out0, yp, ym,
    feat, outs, pad, b1, b2, b3, sems,
):
    ins = (w1_in, b1_in, w2_in, b2_in, w3_in, b3_in, f_in, t_in, code_in, adj_in, theta_in)
    here = (w1, b1, w2, b2, w3, b3, f, t, code, adj, theta)
    copies = [pltpu.make_async_copy(a, b, sems.at[k]) for k, (a, b) in enumerate(zip(ins, here))]
    for c in copies:
        c.start()
    for c in copies[:6]:
        c.wait()
    l1[...] = left_narrow(jnp.transpose(transposed(w1, b1, pad)))
    l2[...] = left(jnp.transpose(w2[...]))
    pad[...] = jnp.zeros((HID, HID), F32)
    pad[0:Q, :] = w3[...]
    l3[...] = left(pad[0:KP, :])
    b2t[...] = wide(column(b2, HID, pad))
    b3t[...] = wide(column(b3, Q, pad)[0:KP])
    copies[6].wait()
    fill_features(feat, f)
    h1, h2, out = forward_chunk(feat, 0, l1[...], l2[...], l3[...], b2t[...], b3t[...])
    h1s[0], h2s[0], out0[...] = h1, h2, out
    outs[...] = jnp.zeros(outs.shape, F32)
    back(outs, 0, out)
    for c in copies[7:]:
        c.wait()
    put_y(lambda i, x: tile(adj, i, x), -1, yp, ym, 12)

    def value(i, x):
        return collided(f, t, code, outs, i)[8 * x : 8 * x + 8]

    put_y(value, 1, yp, ym, 0)
    for x in range(2):
        yp[10 + x : 11 + x, :] = t[8 * x + 7 : 8 * x + 8, :]
        ym[10 + x : 11 + x, :] = t[8 * x : 8 * x + 1, :]


def other_rows_kernel(
    f, t, code, adj, l1, l2, l3, b2t, b3t, out0, w1, w2, w3,
    post, h1s, h2s, xp, xm, w3b, w2b, w1b,
    feat, outs, pad,
):
    w3b[...], w2b[...], w1b[...] = back_weights(w1, w2, w3, pad)
    fill_features(feat, f)
    back(outs, 0, out0[...])
    for c in range(1, ROWS * LANES // CH):
        h1, h2, out = forward_chunk(feat, c, l1[...], l2[...], l3[...], b2t[...], b3t[...])
        h1s[c - 1], h2s[c - 1] = h1, h2
        back(outs, c, out)
    for i in range(Q):
        post[i * ROWS : (i + 1) * ROWS, :] = collided(f, t, code, outs, i)
    put_x(lambda i, x: tile(adj, i, x), -1, xp, xm, 48)
    put_x(lambda i, x: tile(post, i, x), 1, xp, xm, 0)
    xp[40:48, :] = t[8:16, :]
    xm[40:48, :] = t[0:8, :]


def prepare_kernel(
    f, h1a, h2a, h1b, h2b, _,
    fxs, h1xs, h2xs, s1, s2,
    feat,
):
    fill_features(feat, f)
    for c in range(ROWS * LANES // CH):
        h1, h2 = (h1a[0], h2a[0]) if c == 0 else (h1b[c - 1], h2b[c - 1])
        fxs[c], h1xs[c], h2xs[c] = stacked(across(feat, c)), stacked(h1), stacked(h2)
        s1[c], s2[c] = 1.0 - h1 * h1, 1.0 - h2 * h2


def left_narrow(w):
    hi, lo = split(w + pltpu.roll(w, KP, 1))
    return jnp.concatenate([hi, lo], axis=0)[:, : 2 * KP]


def rims_of(below, above, leftward, rightward, at, row):
    return (
        below[at : at + 8, :],
        above[at : at + 8, :],
        [leftward[row + x : row + x + 1, :] for x in range(2)],
        [rightward[row + x : row + x + 1, :] for x in range(2)],
    )


def collision_gradient(adj, halo, code, grad, masked, lift):
    for x in range(2):
        fluid = code[8 * x : 8 * x + 8, :] == 0
        total = None
        for i in range(Q):
            k = i * ROWS + 8 * x
            g = streamed(adj, halo, -1, i, x)
            grad[k : k + 8, :] = g
            g = jnp.where(fluid, g, 0.0)
            masked[k : k + 8, :] = g
            if BUOYANCY[i]:
                total = BUOYANCY[i] * g if total is None else total + BUOYANCY[i] * g
        lift[8 * x : 8 * x + 8, :] = total
    masked[Q * ROWS :, :] = jnp.zeros(((KP - Q) * ROWS, LANES), F32)


def back_weights(w1, w2, w3, pad):
    pad[...] = jnp.zeros((HID, HID), F32)
    pad[0:Q, :] = w3[...]
    w3b = left_narrow(jnp.transpose(pad[...]))
    w2b = left(w2[...])
    pad[...] = jnp.zeros((HID, HID), F32)
    pad[0:Q, :] = w1[...]
    w1b = left(pad[0:KP, :])
    return w3b, w2b, w1b


def middle_kernel(
    x, post, f, t, code, adj, face, leftward, rightward, l1, l2, b2t, w3b, w2b, w1b,
    f1, t1, fbar, lift, accb, accp, fxs, h1xs, h2s, dxs, pxs, qxs,
    feat, grad, masked, dfs,
):
    kind = code[8 * x : 8 * x + 8, :]
    fluid = kind == 0
    halo = (face, face, leftward, rightward, 0, 0, 88)
    adj_halo = (face, face, leftward, rightward, 48, 12, 90)
    warmth = None
    for i in range(Q):
        k = 8 * i
        f1[k : k + 8, :] = streamed(post, halo, 1, i, x)
        g = streamed(adj, adj_halo, -1, i, x)
        grad[k : k + 8, :] = g
        g = jnp.where(fluid, g, 0.0)
        masked[k : k + 8, :] = g
        if BUOYANCY[i]:
            warmth = BUOYANCY[i] * g if warmth is None else warmth + BUOYANCY[i] * g
    lift[...] = warmth
    masked[8 * Q :, :] = jnp.zeros(((KP - Q) * 8, LANES), F32)
    u = motion(f, x)
    here = t[8 * x : 8 * x + 8, :]
    total = 0.4 * here
    rims = rims_of(face, face, leftward, rightward, 40, 10)
    for a, (plus, minus) in enumerate(warm_neighbours(t, rims, x)):
        total = total + (CONDUCTIVITY - 0.5 * u[a]) * plus
        total = total + (CONDUCTIVITY + 0.5 * u[a]) * minus
    t1[...] = jnp.where(fluid, total, jnp.where(kind == 1, here, HEATER))
    fill_features(feat, f1)
    for c in range(8 * LANES // CH):
        fx = stacked(across(feat, c))
        h1, h1x, h2 = hidden(fx, l1[...], l2[...], b2t[...])
        d = across(masked, c)
        df, sums, dx, px, qx = network_back(
            1.0 - h1 * h1, 1.0 - h2 * h2, d, w3b[...], w2b[...], w1b[...]
        )
        gather((accb, accp), sums, c == 0)
        back(dfs, c, df)
        fxs[c], h1xs[c], h2s[c] = fx, h1x, h2
        dxs[c], pxs[c], qxs[c] = dx, px, qx
    for i in range(Q):
        k, o = 8 * i, 8 * OPPOSITE[i]
        fbar[k : k + 8, :] = jnp.where(
            fluid, grad[k : k + 8, :] + dfs[k : k + 8, :], grad[o : o + 8, :]
        )


def weights_kernel(*refs):
    first, second, (_, pack, pad, accb, accp, *accs) = refs[:8], refs[8:16], refs[16:]
    accb[...] = first[0][...] + second[0][...]
    accp[...] = first[1][...] + second[1][...]
    for plane in (first, second):
        for c in range(plane[2].shape[0]):
            fx, h1x, h2, dx, px, qx = (v[c] for v in plane[2:])
            values = weight_products(fx, h1x, stacked(h2), dx, px, qx)
            gather(accs, values, plane is first and c == 0)
    write_pack(pack, *accs, accb, accp, pad)


def coefficient(u, a, s, kind):
    return jnp.where(kind == 0, CONDUCTIVITY - (0.5 * s) * u[a], 0.0)


def adjoint_parts(fbar, lift, f1, t1, theta, code, t_rims, flux_rims):
    codes, thetas = halves(code), halves(theta)
    liquids = [jnp.where(k == 0, v, 0.0) for k, v in zip(codes, thetas)]
    us = [motion(f1, x) for x in range(2)]
    ubar = motion_adjoint(t1, t_rims, liquids)
    warm = heat_adjoint(us, liquids, thetas, codes, flux_rims)
    warm = [v + w for v, w in zip(warm, halves(lift))]

    def adj(i, x):
        return with_motion(tile(fbar, i, x), ubar[x], i)

    return codes, liquids, us, adj, warm


def no_rims():
    blank, row = jnp.zeros((8, LANES), F32), jnp.zeros((1, LANES), F32)
    return blank, blank, [row, row], [row, row]


def rows_of(ref, at):
    return [ref[at + x : at + x + 1, :] for x in range(2)]


def paired(refs):
    return [tuple(refs[2 * k : 2 * k + 2]) for k in range(4)]


def along_y_kernel(*refs):
    fbar, lift, f1, t1 = paired(refs)
    f0, theta, code, yp, ym = refs[8:]
    codes, liquids, us, adj, warm = adjoint_parts(
        fbar, lift, f1, t1, theta, code, no_rims(), no_rims()
    )
    ts = halves(t1)
    for s, e, out in ((1, 7, yp), (-1, 0, ym)):
        for x in range(2):
            u0 = motion(f0, x)
            parts = [adj(i, x) for i in moving(1, s, -1)]
            parts += [ts[x], flux(us[x], 1, s, liquids[x]), liquids[x], warm[x]]
            parts.append(coefficient(u0, 1, s, codes[x]))
            for k, v in enumerate(parts):
                out[2 * k + x : 2 * k + x + 1, :] = v[e : e + 1]
        out[20:21, :] = flux(us[1], 0, 1, liquids[1])[e : e + 1]
        out[21:22, :] = flux(us[0], 0, -1, liquids[0])[e : e + 1]


def along_x_kernel(*refs):
    fbar, lift, f1, t1 = paired(refs)
    f0, theta, code, leftward, rightward, xp, xm, yl, yr = refs[8:]
    zero, _, _, _ = no_rims()
    codes, liquids, us, adj, warm = adjoint_parts(
        fbar, lift, f1, t1, theta, code,
        (zero, zero, rows_of(leftward, 10), rows_of(rightward, 10)),
        (zero, zero, rows_of(leftward, 12), rows_of(rightward, 12)),
    )
    ts = halves(t1)
    for s, x, out in ((1, 1, xp), (-1, 0, xm)):
        parts = [adj(i, x) for i in moving(0, s, -1)]
        parts += [ts[x], liquids[x], warm[x]]
        parts.append(coefficient(motion(f0, x), 0, s, codes[x]))
        parts.append(flux(us[x], 0, s, liquids[x]))
        for k, v in enumerate(parts):
            out[8 * k : 8 * k + 8, :] = v
    for k, (s, e, come, out) in enumerate(((1, 0, leftward, yl), (-1, 7, rightward, yr))):
        t_come, flux_come, liquid, warm_come, factor = (
            rows_of(come, 10 + 2 * j) for j in range(5)
        )
        for x in range(2):
            for j in range(5):
                r = 2 * j + x
                out[r : r + 1, :] = (
                    come[r : r + 1, :] + 0.5 * liquid[x] * ts[x][e : e + 1]
                )
            done = warm_come[x] + flux(us[x], 1, -s, liquids[x])[e : e + 1]
            for j, v in enumerate((t_come[x], liquid[x], done, factor[x], flux_come[x])):
                r = 10 + 2 * j + x
                out[r : r + 1, :] = v
        for sx, x, to in ((1, 1, xp), (-1, 0, xm)):
            r = 2 * moving(1, s, -1).index(diagonal(sx, s, -1)) + x
            for j, v in enumerate(
                (out[r : r + 1, :], liquid[x], t_come[x], come[21 - x : 22 - x, :])
            ):
                to[80 + 4 * k + j : 81 + 4 * k + j, :] = v


def complete(
    fbar, lift, f1, t1, theta, code, below, above, yl, yr,
    adj1, warm1, hbelow, habove, hleft, hright,
):
    _, liquids, us, adj, warm = adjoint_parts(
        fbar, lift, f1, t1, theta, code,
        (below[40:48, :], above[40:48, :], rows_of(yl, 10), rows_of(yr, 10)),
        (below[72:80, :], above[72:80, :], rows_of(yl, 18), rows_of(yr, 18)),
    )
    ts = halves(t1)
    for x in range(2):
        warm1[8 * x : 8 * x + 8, :] = warm[x]
        for i in range(Q):
            k = i * ROWS + 8 * x
            adj1[k : k + 8, :] = adj(i, x)
    faces = []
    for s, x, come, out in ((1, 0, below, hbelow), (-1, 1, above, habove)):
        for k in range(5):
            out[8 * k : 8 * k + 8, :] = (
                come[8 * k : 8 * k + 8, :] + 0.5 * come[48:56, :] * ts[x]
            )
        for k, rows in enumerate((yl, yr)):
            j = 80 + 4 * k
            out[40 + k : 41 + k, :] = (
                come[j : j + 1, :] + 0.5 * come[j + 1 : j + 2, :] * rows[10 + x : 11 + x, :]
            )
        faces.append(come[64:72, :] * (come[56:64, :] + flux(us[x], 0, -s, liquids[x])))
    edges = []
    for k, (s, rows, out) in enumerate(((1, yl, hleft), (-1, yr, hright))):
        j = 80 + 4 * k
        out[0:10, :] = rows[0:10, :]
        edge = []
        for sx, x, come in ((1, 0, below), (-1, 1, above)):
            r = 2 * moving(1, s, -1).index(diagonal(sx, s, -1)) + x
            out[r : r + 1, :] = (
                rows[r : r + 1, :]
                - 0.5 * rows[12 + x : 13 + x, :] * come[j + 2 : j + 3, :]
            )
            edge.append(
                rows[16 + x : 17 + x, :]
                * (rows[14 + x : 15 + x, :] + come[j + 3 : j + 4, :])
            )
        edges.append(edge)
    return (*faces, *edges)


def first_step_kernel(
    scale, known,
    theta2, f, t, below, above, yl, yr,
    tbelow, tabove, tleft, tright, code, w3b, w2b, w1b, fxs, h1xs, h2xs, s1, s2, pack1,
    fbar, thetabar, pack,
    grad, masked, dfs, pad, acc2, acc1, acc3, accb, accp, lift, total,
    adj, theta, hbelow, habove, hleft, hright,
):
    flux_rims = complete(
        *paired(known), theta2, code, below, above, yl, yr,
        adj, theta, hbelow, habove, hleft, hright,
    )
    halo = (hbelow, habove, hleft, hright, 0, 0, 40)
    collision_gradient(adj, halo, code, grad, masked, lift)
    for c in range(ROWS * LANES // CH):
        d = across(masked, c)
        df, sums, dx, px, qx = network_back(s1[c], s2[c], d, w3b[...], w2b[...], w1b[...])
        values = weight_products(fxs[c], h1xs[c], h2xs[c], dx, px, qx)
        gather((acc2, acc1, acc3, accb, accp), (*values, *sums), c == 0)
        back(dfs, c, df)
    write_pack(total, acc2, acc1, acc3, accb, accp, pad)
    parts, part, _ = pack.shape
    total[PACK:, :] = jnp.zeros((parts * part - PACK, HID), F32)
    total[0:PACK, :] = (total[0:PACK, :] + pack1[...]) * scale
    for k in range(parts):
        pack[k] = total[k * part : (k + 1) * part, :]
    codes, thetas = halves(code), halves(theta)
    liquids = [jnp.where(k == 0, v, 0.0) for k, v in zip(codes, thetas)]
    rims = rims_of(tbelow, tabove, tleft, tright, 40, 10)
    ubar = motion_adjoint(t, rims, liquids)
    new = heat_adjoint([motion(f, x) for x in range(2)], liquids, thetas, codes, flux_rims)
    for x in range(2):
        thetabar[8 * x : 8 * x + 8, :] = new[x] + lift[8 * x : 8 * x + 8, :]
        fluid = codes[x] == 0
        for i in range(Q):
            k, o = i * ROWS + 8 * x, OPPOSITE[i] * ROWS + 8 * x
            value = jnp.where(fluid, grad[k : k + 8, :] + dfs[k : k + 8, :], grad[o : o + 8, :])
            fbar[k : k + 8, :] = with_motion(value, ubar[x], i)


def struct(*shape):
    return jax.ShapeDtypeStruct(shape, F32)


def call(kernel, outs, scratch, name, more=(), **specs):
    return pl.pallas_call(
        kernel,
        out_shape=outs,
        scratch_shapes=[pltpu.VMEM(s, F32) for s in scratch] + list(more),
        **specs,
        compiler_params=pltpu.CompilerParams(vmem_limit_bytes=40 * 1024 * 1024),
        name=name,
    )


FULL = (KP * ROWS, LANES)
POPS = struct(Q * ROWS, LANES)
WARM = struct(ROWS, LANES)


def shifted(value, axis, by):
    count = lax.axis_size(axis)
    return lax.ppermute(value, axis, [(s, (s + by) % count) for s in range(count)])


def along(axis, plus, minus):
    return shifted(plus, axis, 1), shifted(minus, axis, -1)


def edge_kernel(blocks, xp, xm, leftward, rightward, xp_out, xm_out):
    xp_out[...] = xp[...]
    xm_out[...] = xm[...]
    for orient, row, at in blocks:
        put_corners(leftward, rightward, orient, xp_out, xm_out, row, at)


def swapped(value, groups):
    return lax.all_to_all(
        value, ("gx", "gy"), 0, 0, axis_index_groups=groups, tiled=True
    )


def factors_of(nx):
    near = 2 if nx % 2 == 0 else 1
    far = nx // 24 if nx % 24 == 0 else 1
    return far, nx // (far * near), near


def shares_of(nx, ny):
    far, _, near = factors_of(nx)
    return far * near * ny


def groups_of(nx, ny):
    far, mid, near = factors_of(nx)
    at = np.arange(nx * ny).reshape(far, mid, near, ny)
    return (
        at.transpose(1, 0, 2, 3).reshape(mid, -1).tolist(),
        at.transpose(0, 2, 3, 1).reshape(-1, mid).tolist(),
    )


def total_kernel(parts, out):
    value = parts[0]
    for k in range(1, parts.shape[0]):
        value = value + parts[k]
    for k in range(out.shape[0]):
        out[k] = value


def summed(parts, copies):
    return call(total_kernel, struct(copies, *parts.shape[1:]), [], "total")(parts)


def reduced(pack):
    share, same = groups_of(lax.axis_size("gx"), lax.axis_size("gy"))
    part = summed(swapped(pack, share), len(same[0]))
    part = summed(swapped(part, same), len(share[0]))
    return swapped(part, share)


def unpack_kernel(parts, w1, b1, w2, b2, w3, b3, pack):
    count, part, _ = parts.shape
    for k in range(count):
        pack[k * part : (k + 1) * part, :] = parts[k]
    w2[...] = pack[0:HID, :]
    w1[...] = pack[HID : HID + Q, :]
    b1[...] = pack[HID + Q : HID + Q + 1, :]
    b2[...] = pack[HID + 21 : HID + 22, :]
    b3[...] = pack[HID + 22 : HID + 23, 0:Q]
    w3[...] = pack[HID + 24 : HID + 24 + Q, :]


def per_device(f, t, code, w1, b1, w2, b2, w3, b3, adj, theta):
    sx, sy, sz = t.shape
    cells = sx * lax.axis_size("gx") * sy * lax.axis_size("gy") * sz
    f, adj = f.reshape(Q * ROWS, LANES), adj.reshape(Q * ROWS, LANES)
    t, code, theta = (v.reshape(ROWS, LANES) for v in (t, code, theta))
    b1, b2, b3 = (v.reshape(1, -1) for v in (b1, b2, b3))
    w3 = w3.T
    ins = (w1, b1, w2, b2, w3, b3, f, t, code, adj, theta)
    like = [jax.ShapeDtypeStruct(v.shape, v.dtype) for v in ins]
    held = [v for k, v in enumerate(like) if k not in (1, 3, 5)]
    count = ROWS * LANES // CH

    def narrow(*shape):
        return jax.ShapeDtypeStruct(shape, BF16)

    outs = call(
        edge_rows_kernel,
        [*held, narrow(2 * HID, 2 * KP), narrow(2 * HID, 2 * HID), narrow(2 * KP, 2 * HID),
         struct(HID, CH), struct(KP, CH), struct(1, HID, CH), struct(1, HID, CH),
         struct(KP, CH), struct(24, LANES), struct(24, LANES)],
        [FULL, FULL, (HID, HID)],
        "edge_rows",
        [pltpu.VMEM(v.shape, v.dtype) for v in (b1, b2, b3)] + [pltpu.SemaphoreType.DMA((11,))],
        in_specs=[pl.BlockSpec(memory_space=pltpu.HBM)] * 11,
    )(*(pltpu.with_memory_space_constraint(v, pltpu.HBM) for v in ins))
    w1, w2, w3, f, t, code, adj, theta, l1, l2, l3, b2t, b3t, h1a, h2a, out0, yp, ym = outs
    sides = along("gy", yp, ym)
    post, h1b, h2b, xp, xm, w3b, w2b, w1b = call(
        other_rows_kernel,
        [POPS, *[struct(count - 1, HID, CH)] * 2, struct(96, LANES), struct(96, LANES),
         narrow(2 * HID, 2 * KP), narrow(2 * HID, 2 * HID), narrow(2 * KP, 2 * HID)],
        [FULL, FULL, (HID, HID)],
        "other_rows",
    )(f, t, code, adj, l1, l2, l3, b2t, b3t, out0, w1, w2, w3)
    blocks = ((1, 0, 88), (-1, 12, 90))
    xp, xm = call(
        lambda *refs: edge_kernel(blocks, *refs), [struct(96, LANES)] * 2, [], "corners"
    )(xp, xm, *sides)
    below, above = along("gx", xp, xm)
    halo0 = (below, above, *sides)
    accs = [(2 * HID, 2 * HID), (2 * KP, 2 * HID), (2 * KP, 2 * HID), (KP, LANES), (HID, LANES)]
    plane, half = struct(8 * Q, LANES), struct(8, LANES)
    small, large = (
        jax.ShapeDtypeStruct((8 * LANES // CH, 2 * n, CH), BF16) for n in (KP, HID)
    )
    planes = [
        call(
            lambda *refs, x=x: middle_kernel(x, *refs),
            [plane, half, plane, half, struct(KP, LANES), struct(HID, LANES), small, large,
             struct(8 * LANES // CH, HID, CH), small, large, large],
            [(8 * KP, LANES), (8 * Q, LANES), (8 * KP, LANES), (8 * KP, LANES)],
            "middle",
        )(post, f, t, code, adj, face, *sides, l1, l2, b2t, w3b, w2b, w1b)
        for x, face in enumerate((below, above))
    ]
    parts = [planes[x][k] for k in (2, 3, 0, 1) for x in range(2)]
    known = (*parts, f, theta, code)
    yp, ym = call(along_y_kernel, [struct(24, LANES)] * 2, [], "along_y")(*known)
    come = along("gy", yp, ym)
    xp, xm, yl, yr = call(
        along_x_kernel, [struct(88, LANES)] * 2 + [struct(24, LANES)] * 2, [], "along_x"
    )(*known, *come)
    faces = along("gx", xp, xm)
    kept = call(
        prepare_kernel,
        [narrow(count, 2 * KP, CH), *[narrow(count, 2 * HID, CH)] * 2, *[struct(count, HID, CH)] * 2],
        [FULL],
        "prepare",
        in_specs=[pl.BlockSpec(memory_space=pltpu.VMEM)] * 5 + [pl.BlockSpec(memory_space=pl.ANY)],
    )(f, h1a, h2a, h1b, h2b, xp)
    pack1 = call(
        weights_kernel,
        struct(PACK, HID),
        [(HID, HID), *accs[3:], *accs[:3]],
        "weights",
        in_specs=[pl.BlockSpec(memory_space=pltpu.VMEM)] * 16 + [pl.BlockSpec(memory_space=pl.ANY)],
    )(*planes[0][4:], *planes[1][4:], xp)
    scale = 1.0 / math.sqrt(cells)
    shares = shares_of(lax.axis_size("gx"), lax.axis_size("gy"))
    part = -(-(PACK + 8) // shares)
    fbar0, theta0, pack = call(
        lambda *refs: first_step_kernel(scale, refs[:8], *refs[8:]),
        [POPS, WARM, struct(shares, part, HID)],
        [(Q * ROWS, LANES), FULL, FULL, (HID, HID), *accs, (ROWS, LANES), (shares * part, HID),
         (Q * ROWS, LANES), (ROWS, LANES), (48, LANES), (48, LANES), (16, LANES), (16, LANES)],
        "first_step",
    )(*parts, theta, f, t, *faces, yl, yr, *halo0, code, w3b, w2b, w1b, *kept, pack1)
    total = reduced(pack)
    g1, gb1, g2, gb2, g3, gb3 = call(
        unpack_kernel,
        [struct(Q, HID), struct(1, HID), struct(HID, HID), struct(1, HID), struct(Q, HID), struct(1, Q)],
        [(shares * part, HID)],
        "unpack",
    )(total)
    return (
        fbar0.reshape(Q, sx, sy, sz),
        theta0.reshape(sx, sy, sz),
        g1,
        gb1.reshape(HID),
        g2,
        gb2.reshape(HID),
        g3.T,
        gb3.reshape(Q),
    )


def solution(mesh):
    pops, cells = P(None, "gx", "gy", None), P("gx", "gy", None)
    return jax.shard_map(
        per_device,
        mesh=mesh,
        in_specs=(pops, cells, cells, P(), P(), P(), P(), P(), P(), pops, cells),
        out_specs=(pops, cells, P(), P(), P(), P(), P(), P()),
        check_vma=False,
    )
```
